32 devices in a mesh: seq: 8 (over z, y), batch: 4 (over x, core).
Axes of the slice: x: 2, y: 2, z: 4, core: 2. Of those that a mesh axis runs over, the one named last changes fastest.
Arguments:
- tokens_in: bfloat16 [4, 2048, 2048], P('batch', 'seq'), may hold values from -6 to 6
- cotangent: bfloat16 [4, 2048, 2048], P('batch', 'seq'), may hold values from -6 to 6
- segment_ids: int32 [4, 2048], P('batch'), may hold values from 0 to 5, never falling along the last dimension, each value on 1 to 682 neighbouring positions
- attn_gain: bfloat16 [2048], P(('seq', 'batch')), may hold values from 0.25 to 1.75
- attn_shift: bfloat16 [2048], P(('seq', 'batch')), may hold values from -2 to 2
- qkv_weight: bfloat16 [2048, 6144], P(('seq', 'batch')), may hold values from -0.125 to 0.125
- qkv_bias: bfloat16 [6144], P(('seq', 'batch')), may hold values from -3 to 3
- out_weight: bfloat16 [2048, 2048], P(('seq', 'batch')), may hold values from -1 to 1
- mlp_gain: bfloat16 [2048], P(('seq', 'batch')), may hold values from 0.25 to 1.75
- mlp_shift: bfloat16 [2048], P(('seq', 'batch')), may hold values from -2 to 2
- gate_weight: bfloat16 [2048, 5632], P(('seq', 'batch')), may hold values from -0.125 to 0.125
- up_weight: bfloat16 [2048, 5632], P(('seq', 'batch')), may hold values from -0.125 to 0.125
- down_weight: bfloat16 [5632, 2048], P(('seq', 'batch')), may hold values from -0.078125 to 0.078125
Outputs:
- block_out: bfloat16 [4, 2048, 2048], P('batch', 'seq')
- grad_tokens: bfloat16 [4, 2048, 2048], P('batch', 'seq')
- grad_attn_gain: float32 [2048], P(('seq', 'batch'))
- grad_attn_shift: float32 [2048], P(('seq', 'batch'))
- grad_qkv_weight: float32 [2048, 6144], P(('seq', 'batch'))
- grad_qkv_bias: float32 [6144], P(('seq', 'batch'))
- grad_out_weight: float32 [2048, 2048], P(('seq', 'batch'))
- grad_mlp_gain: float32 [2048], P(('seq', 'batch'))
- grad_mlp_shift: float32 [2048], P(('seq', 'batch'))
- grad_gate_weight: float32 [2048, 5632], P(('seq', 'batch'))
- grad_up_weight: float32 [2048, 5632], P(('seq', 'batch'))
- grad_down_weight: float32 [5632, 2048], P(('seq', 'batch'))
The draws below stay inside these ranges and needn't reach their ends.
Inputs may be any that keep to these rules, and one draw needn't show every extreme that they name: `segment_ids`: each row holds 6 documents of consecutive ids, each 1 to 2048 // 3 tokens long, one exactly that long.
All inputs are finite; a program needn't handle non-finite values.
Results may differ from the reference program's by a relative error of at most 0.013.
Values may be sent and summed in bfloat16 or wider, within the bound.
No kernel may reach another device: no remote copies, remote signals or barrier semaphores. Data moves between devices by JAX's collectives and lax.ppermute only.
A program may use at most 448 MiB of HBM per device.

```python
import math
import jax
import jax.numpy as jnp
import numpy as np
from jax import lax

HEADS = 32
HEAD_DIM = 64
FF = 5632
ROT = 16
DOCS = 6
D = 2048
LENGTH = 2048
GROUPS = 4


def with_spikes(values, stream_key, source, target, shards_of, factor):
    owner, partner = [(jnp.arange(values.shape[dim]) // (values.shape[dim] // shards_of)).reshape([-1 if axis == dim else 1 for axis in range(values.ndim)]) for dim in (source, target)]
    chosen = jax.random.permutation(stream_key, shards_of)[partner]
    strong = (owner == chosen) | (owner == (partner + shards_of // 2) % shards_of)
    return jnp.where(strong, factor * values, values)


def shard_levels(stream_key, extent, shards, low, top_value):
    def one(dim, parts):
        draws = jax.random.uniform(jax.random.fold_in(jax.random.fold_in(stream_key, 6), dim), (parts,), jnp.float32, low / len(shards), top_value / len(shards))
        return jnp.repeat(jnp.exp(draws), extent[dim] // parts).reshape((-1,) + (1,) * (len(extent) - dim - 1))

    factor_of = one(*shards[0])
    for cut in shards[1:]:
        factor_of = factor_of * one(*cut)
    return factor_of


def length_profile(amount, total, reach, lean):
    weights = [(1 << 20) // math.isqrt(standing ** lean) + 1 for standing in range(2, amount + 1)]
    spare, counts = total - reach - (amount - 1), [1] * (amount - 1)
    while spare > 0:
        candidates = [i for i in range(amount - 1) if counts[i] < reach]
        whole, left = sum([weights[i] for i in candidates]), spare
        for i in candidates:
            more = min(reach - counts[i], max(1, left * weights[i] // whole), spare)
            counts[i] = counts[i] + more
            spare = spare - more
    return np.array([reach] + counts)


def uneven_parts(stream_key, number_of, total, most, slope):
    if number_of == 2:
        one = jax.random.randint(stream_key, (), max(1, total - most), min(most, total - 1) + 1)
        return jnp.stack([one, total - one])
    sizes = jnp.asarray(length_profile(number_of, total, most, slope), jnp.int32)
    twos = (number_of - 1) // 2
    source_of, sink = sizes[1:1 + 2 * twos:2], sizes[2:2 + 2 * twos:2]
    margin = jnp.minimum(source_of - 1, most - sink)
    shifted = jax.random.randint(jax.random.fold_in(stream_key, 1), (twos,), 0, 1 << 20) % (margin + 1)
    sizes = sizes.at[1:1 + 2 * twos:2].set(source_of - shifted).at[2:2 + 2 * twos:2].set(sink + shifted)
    return sizes[jax.random.permutation(jax.random.fold_in(stream_key, 2), number_of)]


def gaussian(stream_key, extent, width, most, split=(), held_as=jnp.bfloat16):
    loudness = shard_levels(stream_key, extent, split, -0.22, 0.18) if split else 1.0
    drawn = jax.random.normal(stream_key, extent, jnp.float32) * width * loudness
    return jnp.minimum(jnp.maximum(drawn, -most), most).astype(held_as)


def gaussian_with(key, extent, scale, reach, cuts, heavy, kind=jnp.bfloat16):
    drawn = scale * jax.random.normal(key, extent, jnp.float32)
    if cuts:
        drawn = drawn * shard_levels(key, extent, cuts, -0.22, 0.18)
    return jnp.clip(with_spikes(drawn, jax.random.fold_in(key, 3), *heavy), -reach, reach).astype(kind)


def setup_inputs(seed: int = 0) -> dict:
    key_of = jax.random.split(jax.random.key(seed), 14)
    tokens_in = gaussian_with(key_of[0], (GROUPS, LENGTH, D), 1.0, 6.0, ((0, 4), (1, 8)), (1, 2, 8, 2.0))
    cotangent = gaussian_with(key_of[1], (GROUPS, LENGTH, D), 1.0, 6.0, ((0, 4), (1, 8)), (1, 2, 8, 2.0))
    segment_ids = jax.vmap(lambda own: jnp.searchsorted(jnp.cumsum(uneven_parts(own, DOCS, LENGTH, LENGTH // 3, 2)), jnp.arange(LENGTH), side="right"))(jax.random.split(key_of[2], GROUPS)).reshape((GROUPS, LENGTH)).astype(jnp.int32)
    attn_gain = jnp.clip(1.0 + 0.15 * jax.random.normal(key_of[3], (D,), jnp.float32), 0.25, 1.75).astype(jnp.bfloat16)
    attn_shift = gaussian(key_of[4], (D,), 0.3, 2.0, ((0, 32),))
    qkv_weight = gaussian(key_of[5], (D, 3 * D), D ** -0.5, 0.125, ((0, 32),))
    qkv_bias = gaussian(key_of[6], (3 * D,), 0.5, 3.0, ((0, 32),))
    out_weight = gaussian(key_of[7], (D, D), (D // 64) ** -0.5, 1.0, ((0, 32),))
    mlp_gain = jnp.clip(1.0 + 0.15 * jax.random.normal(key_of[8], (D,), jnp.float32), 0.25, 1.75).astype(jnp.bfloat16)
    mlp_shift = gaussian(key_of[9], (D,), 0.3, 2.0, ((0, 32),))
    gate_weight = gaussian(key_of[10], (D, FF), D ** -0.5, 0.125, ((0, 32),))
    up_weight = gaussian(key_of[11], (D, FF), D ** -0.5, 0.125, ((0, 32),))
    down_weight = gaussian(key_of[12], (FF, D), FF ** -0.5, 0.078125, ((0, 32),))
    return {"tokens_in": tokens_in, "cotangent": cotangent, "segment_ids": segment_ids, "attn_gain": attn_gain, "attn_shift": attn_shift, "qkv_weight": qkv_weight, "qkv_bias": qkv_bias, "out_weight": out_weight, "mlp_gain": mlp_gain, "mlp_shift": mlp_shift, "gate_weight": gate_weight, "up_weight": up_weight, "down_weight": down_weight}


@jax.custom_vjp
def low(v):
    return lax.optimization_barrier(v.astype(jnp.bfloat16)).astype(jnp.float32)

@jax.custom_vjp
def low_back(v):
    return v

def low_keep(v):
    return (low(v), None)

def low_pass(kept, grad):
    return (grad,)

def back_keep(v):
    return (v, None)

def back_low(kept, grad):
    return (low(grad),)
low.defvjp(low_keep, low_pass)
low_back.defvjp(back_keep, back_low)
epsilon = 1e-05
precise = lax.Precision.HIGHEST

def layer_norm(value, gain, shift):
    centred = value - lax.optimization_barrier(jnp.mean(value, axis=-1, keepdims=True))
    variance = lax.optimization_barrier(jnp.mean(centred * centred, axis=-1, keepdims=True))
    return centred * lax.rsqrt(variance + epsilon) * gain + shift

def doc_positions(segment):
    length = segment.shape[-1]
    places = jnp.broadcast_to(jnp.arange(length, dtype=jnp.int32), segment.shape)
    leading = jnp.ones(segment.shape[:-1] + (1,), dtype=bool)
    begins = jnp.concatenate([leading, segment[..., 1:] != segment[..., :-1]], axis=-1)
    starts = lax.cummax(jnp.where(begins, places, 0), axis=segment.ndim - 1)
    return places - starts

def angles(segment):
    position = doc_positions(segment).astype(jnp.float32)
    halfway = ROT // 2
    inverse = 10000.0 ** (-jnp.arange(halfway, dtype=jnp.float32) / halfway)
    theta = position[..., None] * inverse
    return (jnp.cos(theta), jnp.sin(theta))

def rotate(value, cosine, sine):
    halfway = ROT // 2
    first_part = value[..., :halfway]
    second_part = value[..., halfway:ROT]
    cos_part = cosine[..., None, :]
    sin_part = sine[..., None, :]
    return jnp.concatenate([first_part * cos_part - second_part * sin_part, second_part * cos_part + first_part * sin_part, value[..., ROT:]], axis=-1)

def matmul(left, right):
    return jnp.einsum('gtd,de->gte', left, right, precision=precise)

def attention(queries, keys, values, segment):
    groups, length = (queries.shape[0], queries.shape[1])
    block_rows = min(512, length)
    blocks = length // block_rows
    score_scale = HEAD_DIM ** (-0.5)

    def per_group(packed):
        group_q, group_k, group_v, group_seg = packed
        columns = jnp.arange(length, dtype=jnp.int32)

        def per_block(number):
            first_row = number * block_rows
            query_rows = lax.dynamic_slice_in_dim(group_q, first_row, block_rows, 0)
            seg_rows = lax.dynamic_slice_in_dim(group_seg, first_row, block_rows, 0)
            scores = jnp.einsum('bhd,khd->hbk', query_rows, group_k, precision=precise) * score_scale
            scores = low_back(scores)
            row_index = first_row + jnp.arange(block_rows, dtype=jnp.int32)
            allowed = (columns[None, :] <= row_index[:, None]) & (group_seg[None, :] == seg_rows[:, None])
            scores = jnp.where(allowed[None], scores, -1e+30)
            row_max = lax.optimization_barrier(jnp.max(scores, axis=-1, keepdims=True))
            weights = jnp.exp(scores - row_max)
            weights = weights / lax.optimization_barrier(jnp.sum(weights, axis=-1, keepdims=True))
            return jnp.einsum('hbk,khd->bhd', low(weights), group_v, precision=precise)
        outputs = lax.map(jax.checkpoint(per_block), jnp.arange(blocks, dtype=jnp.int32))
        return outputs.reshape(length, HEADS * HEAD_DIM)
    return lax.map(per_group, (queries, keys, values, segment))

def forward(inputs, attn_gain, attn_shift, qkv_weight, qkv_bias, out_weight, mlp_gain, mlp_shift, gate_weight, up_weight, down_weight, cosine, sine, segment):
    normed = low(layer_norm(inputs, attn_gain, attn_shift))
    projected = low_back(matmul(normed, qkv_weight) + qkv_bias)
    head_shape = inputs.shape[:2] + (HEADS, HEAD_DIM)
    queries = rotate(projected[..., :D].reshape(head_shape), cosine, sine)
    keys = rotate(projected[..., D:2 * D].reshape(head_shape), cosine, sine)
    values = projected[..., 2 * D:].reshape(head_shape)
    queries = low_back(low(queries))
    keys = low_back(low(keys))
    values = low_back(low(values))
    mixed = low_back(low(attention(queries, keys, values, segment)))
    hidden = inputs + low_back(matmul(mixed, out_weight))
    normed_two = low(layer_norm(hidden, mlp_gain, mlp_shift))
    gate_sum = low_back(matmul(normed_two, gate_weight))
    up_sum = low_back(matmul(normed_two, up_weight))
    activated = low(jax.nn.silu(gate_sum) * up_sum)
    return hidden + low_back(matmul(activated, down_weight))

def reference(tokens_in, cotangent, segment_ids, attn_gain, attn_shift, qkv_weight, qkv_bias, out_weight, mlp_gain, mlp_shift, gate_weight, up_weight, down_weight):
    params = tuple((item.astype(jnp.float32) for item in (attn_gain, attn_shift, qkv_weight, qkv_bias, out_weight, mlp_gain, mlp_shift, gate_weight, up_weight, down_weight)))
    cosine, sine = angles(segment_ids)

    def wrapped(inputs, *weights):
        return forward(inputs, *weights, cosine, sine, segment_ids)
    output, pullback = jax.vjp(wrapped, tokens_in.astype(jnp.float32), *params)
    grads = pullback(cotangent.astype(jnp.float32))
    return (output.astype(jnp.bfloat16), grads[0].astype(jnp.bfloat16), grads[1], grads[2], grads[3], grads[4], grads[5], grads[6], grads[7], grads[8], grads[9], grads[10])
```

```python
import functools

import jax
import jax.numpy as jnp
from jax import lax
from jax.experimental import pallas as pl
from jax.experimental.pallas import tpu as pltpu
from jax.sharding import Mesh
from jax.sharding import PartitionSpec as P

HEAD_DIM = 64
ROT = 16
DOCS = 6
LANES = 128
EPS = 1e-05
BF = jnp.bfloat16
F32 = jnp.float32
NEG = -1e30
ALL = ("z", "y", "x", "c")
SEQ = ("z", "y")
BATCH = ("x", "c")
SWAP = ((0, 1), (1, 0))


def dot(a, b, out=F32):
    return jnp.dot(a, b, preferred_element_type=out)


def dot_nt(a, b, out=F32):
    return lax.dot_general(a, b, (((1,), (1,)), ((), ())), preferred_element_type=out)


def dot_tn(a, b, out=F32):
    return lax.dot_general(a, b, (((0,), (0,)), ((), ())), preferred_element_type=out)


def gather_batch(x, pair):
    if not pair:
        return lax.all_gather(x, BATCH, axis=0, tiled=True)
    other = lax.ppermute(x, "x", SWAP)
    near = jnp.concatenate([x, other], axis=0)
    far = lax.ppermute(near, "c", SWAP)
    return jnp.concatenate([near, far], axis=0)


def reduce_batch(part, pair):
    if not pair:
        return lax.psum_scatter(part, BATCH, scatter_dimension=0, tiled=True).astype(F32)
    rows = part.shape[0] // 4
    got = lax.ppermute(part[2 * rows :], "c", SWAP)
    send = (part[rows : 2 * rows].astype(F32) + got[rows:].astype(F32)).astype(BF)
    last = lax.ppermute(send, "x", SWAP)
    return part[:rows].astype(F32) + got[:rows].astype(F32) + last.astype(F32)


def gather_seq(w, ny):
    near = lax.all_gather(w, "z", axis=0, tiled=True)
    if ny != 2:
        full = lax.all_gather(near.reshape((-1,) + w.shape), "y", axis=1)
        return full.reshape((-1,) + w.shape[1:])
    far = lax.ppermute(near, "y", SWAP)
    near = near.reshape((-1, 1) + w.shape)
    far = far.reshape((-1, 1) + w.shape)
    first = lax.axis_index("y") == 0
    full = jnp.concatenate([jnp.where(first, near, far), jnp.where(first, far, near)], axis=1)
    return full.reshape((-1,) + w.shape[1:])


def reduce_seq(g, nz, ny):
    rows = g.shape[0] // (nz * ny)
    g = g.reshape((nz, ny, rows) + g.shape[1:])
    if ny != 2:
        g = lax.psum_scatter(g, "y", scatter_dimension=1, tiled=True)
        return lax.psum_scatter(
            g.reshape((nz * rows,) + g.shape[3:]), "z", scatter_dimension=0, tiled=True
        )
    here = lax.axis_index("y")
    send = lax.dynamic_index_in_dim(g, 1 - here, 1, keepdims=False)
    got = lax.ppermute(send, "y", SWAP)
    keep = lax.dynamic_index_in_dim(g, here, 1, keepdims=False)
    both = (keep.astype(F32) + got.astype(F32)).astype(BF)
    return lax.psum_scatter(
        both.reshape((nz * rows,) + both.shape[2:]), "z", scatter_dimension=0, tiled=True
    )


def swap_batch(x):
    return lax.all_to_all(x, BATCH, split_axis=0, concat_axis=0, tiled=True)


def swap_seq(x):
    return lax.all_to_all(x, SEQ, split_axis=0, concat_axis=0, tiled=True)


def norm_stats(value):
    centred = value - jnp.mean(value, axis=-1, keepdims=True)
    scale = lax.rsqrt(jnp.mean(centred * centred, axis=-1, keepdims=True) + EPS)
    return centred * scale, scale


def norm_back(grad, unit, scale, gain):
    e = grad * gain
    back = scale * (
        e - jnp.mean(e, axis=-1, keepdims=True) - unit * jnp.mean(e * unit, axis=-1, keepdims=True)
    )
    return back, jnp.sum(grad * unit, axis=0), jnp.sum(grad, axis=0)


def turn(value, cosine, sine, lane):
    inner = lane % HEAD_DIM
    ahead = pltpu.roll(value, LANES - ROT // 2, 1)
    behind = pltpu.roll(value, ROT // 2, 1)
    return value * cosine + jnp.where(inner < ROT // 2, ahead, behind) * sine


def rotary_out_body(proj_ref, bias_ref, cos_ref, sin_ref, out_ref):
    value = proj_ref[...] + bias_ref[...]
    lane = lax.broadcasted_iota(jnp.int32, value.shape, 1)
    turned = turn(value, cos_ref[...], sin_ref[...], lane)
    value = jnp.where(pl.program_id(1) < 2, turned, value)
    out_ref[...] = value.astype(BF).reshape(out_ref.shape)


def rotary_out(proj, bias, cosine, sine, pairs, rpg, t):
    groups = proj.shape[0] // (rpg * t)
    block = rpg * t
    return pl.pallas_call(
        rotary_out_body,
        grid=(pairs * groups, 3),
        in_specs=[
            pl.BlockSpec((block, LANES), lambda d, p: (d % groups, p * pairs + d // groups)),
            pl.BlockSpec((1, LANES), lambda d, p: (0, p * pairs + d // groups)),
            pl.BlockSpec((block, LANES), lambda d, p: (d % groups, 0)),
            pl.BlockSpec((block, LANES), lambda d, p: (d % groups, 0)),
        ],
        out_specs=pl.BlockSpec((1, 1, rpg, t, LANES), lambda d, p: (d, p, 0, 0, 0)),
        out_shape=jax.ShapeDtypeStruct((pairs * groups, 3, rpg, t, LANES), BF),
        cost_estimate=pl.CostEstimate(
            flops=6 * proj.size, bytes_accessed=6 * proj.size, transcendentals=0
        ),
        name="rotary_out",
    )(proj, bias, cosine, sine)


def rotary_in_body(grad_ref, cos_ref, sin_ref, out_ref):
    value = grad_ref[...].reshape(out_ref.shape).astype(F32)
    lane = lax.broadcasted_iota(jnp.int32, value.shape, 1)
    turned = turn(value, cos_ref[...], -sin_ref[...], lane)
    out_ref[...] = jnp.where(pl.program_id(1) < 2, turned, value).astype(BF)


def rotary_in(grad, cosine, sine, pairs):
    dests, _, rpg, t, _ = grad.shape
    groups = dests // pairs
    block = rpg * t
    return pl.pallas_call(
        rotary_in_body,
        grid=(dests, 3),
        in_specs=[
            pl.BlockSpec((1, 1, rpg, t, LANES), lambda d, p: (d, p, 0, 0, 0)),
            pl.BlockSpec((block, LANES), lambda d, p: (d % groups, 0)),
            pl.BlockSpec((block, LANES), lambda d, p: (d % groups, 0)),
        ],
        out_specs=pl.BlockSpec((block, LANES), lambda d, p: (d % groups, p * pairs + d // groups)),
        out_shape=jax.ShapeDtypeStruct((groups * block, 3 * pairs * LANES), BF),
        cost_estimate=pl.CostEstimate(
            flops=6 * grad.size, bytes_accessed=4 * grad.size, transcendentals=0
        ),
        name="rotary_in",
    )(grad, cosine, sine)


def by_head(x):
    lane = lax.broadcasted_iota(jnp.int32, x.shape, 1)
    zero = jnp.zeros_like(x)
    return jnp.concatenate(
        [jnp.where(lane < HEAD_DIM, x, zero), jnp.where(lane >= HEAD_DIM, x, zero)], axis=0
    )


def one_head(x):
    t = x.shape[0] // 2
    lane = lax.broadcasted_iota(jnp.int32, (t, LANES), 1)
    return jnp.where(lane < HEAD_DIM, x[:t], x[t:])


def window_weights(q2, keys, start, row0, col0):
    scores = dot_nt(q2, keys) * (HEAD_DIM**-0.5)
    t = q2.shape[0] // 2
    shape = (t, keys.shape[0])
    rows = row0 + lax.broadcasted_iota(jnp.int32, shape, 0)
    cols = col0 + lax.broadcasted_iota(jnp.int32, shape, 1)
    allowed = (cols <= rows) & (cols >= start)
    allowed = jnp.concatenate([allowed, allowed], axis=0)
    scores = jnp.where(allowed, scores, NEG)
    weights = jnp.exp(scores - jnp.max(scores, axis=-1, keepdims=True))
    return weights / jnp.sum(weights, axis=-1, keepdims=True)


def forward_body(window, q_ref, k_ref, v_ref, start_ref, out_ref):
    number = pl.program_id(1)
    t = q_ref.shape[3]
    first = jnp.maximum(number - (window - 1), 0)
    keys = k_ref[pl.ds(first, window), 0, 0].reshape(window * t, LANES)
    values = v_ref[pl.ds(first, window), 0, 0].reshape(window * t, LANES)
    q2 = by_head(q_ref[0, 0, 0])
    weights = window_weights(q2, keys, start_ref[0, 0], number * t, first * t)
    out_ref[0, 0] = one_head(dot(weights.astype(BF), values)).astype(BF)


def attention_specs(blocks, t):
    return [
        pl.BlockSpec((1, 1, 1, t, LANES), lambda r, i: (i, 0, r, 0, 0)),
        pl.BlockSpec((blocks, 1, 1, t, LANES), lambda r, i: (0, 1, r, 0, 0)),
        pl.BlockSpec((blocks, 1, 1, t, LANES), lambda r, i: (0, 2, r, 0, 0)),
        pl.BlockSpec((1, 1, t, 1), lambda r, i: (r, i, 0, 0)),
    ]


def attend(qkv, start, window):
    blocks, _, rpg, t, _ = qkv.shape
    work = rpg * blocks * 2 * t * window * t
    return pl.pallas_call(
        functools.partial(forward_body, window),
        grid=(rpg, blocks),
        in_specs=attention_specs(blocks, t),
        out_specs=pl.BlockSpec((1, 1, t, LANES), lambda r, i: (i, r, 0, 0)),
        out_shape=jax.ShapeDtypeStruct((blocks, rpg, t, LANES), BF),
        cost_estimate=pl.CostEstimate(
            flops=4 * LANES * work, bytes_accessed=4 * qkv.size, transcendentals=work
        ),
        name="attend",
    )(qkv, qkv, qkv, start)


def backward_body(window, q_ref, k_ref, v_ref, start_ref, do_ref, out_ref, dk_ref, dv_ref):
    number = pl.program_id(1)
    t = q_ref.shape[3]
    scale = HEAD_DIM**-0.5

    @pl.when(number == 0)
    def _():
        dk_ref[...] = jnp.zeros_like(dk_ref)
        dv_ref[...] = jnp.zeros_like(dv_ref)

    first = jnp.maximum(number - (window - 1), 0)
    keys = k_ref[pl.ds(first, window), 0, 0].reshape(window * t, LANES)
    values = v_ref[pl.ds(first, window), 0, 0].reshape(window * t, LANES)
    q2 = by_head(q_ref[0, 0, 0])
    do2 = by_head(do_ref[0, 0])
    weights = window_weights(q2, keys, start_ref[0, 0], number * t, first * t)
    grad = dot_nt(do2, values)
    inner = jnp.sum(weights * grad, axis=-1, keepdims=True)
    ds = (weights * (grad - inner)).astype(BF)
    out_ref[number, 0, 0] = one_head(dot(ds, keys) * scale).astype(BF)
    shape = (window, t, LANES)
    dk_ref[pl.ds(first, window)] += dot_tn(ds, q2).reshape(shape)
    dv_ref[pl.ds(first, window)] += dot_tn(weights.astype(BF), do2).reshape(shape)

    @pl.when(number == pl.num_programs(1) - 1)
    def _():
        out_ref[:, 1, 0] = (dk_ref[...] * scale).astype(BF)
        out_ref[:, 2, 0] = dv_ref[...].astype(BF)


def attend_back(qkv, start, grad, window):
    blocks, _, rpg, t, _ = qkv.shape
    work = rpg * blocks * 2 * t * window * t
    return pl.pallas_call(
        functools.partial(backward_body, window),
        grid=(rpg, blocks),
        in_specs=attention_specs(blocks, t)
        + [pl.BlockSpec((1, 1, t, LANES), lambda r, i: (i, r, 0, 0))],
        out_specs=pl.BlockSpec((blocks, 3, 1, t, LANES), lambda r, i: (0, 0, r, 0, 0)),
        out_shape=jax.ShapeDtypeStruct((blocks, 3, rpg, t, LANES), BF),
        scratch_shapes=[
            pltpu.VMEM((blocks, t, LANES), F32),
            pltpu.VMEM((blocks, t, LANES), F32),
        ],
        cost_estimate=pl.CostEstimate(
            flops=10 * LANES * work, bytes_accessed=4 * qkv.size, transcendentals=work
        ),
        name="attend_back",
    )(qkv, qkv, qkv, start, grad)


def local(
    sizes,
    tokens_in,
    cotangent,
    segment_ids,
    attn_gain,
    attn_shift,
    qkv_weight,
    qkv_bias,
    out_weight,
    mlp_gain,
    mlp_shift,
    gate_weight,
    up_weight,
    down_weight,
):
    nz, ny, nx, nc = sizes
    seq, peers = nz * ny, nx * nc
    devices = seq * peers
    pair = nx == 2
    t, width = tokens_in.shape[1:]
    length = segment_ids.shape[1]
    heads = width // HEAD_DIM // peers
    pairs = heads // 2
    groups = seq // pairs
    rpg = peers // groups
    ff = down_weight.shape[0] * devices
    strip = ff // devices
    own_head = width // devices == HEAD_DIM
    window = min((length // 3 - 1 + t - 1) // t + 1, length // t)
    me_seq = lax.axis_index(SEQ)
    me_peer = lax.axis_index(BATCH)

    small = jnp.concatenate([attn_gain, attn_shift, mlp_gain, mlp_shift, qkv_bias])
    small = jnp.broadcast_to(small[None], (devices, small.size))
    small = lax.all_to_all(small, ALL, split_axis=0, concat_axis=0, tiled=True).astype(F32)
    each = attn_gain.size
    gain_one, shift_one, gain_two, shift_two = [
        small[:, i * each : (i + 1) * each].reshape(1, width) for i in range(4)
    ]
    bias = small[:, 4 * each :].reshape(3, heads, peers, HEAD_DIM)
    bias = lax.dynamic_index_in_dim(bias, me_peer, 2, keepdims=False).reshape(1, -1)

    rows = qkv_weight.shape[0]
    qkv_mine = qkv_weight.reshape(rows, 3, heads, peers, HEAD_DIM).transpose(3, 0, 1, 2, 4)
    qkv_mine = swap_batch(qkv_mine.reshape(peers, rows, -1)).reshape(peers * rows, -1)
    qkv_full = gather_seq(qkv_mine, ny)
    if own_head:
        out_full = gather_seq(out_weight, ny)
    else:
        out_full = lax.all_gather(out_weight, ALL, axis=0, tiled=True)
        out_full = out_full.reshape(heads, peers, HEAD_DIM, width)
        out_full = lax.dynamic_index_in_dim(out_full, me_peer, 1, keepdims=False)
        out_full = out_full.reshape(heads * HEAD_DIM, width)

    def columns(w):
        w = w.reshape(rows, seq, peers, strip).transpose(2, 0, 1, 3)
        w = swap_batch(w.reshape(peers, rows, -1))
        return gather_seq(w.reshape(peers * rows, -1), ny)

    gate_full = columns(gate_weight)
    up_full = columns(up_weight)
    down_full = gather_seq(down_weight, ny)

    segment = gather_batch(segment_ids, pair)
    start = jnp.zeros_like(segment)
    for doc in range(DOCS):
        count = jnp.sum((segment == doc).astype(jnp.int32), axis=1, keepdims=True)
        start = start + jnp.where(segment > doc, count, 0)
    places = me_seq * t + jnp.arange(t, dtype=jnp.int32)
    here = places[None] - lax.dynamic_slice_in_dim(start, me_seq * t, t, 1)
    half = ROT // 2
    inverse = 10000.0 ** (-jnp.arange(half, dtype=F32) / half)
    theta = inverse[:, None] * here.reshape(1, -1).astype(F32)
    cosine, sine = jnp.cos(theta), jnp.sin(theta)
    rest = jnp.ones((HEAD_DIM - ROT, theta.shape[1]), F32)
    cosine = jnp.concatenate([cosine, cosine, rest] * 2, axis=0).T
    sine = jnp.concatenate([-sine, sine, 0.0 * rest] * 2, axis=0).T
    start = lax.dynamic_slice_in_dim(start, (me_seq % groups) * rpg, rpg, 0)
    start = start.reshape(rpg, length // t, t, 1)

    inputs = tokens_in[0].astype(F32)
    unit_one, scale_one = norm_stats(inputs)
    normed = (unit_one * gain_one + shift_one).astype(BF)
    normed_all = gather_batch(normed, pair)
    proj = dot(normed_all, qkv_full)
    qkv = rotary_out(proj, bias, cosine, sine, pairs, rpg, t)
    qkv = swap_seq(qkv)
    mixed = swap_seq(attend(qkv, start, window))

    def token_rows(x):
        x = x.reshape(pairs, groups * rpg * t, LANES).transpose(1, 0, 2)
        return x.reshape(groups * rpg * t, pairs * LANES)

    def head_rows(x):
        x = x.reshape(groups * rpg * t, pairs, LANES).transpose(1, 0, 2)
        return x.reshape(seq, rpg, t, LANES)

    mixed = token_rows(mixed)
    hidden = inputs + reduce_batch(dot(mixed, out_full, BF), pair)

    unit_two, scale_two = norm_stats(hidden)
    normed_two = (unit_two * gain_two + shift_two).astype(BF)
    normed_two_all = gather_batch(normed_two, pair)
    grad_output = cotangent[0]
    grad_all = gather_batch(grad_output, pair)
    gate = dot(normed_two_all, gate_full)
    up = dot(normed_two_all, up_full)
    sigmoid = jax.nn.sigmoid(gate)
    act = (gate * sigmoid * up).astype(BF)
    block_out = hidden + reduce_batch(dot(act, down_full, BF), pair)
    block_out = block_out.astype(BF).reshape(tokens_in.shape)

    grad_down = reduce_seq(dot_tn(act, grad_all, BF), nz, ny).astype(F32)
    grad_act = dot_nt(grad_all, down_full)
    grad_gate = (grad_act * up * sigmoid * (1.0 + gate * (1.0 - sigmoid))).astype(BF)
    grad_up = (grad_act * gate * sigmoid).astype(BF)
    part = dot_nt(grad_gate, gate_full) + dot_nt(grad_up, up_full)
    grad_normed_two = reduce_batch(part.astype(BF), pair)

    def uncolumns(g):
        g = reduce_seq(g, nz, ny).reshape(peers, rows, -1)
        return swap_batch(g)

    def ff_columns(g):
        g = uncolumns(g).reshape(peers, rows, seq, strip).transpose(1, 2, 0, 3)
        return g.reshape(rows, ff).astype(F32)

    grad_gate_w = ff_columns(dot_tn(normed_two_all, grad_gate, BF))
    grad_up_w = ff_columns(dot_tn(normed_two_all, grad_up, BF))
    back, grad_gain_two, grad_shift_two = norm_back(grad_normed_two, unit_two, scale_two, gain_two)
    grad_hidden = grad_output.astype(F32) + back

    branch = gather_batch(grad_hidden.astype(BF), pair)
    grad_out = dot_tn(mixed, branch, BF)
    if own_head:
        grad_out = reduce_seq(grad_out, nz, ny).astype(F32)
    else:
        mine = (jnp.arange(peers) == me_peer).astype(BF)[None, :, None, None]
        grad_out = grad_out.reshape(heads, 1, HEAD_DIM, width) * mine
        grad_out = lax.psum_scatter(
            grad_out.reshape(width, width), ALL, scatter_dimension=0, tiled=True
        ).astype(F32)
    grad_mixed = head_rows(dot_nt(branch, out_full, BF))
    grad_qkv = attend_back(qkv, start, swap_seq(grad_mixed), window)
    grad_proj = rotary_in(swap_seq(grad_qkv), cosine, sine, pairs)
    grad_qkv_w = uncolumns(dot_tn(normed_all, grad_proj, BF))
    grad_qkv_w = grad_qkv_w.reshape(peers, rows, 3, heads, HEAD_DIM).transpose(1, 2, 3, 0, 4)
    grad_qkv_w = grad_qkv_w.reshape(rows, 3 * width).astype(F32)
    grad_bias = jnp.sum(grad_proj.astype(F32), axis=0).reshape(3, heads, 1, HEAD_DIM)
    mine = (jnp.arange(peers) == me_peer).astype(F32)[None, None, :, None]
    grad_bias = (grad_bias * mine).reshape(devices, -1)
    grad_normed = reduce_batch(dot_nt(grad_proj, qkv_full, BF), pair)
    back, grad_gain_one, grad_shift_one = norm_back(grad_normed, unit_one, scale_one, gain_one)
    grad_tokens = (grad_hidden + back).astype(BF).reshape(tokens_in.shape)

    vectors = [grad_gain_one, grad_shift_one, grad_gain_two, grad_shift_two]
    vectors = [v.reshape(devices, each) for v in vectors] + [grad_bias]
    vectors = jnp.concatenate(vectors, axis=1)
    vectors = lax.all_to_all(vectors, ALL, split_axis=0, concat_axis=0, tiled=True)
    vectors = jnp.sum(vectors, axis=0)
    g1, s1, g2, s2 = [vectors[i * each : (i + 1) * each] for i in range(4)]
    return (
        block_out,
        grad_tokens,
        g1,
        s1,
        grad_qkv_w,
        vectors[4 * each :],
        grad_out,
        g2,
        s2,
        grad_gate_w,
        grad_up_w,
        grad_down,
    )


def solution(mesh):
    seq, batch = mesh.shape["seq"], mesh.shape["batch"]
    sizes = (4, seq // 4, batch // 2, 2)
    fine = Mesh(mesh.devices.reshape(sizes), ALL)
    token = P(BATCH, SEQ, None)
    vector = P(ALL)
    matrix = P(ALL, None)
    return jax.shard_map(
        functools.partial(local, sizes),
        mesh=fine,
        in_specs=(
            token,
            token,
            P(BATCH, None),
            vector,
            vector,
            matrix,
            vector,
            matrix,
            vector,
            vector,
            matrix,
            matrix,
            matrix,
        ),
        out_specs=(
            token,
            token,
            vector,
            vector,
            matrix,
            vector,
            matrix,
            vector,
            vector,
            matrix,
            matrix,
            matrix,
        ),
        check_vma=False,
    )
```

```python
import functools

import jax
import jax.numpy as jnp
from jax import lax
from jax.experimental import pallas as pl
from jax.experimental.pallas import tpu as pltpu
from jax.sharding import Mesh
from jax.sharding import PartitionSpec as P

HEAD_DIM = 64
ROT = 16
DOCS = 6
LANES = 128
EPS = 1e-05
BF = jnp.bfloat16
F32 = jnp.float32
NEG = -1e30
ALL = ("z", "y", "x", "c")
SEQ = ("z", "y")
BATCH = ("x", "c")
SWAP = ((0, 1), (1, 0))


def dot(a, b, out=F32):
    return jnp.dot(a, b, preferred_element_type=out)


def dot_nt(a, b, out=F32):
    return lax.dot_general(a, b, (((1,), (1,)), ((), ())), preferred_element_type=out)


def dot_tn(a, b, out=F32):
    return lax.dot_general(a, b, (((0,), (0,)), ((), ())), preferred_element_type=out)


def after(x, *first):
    return lax.optimization_barrier((x,) + first)[0]


def gather_peers(x, axis):
    if axis is None:
        return lax.all_gather(x, BATCH, axis=0, tiled=True)
    other = lax.ppermute(x, axis, SWAP)
    near = jnp.concatenate([x, other], axis=0)
    far = lax.ppermute(near, "c", SWAP)
    return jnp.concatenate([near, far], axis=0)


def reduce_peers(part, axis):
    if axis is None:
        return lax.psum_scatter(part, BATCH, scatter_dimension=0, tiled=True).astype(F32)
    rows = part.shape[0] // 4
    got = lax.ppermute(part[2 * rows :], "c", SWAP)
    send = (part[rows : 2 * rows].astype(F32) + got[rows:].astype(F32)).astype(BF)
    last = lax.ppermute(send, axis, SWAP)
    return part[:rows].astype(F32) + got[:rows].astype(F32) + last.astype(F32)


def gather_z(w):
    return lax.all_gather(w, "z", axis=0, tiled=True)


def gather_far(near, axis):
    if axis is None:
        return lax.all_gather(near, "y", axis=0)
    return lax.ppermute(near, axis, SWAP)


def merge_rows(near, far, axis, nz, inner=1):
    wide = near.shape[-1]
    if axis is None:
        far = far.reshape(far.shape[0], nz, -1, wide).transpose(1, 0, 2, 3)
        return far.reshape(-1, wide)
    near = near.reshape(nz * inner, 1, -1, wide)
    far = far.reshape(near.shape)
    first = lax.axis_index(axis) == 0
    full = jnp.concatenate([jnp.where(first, near, far), jnp.where(first, far, near)], axis=1)
    return full.reshape(-1, wide)


def send_rows(g, axis, nz, na, inner=1):
    rows = g.shape[0] // (nz * na)
    if axis is None:
        g = g.reshape(nz, na, rows, -1).transpose(1, 0, 2, 3).reshape(na, nz * rows, -1)
        return None, lax.psum_scatter(g, "y", scatter_dimension=0, tiled=True)[0]
    g = g.reshape(nz * inner, na, rows // inner, g.shape[1])
    here = lax.axis_index(axis)
    send = lax.dynamic_index_in_dim(g, 1 - here, 1, keepdims=False)
    keep = lax.dynamic_index_in_dim(g, here, 1, keepdims=False)
    return keep, lax.ppermute(send, axis, SWAP)


def add_rows(keep, got):
    if keep is None:
        return got
    got = (keep.astype(F32) + got.astype(F32)).astype(BF)
    return got.reshape(-1, got.shape[-1])


def scatter_z(g):
    return lax.psum_scatter(g, "z", scatter_dimension=0, tiled=True)


def reduce_z(keep, got):
    return scatter_z(add_rows(keep, got))


def swap_peers(x, axes):
    return lax.all_to_all(x, axes, split_axis=0, concat_axis=0, tiled=True)


def swap_seq(x):
    return lax.all_to_all(x, SEQ, split_axis=0, concat_axis=0, tiled=True)


def norm_stats(value):
    centred = value - jnp.mean(value, axis=-1, keepdims=True)
    scale = lax.rsqrt(jnp.mean(centred * centred, axis=-1, keepdims=True) + EPS)
    return centred * scale, scale


def norm_back(grad, unit, scale, gain):
    e = grad * gain
    back = scale * (
        e - jnp.mean(e, axis=-1, keepdims=True) - unit * jnp.mean(e * unit, axis=-1, keepdims=True)
    )
    return back, jnp.sum(grad * unit, axis=0), jnp.sum(grad, axis=0)


def turn(value, cosine, sine, lane):
    inner = lane % HEAD_DIM
    ahead = pltpu.roll(value, LANES - ROT // 2, 1)
    behind = pltpu.roll(value, ROT // 2, 1)
    return value * cosine + jnp.where(inner < ROT // 2, ahead, behind) * sine


def rotary_out_body(turned, proj_ref, bias_ref, cos_ref, sin_ref, out_ref):
    pairs = out_ref.shape[0]
    cosine, sine = cos_ref[...], sin_ref[...]
    lane = lax.broadcasted_iota(jnp.int32, cosine.shape, 1)
    rotate = pl.program_id(1) < turned
    for i in range(pairs):
        at = slice(i * LANES, (i + 1) * LANES)
        value = proj_ref[:, at] + bias_ref[:, at]
        value = jnp.where(rotate, turn(value, cosine, sine, lane), value)
        out_ref[i] = value.astype(BF).reshape(out_ref.shape[1:])


def rotary_out(proj, bias, cosine, sine, pairs, rpg, t, turned):
    peers = proj.shape[0] // t
    groups = peers // rpg
    wide = pairs * LANES
    parts = proj.shape[1] // wide
    out = pl.pallas_call(
        functools.partial(rotary_out_body, turned),
        grid=(peers, parts),
        in_specs=[
            pl.BlockSpec((t, wide), lambda b, p: (b, p)),
            pl.BlockSpec((1, wide), lambda b, p: (0, p)),
            pl.BlockSpec((t, LANES), lambda b, p: (b, 0)),
            pl.BlockSpec((t, LANES), lambda b, p: (b, 0)),
        ],
        out_specs=pl.BlockSpec(
            (pairs, 1, 1, 1, t, LANES), lambda b, p: (0, b // rpg, p, b % rpg, 0, 0)
        ),
        out_shape=jax.ShapeDtypeStruct((pairs, groups, parts, rpg, t, LANES), BF),
        cost_estimate=pl.CostEstimate(
            flops=1, bytes_accessed=1, transcendentals=0
        ),
        name="rotary_out",
    )(proj, bias, cosine, sine)
    return out.reshape((pairs * groups,) + out.shape[2:])


def rotary_in_body(grad_ref, cos_ref, sin_ref, out_ref):
    pairs = grad_ref.shape[0]
    cosine, sine = cos_ref[...], -sin_ref[...]
    lane = lax.broadcasted_iota(jnp.int32, cosine.shape, 1)
    rotate = pl.program_id(1) < 2
    for i in range(pairs):
        value = grad_ref[i].reshape(cosine.shape).astype(F32)
        value = jnp.where(rotate, turn(value, cosine, sine, lane), value)
        out_ref[:, i * LANES : (i + 1) * LANES] = value.astype(BF)


def rotary_in(grad, cosine, sine, pairs):
    dests, parts, rpg, t, _ = grad.shape
    groups = dests // pairs
    wide = pairs * LANES
    return pl.pallas_call(
        rotary_in_body,
        grid=(groups * rpg, parts),
        in_specs=[
            pl.BlockSpec(
                (pairs, 1, 1, 1, t, LANES), lambda b, p: (0, b // rpg, p, b % rpg, 0, 0)
            ),
            pl.BlockSpec((t, LANES), lambda b, p: (b, 0)),
            pl.BlockSpec((t, LANES), lambda b, p: (b, 0)),
        ],
        out_specs=pl.BlockSpec((t, wide), lambda b, p: (b, p)),
        out_shape=jax.ShapeDtypeStruct((groups * rpg * t, parts * wide), BF),
        cost_estimate=pl.CostEstimate(
            flops=1, bytes_accessed=1, transcendentals=0
        ),
        name="rotary_in",
    )(grad.reshape((pairs, groups) + grad.shape[1:]), cosine, sine)


def by_head(x):
    lane = lax.broadcasted_iota(jnp.int32, x.shape, 1)
    zero = jnp.zeros_like(x)
    return jnp.concatenate(
        [jnp.where(lane < HEAD_DIM, x, zero), jnp.where(lane >= HEAD_DIM, x, zero)], axis=0
    )


def one_head(x):
    t = x.shape[0] // 2
    lane = lax.broadcasted_iota(jnp.int32, (t, LANES), 1)
    return jnp.where(lane < HEAD_DIM, x[:t], x[t:])


def window_weights(q2, keys, start, row0, col0):
    scores = dot_nt(q2, keys) * (HEAD_DIM**-0.5)
    t = q2.shape[0] // 2
    shape = (t, keys.shape[0])
    rows = row0 + lax.broadcasted_iota(jnp.int32, shape, 0)
    cols = col0 + lax.broadcasted_iota(jnp.int32, shape, 1)
    allowed = (cols <= rows) & (cols >= start)
    allowed = jnp.concatenate([allowed, allowed], axis=0)
    scores = jnp.where(allowed, scores, NEG)
    weights = jnp.exp(scores - jnp.max(scores, axis=-1, keepdims=True))
    return weights / jnp.sum(weights, axis=-1, keepdims=True)


def forward_body(window, q_ref, k_ref, v_ref, start_ref, out_ref):
    number = pl.program_id(1)
    t = q_ref.shape[3]
    first = jnp.maximum(number - (window - 1), 0)
    keys = k_ref[pl.ds(first, window), 0, 0].reshape(window * t, LANES)
    values = v_ref[pl.ds(first, window), 0, 0].reshape(window * t, LANES)
    q2 = by_head(q_ref[0, 0, 0])
    weights = window_weights(q2, keys, start_ref[0, 0], number * t, first * t)
    out_ref[0, 0] = one_head(dot(weights.astype(BF), values)).astype(BF)


def attention_specs(blocks, t):
    return [
        pl.BlockSpec((1, 1, 1, t, LANES), lambda r, i: (i, 0, r, 0, 0)),
        pl.BlockSpec((blocks, 1, 1, t, LANES), lambda r, i: (0, 0, r, 0, 0)),
        pl.BlockSpec((blocks, 1, 1, t, LANES), lambda r, i: (0, 1, r, 0, 0)),
        pl.BlockSpec((1, 1, t, 1), lambda r, i: (r, i, 0, 0)),
    ]


def attend(q, kv, start, window):
    blocks, _, rpg, t, _ = q.shape
    work = rpg * blocks * 2 * t * window * t
    return pl.pallas_call(
        functools.partial(forward_body, window),
        grid=(rpg, blocks),
        in_specs=attention_specs(blocks, t),
        out_specs=pl.BlockSpec((1, 1, t, LANES), lambda r, i: (i, r, 0, 0)),
        out_shape=jax.ShapeDtypeStruct((blocks, rpg, t, LANES), BF),
        cost_estimate=pl.CostEstimate(
            flops=1, bytes_accessed=1, transcendentals=0
        ),
        name="attend",
    )(q, kv, kv, start)


def backward_body(window, q_ref, k_ref, v_ref, start_ref, do_ref, out_ref, dk_ref, dv_ref):
    number = pl.program_id(1)
    t = q_ref.shape[3]
    scale = HEAD_DIM**-0.5

    @pl.when(number == 0)
    def _():
        dk_ref[...] = jnp.zeros_like(dk_ref)
        dv_ref[...] = jnp.zeros_like(dv_ref)

    first = jnp.maximum(number - (window - 1), 0)
    keys = k_ref[pl.ds(first, window), 0, 0].reshape(window * t, LANES)
    values = v_ref[pl.ds(first, window), 0, 0].reshape(window * t, LANES)
    q2 = by_head(q_ref[0, 0, 0])
    do2 = by_head(do_ref[0, 0])
    weights = window_weights(q2, keys, start_ref[0, 0], number * t, first * t)
    grad = dot_nt(do2, values)
    inner = jnp.sum(weights * grad, axis=-1, keepdims=True)
    ds = (weights * (grad - inner)).astype(BF)
    out_ref[number, 0, 0] = one_head(dot(ds, keys) * scale).astype(BF)
    shape = (window, t, LANES)
    dk_ref[pl.ds(first, window)] += dot_tn(ds, q2).reshape(shape)
    dv_ref[pl.ds(first, window)] += dot_tn(weights.astype(BF), do2).reshape(shape)

    @pl.when(number == pl.num_programs(1) - 1)
    def _():
        out_ref[:, 1, 0] = (dk_ref[...] * scale).astype(BF)
        out_ref[:, 2, 0] = dv_ref[...].astype(BF)


def attend_back(q, kv, start, grad, window):
    blocks, _, rpg, t, _ = q.shape
    work = rpg * blocks * 2 * t * window * t
    return pl.pallas_call(
        functools.partial(backward_body, window),
        grid=(rpg, blocks),
        in_specs=attention_specs(blocks, t)
        + [pl.BlockSpec((1, 1, t, LANES), lambda r, i: (i, r, 0, 0))],
        out_specs=pl.BlockSpec((blocks, 3, 1, t, LANES), lambda r, i: (0, 0, r, 0, 0)),
        out_shape=jax.ShapeDtypeStruct((blocks, 3, rpg, t, LANES), BF),
        scratch_shapes=[
            pltpu.VMEM((blocks, t, LANES), F32),
            pltpu.VMEM((blocks, t, LANES), F32),
        ],
        cost_estimate=pl.CostEstimate(
            flops=1, bytes_accessed=1, transcendentals=0
        ),
        name="attend_back",
    )(q, kv, kv, start, grad)


FREE = pl.CostEstimate(flops=1, bytes_accessed=1, transcendentals=0)


def split_body(here_ref, x_ref, out_ref):
    count = x_ref.shape[1] // LANES
    first = here_ref[0] == 0
    for i in range(count):
        place = (i % 2) * (count // 2) + i // 2
        other = (1 - i % 2) * (count // 2) + i // 2
        value = x_ref[:, i * LANES : (i + 1) * LANES]

        @pl.when(first)
        def _():
            out_ref[:, place * LANES : (place + 1) * LANES] = value

        @pl.when(jnp.logical_not(first))
        def _():
            out_ref[:, other * LANES : (other + 1) * LANES] = value


def join_body(here_ref, x_ref, out_ref):
    count = x_ref.shape[1] // LANES
    first = here_ref[0] == 0
    for i in range(count):
        place = (i % 2) * (count // 2) + i // 2
        other = (1 - i % 2) * (count // 2) + i // 2
        one = x_ref[:, place * LANES : (place + 1) * LANES]
        two = x_ref[:, other * LANES : (other + 1) * LANES]
        out_ref[:, i * LANES : (i + 1) * LANES] = jnp.where(first, one, two)


def regroup(body, here, x, name):
    return pl.pallas_call(
        body,
        in_specs=[
            pl.BlockSpec(memory_space=pltpu.SMEM),
            pl.BlockSpec(memory_space=pltpu.VMEM),
        ],
        out_specs=pl.BlockSpec(memory_space=pltpu.VMEM),
        out_shape=jax.ShapeDtypeStruct(x.shape, x.dtype),
        cost_estimate=FREE,
        name=name,
    )(here.reshape(1), x)


def hidden_body(x_ref, gn_ref, gf_ref, un_ref, uf_ref, gate_ref, up_ref, act_ref):
    k = gn_ref.shape[0]
    tile = gn_ref.shape[1]
    near = jnp.concatenate([gn_ref[...], un_ref[...]], axis=1)
    far = jnp.concatenate([gf_ref[...], uf_ref[...]], axis=1)
    both = dot(x_ref[:, :k], near) + dot(x_ref[:, k:], far)
    gate, up = both[:, :tile], both[:, tile:]
    gate_ref[...] = gate
    up_ref[...] = up
    act_ref[...] = (gate * jax.nn.sigmoid(gate) * up).astype(BF)


def hidden_units(x, gate, up):
    m, width = x.shape
    k, n = gate[0].shape
    weight = pl.BlockSpec((k, LANES), lambda j: (0, j))
    tile = pl.BlockSpec((m, LANES), lambda j: (0, j))
    return pl.pallas_call(
        hidden_body,
        grid=(pl.cdiv(n, LANES),),
        in_specs=[pl.BlockSpec((m, width), lambda j: (0, 0))] + [weight] * 4,
        out_specs=[tile] * 3,
        out_shape=[jax.ShapeDtypeStruct((m, n), d) for d in (F32, F32, BF)],
        cost_estimate=FREE,
        name="hidden_units",
    )(x, *gate, *up)


def hidden_back_body(grad_ref, down_ref, gate_ref, up_ref, gg_ref, gu_ref):
    grad = dot_nt(grad_ref[...], down_ref[...])
    gate = gate_ref[...]
    sigmoid = jax.nn.sigmoid(gate)
    gg_ref[...] = (grad * up_ref[...] * sigmoid * (1.0 + gate * (1.0 - sigmoid))).astype(BF)
    gu_ref[...] = (grad * gate * sigmoid).astype(BF)


def hidden_back(grad, down, gate, up, t):
    m, width = grad.shape
    n = down.shape[0]
    tile = pl.BlockSpec((t, n), lambda i: (i, 0))
    return pl.pallas_call(
        hidden_back_body,
        grid=(m // t,),
        in_specs=[
            pl.BlockSpec((t, width), lambda i: (i, 0)),
            pl.BlockSpec((n, width), lambda i: (0, 0)),
            tile,
            tile,
        ],
        out_specs=[tile] * 2,
        out_shape=[jax.ShapeDtypeStruct((m, n), BF)] * 2,
        cost_estimate=FREE,
        name="hidden_back",
    )(grad, down, gate, up)


def input_back_body(steps, gg_ref, gu_ref, gn_ref, gf_ref, un_ref, uf_ref, out_ref):
    @pl.when(pl.program_id(0) < steps)
    def _():
        part = dot_nt(gg_ref[...], gn_ref[...]) + dot_nt(gu_ref[...], un_ref[...])
        out_ref[...] = part.astype(BF)

    @pl.when(pl.program_id(0) >= steps)
    def _():
        part = dot_nt(gg_ref[...], gf_ref[...]) + dot_nt(gu_ref[...], uf_ref[...])
        out_ref[...] = part.astype(BF)


def input_back(grad_gate, grad_up, gate, up):
    m, n = grad_gate.shape
    k = gate[0].shape[0]
    tile = 2 * LANES
    steps = k // tile
    whole = pl.BlockSpec((m, n), lambda i: (0, 0))
    near = pl.BlockSpec((tile, n), lambda i: (jnp.minimum(i, steps - 1), 0))
    far = pl.BlockSpec((tile, n), lambda i: (jnp.maximum(i - steps, 0), 0))
    return pl.pallas_call(
        functools.partial(input_back_body, steps),
        grid=(2 * steps,),
        in_specs=[whole, whole, near, far, near, far],
        out_specs=pl.BlockSpec((m, tile), lambda i: (0, i)),
        out_shape=jax.ShapeDtypeStruct((m, 2 * k), BF),
        cost_estimate=FREE,
        name="input_back",
    )(grad_gate, grad_up, *gate, *up)


def local(
    sizes,
    tokens_in,
    cotangent,
    segment_ids,
    attn_gain,
    attn_shift,
    qkv_weight,
    qkv_bias,
    out_weight,
    mlp_gain,
    mlp_shift,
    gate_weight,
    up_weight,
    down_weight,
):
    nz, ny, nx, nc = sizes
    seq, peers = nz * ny, nx * nc
    devices = seq * peers
    pair = nx == 2 and ny == 2
    att, att_rows = ("x", "y") if pair else (None, None)
    fwd, fwd_rows = ("y", "x") if pair else (None, None)
    fwd_axes = ("y", "c") if pair else BATCH
    t, width = tokens_in.shape[1:]
    length = segment_ids.shape[1]
    heads = width // HEAD_DIM // peers
    pairs = heads // 2
    groups = seq // pairs
    rpg = peers // groups
    ff = down_weight.shape[0] * devices
    strip = ff // devices
    own_head = width // devices == HEAD_DIM
    window = min((length // 3 - 1 + t - 1) // t + 1, length // t)
    me_seq = lax.axis_index(SEQ)
    me_peer = lax.axis_index(BATCH)

    small = jnp.concatenate([attn_gain, attn_shift, mlp_gain, mlp_shift, qkv_bias])
    small = jnp.broadcast_to(small[None], (devices, small.size))
    small = lax.all_to_all(small, ALL, split_axis=0, concat_axis=0, tiled=True).astype(F32)
    each = attn_gain.size
    gain_one, shift_one, gain_two, shift_two = [
        small[:, i * each : (i + 1) * each].reshape(1, width) for i in range(4)
    ]
    bias = small[:, 4 * each :].reshape(3, heads, peers, HEAD_DIM)
    bias = lax.dynamic_index_in_dim(bias, me_peer, 2, keepdims=False).reshape(1, -1)

    rows = qkv_weight.shape[0]
    third = width // peers
    qkv_mine = qkv_weight.reshape(rows, 3, heads, peers, HEAD_DIM).transpose(3, 0, 1, 2, 4)
    qkv_mine = swap_peers(qkv_mine.reshape(peers, rows, -1), BATCH).reshape(peers * rows, -1)

    def columns(w):
        if pair:
            w = w.reshape(rows, nz, 2, 2, nc, strip).transpose(2, 4, 0, 1, 3, 5)
        else:
            w = w.reshape(rows, seq, peers, strip).transpose(2, 0, 1, 3)
        return w.reshape(peers, rows, -1)

    mine = jnp.concatenate([columns(gate_weight), columns(up_weight)], axis=1)
    mine = swap_peers(mine, fwd_axes)
    gate_mine = mine[:, :rows].reshape(peers * rows, -1)
    up_mine = mine[:, rows:].reshape(peers * rows, -1)

    merge_att = functools.partial(merge_rows, axis=att_rows, nz=nz)
    merge_ff = functools.partial(merge_rows, axis=fwd_rows, nz=nz)
    split = 2 if pair else 1
    q_near = gather_z(qkv_mine[:, :third])
    kv_near = gather_z(qkv_mine[:, third:])
    q_near, gate_mine, up_mine = lax.optimization_barrier((q_near, gate_mine, up_mine))
    q_full = merge_att(q_near, gather_far(q_near, att_rows))
    kv_full = merge_att(kv_near, gather_far(kv_near, att_rows))
    if own_head:
        out_near = gather_z(out_weight)
    else:
        out_full = lax.all_gather(out_weight, ALL, axis=0, tiled=True)
        out_full = out_full.reshape(heads, peers, HEAD_DIM, width)
        out_full = lax.dynamic_index_in_dim(out_full, me_peer, 1, keepdims=False)
        out_full = out_full.reshape(heads * HEAD_DIM, width)
    gate_near = gather_z(gate_mine)
    gate_far = gather_far(gate_near, fwd_rows)

    segment = gather_peers(segment_ids, att)
    start = jnp.zeros_like(segment)
    for doc in range(DOCS):
        count = jnp.sum((segment == doc).astype(jnp.int32), axis=1, keepdims=True)
        start = start + jnp.where(segment > doc, count, 0)
    places = me_seq * t + jnp.arange(t, dtype=jnp.int32)
    here = places[None] - lax.dynamic_slice_in_dim(start, me_seq * t, t, 1)
    half = ROT // 2
    inverse = 10000.0 ** (-jnp.arange(half, dtype=F32) / half)
    theta = inverse[:, None] * here.reshape(1, -1).astype(F32)
    cosine, sine = jnp.cos(theta), jnp.sin(theta)
    rest = jnp.ones((HEAD_DIM - ROT, theta.shape[1]), F32)
    cosine = jnp.concatenate([cosine, cosine, rest] * 2, axis=0).T
    sine = jnp.concatenate([-sine, sine, 0.0 * rest] * 2, axis=0).T
    start = lax.dynamic_slice_in_dim(start, (me_seq % groups) * rpg, rpg, 0)
    start = start.reshape(rpg, length // t, t, 1)

    inputs = tokens_in[0].astype(F32)
    unit_one, scale_one = norm_stats(inputs)
    normed = (unit_one * gain_one + shift_one).astype(BF)
    normed_all = gather_peers(normed, att)
    query = rotary_out(dot(normed_all, q_full), bias[:, :third], cosine, sine, pairs, rpg, t, 1)
    query = swap_seq(query)
    key_value = dot(normed_all, kv_full)
    key_value = rotary_out(key_value, bias[:, third:], cosine, sine, pairs, rpg, t, 1)
    if own_head:
        key_value, out_near = lax.optimization_barrier((key_value, out_near))
        out_full = merge_att(out_near, gather_far(out_near, att_rows))
    key_value = swap_seq(key_value)
    up_near = gather_z(up_mine)
    up_far = gather_far(up_near, fwd_rows)
    down_near = gather_z(down_weight)
    grad_output = cotangent[0]
    grad_all = gather_peers(grad_output, fwd)
    query, key_value, gate_far = lax.optimization_barrier((query, key_value, gate_far))
    mixed = swap_seq(attend(query, key_value, start, window))
    mixed, up_far, down_near, grad_all = lax.optimization_barrier(
        (mixed, up_far, down_near, grad_all)
    )

    def token_rows(x):
        x = x.reshape(pairs, groups * rpg * t, LANES).transpose(1, 0, 2)
        return x.reshape(groups * rpg * t, pairs * LANES)

    def head_rows(x):
        x = x.reshape(groups * rpg * t, pairs, LANES).transpose(1, 0, 2)
        return x.reshape(seq, rpg, t, LANES)

    mixed = token_rows(mixed)
    hidden = inputs + reduce_peers(dot(mixed, out_full, BF), att)

    unit_two, scale_two = norm_stats(hidden)
    normed_two = (unit_two * gain_two + shift_two).astype(BF)
    down_far = gather_far(after(down_near, hidden), fwd_rows)
    if pair:
        here_x = lax.axis_index("x")
        normed_two = regroup(split_body, here_x, normed_two, "own_first")
        gate_full, up_full = (gate_near, gate_far), (up_near, up_far)
    else:
        gate_full = jnp.split(merge_ff(gate_near, gate_far), 2)
        up_full = jnp.split(merge_ff(up_near, up_far), 2)
    normed_two_all = gather_peers(normed_two, fwd)
    gate, up, act = hidden_units(normed_two_all, gate_full, up_full)
    down_full = merge_ff(down_near, down_far)
    down_part = dot(act, down_full, BF)

    send_att = functools.partial(send_rows, axis=att_rows, nz=nz, na=ny)
    send_ff = functools.partial(send_rows, axis=fwd_rows, nz=nz, na=nx if pair else ny)
    wide = width // 2
    down_one = send_ff(dot_tn(act, grad_all[:, :wide], BF))
    down_two = send_ff(dot_tn(act, grad_all[:, wide:], BF))
    grad_gate, grad_up = hidden_back(grad_all, down_full, gate, up, t)
    part = input_back(grad_gate, grad_up, gate_full, up_full)
    branch_two = reduce_peers(down_part, fwd)
    part, branch_two, down_one = lax.optimization_barrier((part, branch_two, down_one))
    block_out = (hidden + branch_two).astype(BF).reshape(tokens_in.shape)
    grad_normed_two = reduce_peers(part, fwd)

    def send_columns(g):
        if not pair:
            return send_ff(dot_tn(normed_two_all, g, BF))
        far = dot_tn(normed_two_all[:, wide:], g, BF)
        near = dot_tn(normed_two_all[:, :wide], g, BF)
        return near, lax.ppermute(far, "x", SWAP)

    cut_ff = grad_gate.shape[1] // 256 * 128 + LANES
    pieces = [g[:, at] for g in (grad_gate, grad_up) for at in (slice(0, cut_ff), slice(cut_ff, None))]
    gate_one, gate_two, up_one, up_two = [send_columns(g) for g in pieces]
    grad_normed_two, down_two = lax.optimization_barrier((grad_normed_two, down_two))
    grad_down = [reduce_z(*down_one), reduce_z(*down_two)]
    if pair:
        grad_normed_two = regroup(join_body, here_x, grad_normed_two, "own_back")
    back, grad_gain_two, grad_shift_two = norm_back(grad_normed_two, unit_two, scale_two, gain_two)
    grad_hidden = grad_output.astype(F32) + back

    def ff_columns(*parts):
        g = jnp.concatenate(parts, axis=1)
        g = swap_peers(g.reshape(peers, rows, -1), fwd_axes)
        if pair:
            g = g.reshape(2, nc, rows, nz, 2, strip).transpose(2, 3, 0, 4, 1, 5)
        else:
            g = g.reshape(peers, rows, seq, strip).transpose(1, 2, 0, 3)
        return g.reshape(rows, ff).astype(F32)

    branch = gather_peers(grad_hidden.astype(BF), att)
    grad_mixed = head_rows(dot_nt(branch, out_full, BF))
    grad_mixed = swap_seq(grad_mixed)
    grad_out = dot_tn(mixed, branch, BF)
    grad_mixed, gate_one, grad_out = lax.optimization_barrier((grad_mixed, gate_one, grad_out))
    gate_one = reduce_z(*gate_one)
    grad_qkv = attend_back(query, key_value, start, grad_mixed, window)
    if own_head:
        grad_out = send_att(grad_out)
    grad_qkv, gate_two = lax.optimization_barrier((grad_qkv, gate_two))
    gate_two = reduce_z(*gate_two)
    grad_qkv = swap_seq(grad_qkv)
    grad_down = jnp.concatenate(grad_down, axis=1).astype(F32)
    up_one, up_two = add_rows(*up_one), add_rows(*up_two)
    if own_head:
        grad_out = add_rows(*grad_out)
    grad_qkv, up_one, up_two, grad_out, grad_down = lax.optimization_barrier(
        (grad_qkv, up_one, up_two, grad_out, grad_down)
    )
    if own_head:
        grad_out = scatter_z(grad_out)
    up_one, up_two = scatter_z(up_one), scatter_z(up_two)
    if not own_head:
        mine = (jnp.arange(peers) == me_peer).astype(BF)[None, :, None, None]
        grad_out = grad_out.reshape(heads, 1, HEAD_DIM, width) * mine
        grad_out = lax.psum_scatter(
            grad_out.reshape(width, width), ALL, scatter_dimension=0, tiled=True
        )
    grad_proj = rotary_in(grad_qkv, cosine, sine, pairs)
    cut = 3 * third // 2
    first = dot_tn(normed_all, grad_proj[:, :cut], BF)
    second = dot_tn(normed_all, grad_proj[:, cut:], BF)
    grad_proj, first, second = lax.optimization_barrier((grad_proj, first, second))
    first, second = send_att(first), send_att(second)
    grad_normed = dot_nt(grad_proj[:, :third], q_full) + dot_nt(grad_proj[:, third:], kv_full)
    grad_normed = reduce_peers(grad_normed.astype(BF), att)
    grad_gate_w = ff_columns(gate_one, gate_two)
    grad_normed, first, grad_gate_w, grad_out = lax.optimization_barrier(
        (grad_normed, first, grad_gate_w, grad_out)
    )
    first = reduce_z(*first)
    back, grad_gain_one, grad_shift_one = norm_back(grad_normed, unit_one, scale_one, gain_one)
    grad_tokens = (grad_hidden + back).astype(BF).reshape(tokens_in.shape)
    second, grad_tokens = lax.optimization_barrier((second, grad_tokens))
    second = reduce_z(*second)
    grad_up_w = ff_columns(up_one, up_two)
    grad_out = grad_out.astype(F32)
    grad_qkv_w = jnp.concatenate([first, second], axis=1)
    grad_qkv_w = swap_peers(grad_qkv_w.reshape(peers, rows, -1), BATCH)
    grad_qkv_w = grad_qkv_w.reshape(peers, rows, 3, heads, HEAD_DIM).transpose(1, 2, 3, 0, 4)
    grad_qkv_w = grad_qkv_w.reshape(rows, 3 * width).astype(F32)
    grad_bias = jnp.sum(grad_proj.astype(F32), axis=0).reshape(3, heads, 1, HEAD_DIM)
    mine = (jnp.arange(peers) == me_peer).astype(F32)[None, None, :, None]
    grad_bias = (grad_bias * mine).reshape(devices, -1)

    vectors = [grad_gain_one, grad_shift_one, grad_gain_two, grad_shift_two]
    vectors = [v.reshape(devices, each) for v in vectors] + [grad_bias]
    vectors = jnp.concatenate(vectors, axis=1)
    vectors = lax.all_to_all(vectors, ALL, split_axis=0, concat_axis=0, tiled=True)
    vectors = jnp.sum(vectors, axis=0)
    g1, s1, g2, s2 = [vectors[i * each : (i + 1) * each] for i in range(4)]
    return (
        block_out,
        grad_tokens,
        g1,
        s1,
        grad_qkv_w,
        vectors[4 * each :],
        grad_out,
        g2,
        s2,
        grad_gate_w,
        grad_up_w,
        grad_down,
    )


def solution(mesh):
    seq, batch = mesh.shape["seq"], mesh.shape["batch"]
    sizes = (4, seq // 4, batch // 2, 2)
    fine = Mesh(mesh.devices.reshape(sizes), ALL)
    token = P(BATCH, SEQ, None)
    vector = P(ALL)
    matrix = P(ALL, None)
    return jax.shard_map(
        functools.partial(local, sizes),
        mesh=fine,
        in_specs=(
            token,
            token,
            P(BATCH, None),
            vector,
            vector,
            matrix,
            vector,
            matrix,
            vector,
            vector,
            matrix,
            matrix,
            matrix,
        ),
        out_specs=(
            token,
            token,
            vector,
            vector,
            matrix,
            vector,
            matrix,
            vector,
            vector,
            matrix,
            matrix,
            matrix,
        ),
        check_vma=False,
    )
```

```python
import functools

import jax
import jax.numpy as jnp
from jax import lax
from jax.experimental import pallas as pl
from jax.experimental.pallas import tpu as pltpu
from jax.sharding import Mesh
from jax.sharding import PartitionSpec as P

HEAD_DIM = 64
ROT = 16
DOCS = 6
LANES = 128
EPS = 1e-05
BF = jnp.bfloat16
F32 = jnp.float32
NEG = -1e30
ALL = ("z", "y", "x", "c")
SEQ = ("z", "y")
BATCH = ("x", "c")
SWAP = ((0, 1), (1, 0))


def dot(a, b, out=F32):
    return jnp.dot(a, b, preferred_element_type=out)


def dot_nt(a, b, out=F32):
    return lax.dot_general(a, b, (((1,), (1,)), ((), ())), preferred_element_type=out)


def dot_tn(a, b, out=F32):
    return lax.dot_general(a, b, (((0,), (0,)), ((), ())), preferred_element_type=out)


def after(x, *first):
    return lax.optimization_barrier((x,) + first)[0]


def gather_peers(x, axis):
    if axis is None:
        return lax.all_gather(x, BATCH, axis=0, tiled=True)
    other = lax.ppermute(x, axis, SWAP)
    far = lax.ppermute(x, "c", SWAP)
    last = lax.ppermute(other, "c", SWAP)
    return jnp.concatenate([x, other, far, last], axis=0)


def reduce_peers(part, axis):
    if axis is None:
        return lax.psum_scatter(part, BATCH, scatter_dimension=0, tiled=True).astype(F32)
    rows = part.shape[0] // 4
    got = lax.ppermute(part[2 * rows :], "c", SWAP)
    send = (part[rows : 2 * rows].astype(F32) + got[rows:].astype(F32)).astype(BF)
    last = lax.ppermute(send, axis, SWAP)
    return part[:rows].astype(F32) + got[:rows].astype(F32) + last.astype(F32)


def gather_z(w):
    return lax.all_gather(w, "z", axis=0, tiled=True)


def gather_far(near, axis):
    if axis is None:
        return lax.all_gather(near, "y", axis=0)
    return lax.ppermute(near, axis, SWAP)


def merge_rows(near, far, axis, nz, inner=1):
    wide = near.shape[-1]
    if axis is None:
        far = far.reshape(far.shape[0], nz, -1, wide).transpose(1, 0, 2, 3)
        return far.reshape(-1, wide)
    near = near.reshape(nz * inner, 1, -1, wide)
    far = far.reshape(near.shape)
    first = lax.axis_index(axis) == 0
    full = jnp.concatenate([jnp.where(first, near, far), jnp.where(first, far, near)], axis=1)
    return full.reshape(-1, wide)


def send_rows(g, axis, nz, na, inner=1):
    rows = g.shape[0] // (nz * na)
    if axis is None:
        g = g.reshape(nz, na, rows, -1).transpose(1, 0, 2, 3).reshape(na, nz * rows, -1)
        return None, lax.psum_scatter(g, "y", scatter_dimension=0, tiled=True)[0]
    g = g.reshape(nz * inner, na, rows // inner, g.shape[1])
    here = lax.axis_index(axis)
    send = lax.dynamic_index_in_dim(g, 1 - here, 1, keepdims=False)
    keep = lax.dynamic_index_in_dim(g, here, 1, keepdims=False)
    return keep, lax.ppermute(send, axis, SWAP)


def add_rows(keep, got):
    if keep is None:
        return got
    got = (keep.astype(F32) + got.astype(F32)).astype(BF)
    return got.reshape(-1, got.shape[-1])


def scatter_z(g):
    return lax.psum_scatter(g, "z", scatter_dimension=0, tiled=True)


def reduce_z(keep, got):
    return scatter_z(add_rows(keep, got))


def swap_peers(x, axes):
    return lax.all_to_all(x, axes, split_axis=0, concat_axis=0, tiled=True)


def swap_seq(x):
    return lax.all_to_all(x, SEQ, split_axis=0, concat_axis=0, tiled=True)


def norm_stats(value):
    centred = value - jnp.mean(value, axis=-1, keepdims=True)
    scale = lax.rsqrt(jnp.mean(centred * centred, axis=-1, keepdims=True) + EPS)
    return centred * scale, scale


def norm_back(grad, unit, scale, gain):
    e = grad * gain
    back = scale * (
        e - jnp.mean(e, axis=-1, keepdims=True) - unit * jnp.mean(e * unit, axis=-1, keepdims=True)
    )
    return back, jnp.sum(grad * unit, axis=0), jnp.sum(grad, axis=0)


def turn(value, cosine, sine, lane):
    inner = lane % HEAD_DIM
    ahead = pltpu.roll(value, LANES - ROT // 2, 1)
    behind = pltpu.roll(value, ROT // 2, 1)
    return value * cosine + jnp.where(inner < ROT // 2, ahead, behind) * sine


def rotary_out_body(turned, proj_ref, bias_ref, cos_ref, sin_ref, out_ref):
    pairs = out_ref.shape[0]
    cosine, sine = cos_ref[...], sin_ref[...]
    lane = lax.broadcasted_iota(jnp.int32, cosine.shape, 1)
    rotate = pl.program_id(1) < turned
    for i in range(pairs):
        at = slice(i * LANES, (i + 1) * LANES)
        value = proj_ref[:, at] + bias_ref[:, at]
        value = jnp.where(rotate, turn(value, cosine, sine, lane), value)
        out_ref[i] = value.astype(BF).reshape(out_ref.shape[1:])


def rotary_out(proj, bias, cosine, sine, pairs, rpg, t, turned):
    peers = proj.shape[0] // t
    groups = peers // rpg
    wide = pairs * LANES
    parts = proj.shape[1] // wide
    out = pl.pallas_call(
        functools.partial(rotary_out_body, turned),
        grid=(peers, parts),
        in_specs=[
            pl.BlockSpec((t, wide), lambda b, p: (b, p)),
            pl.BlockSpec((1, wide), lambda b, p: (0, p)),
            pl.BlockSpec((t, LANES), lambda b, p: (b, 0)),
            pl.BlockSpec((t, LANES), lambda b, p: (b, 0)),
        ],
        out_specs=pl.BlockSpec(
            (pairs, 1, 1, 1, t, LANES), lambda b, p: (0, b // rpg, p, b % rpg, 0, 0)
        ),
        out_shape=jax.ShapeDtypeStruct((pairs, groups, parts, rpg, t, LANES), BF),
        cost_estimate=pl.CostEstimate(
            flops=1, bytes_accessed=1, transcendentals=0
        ),
        name="rotary_out",
    )(proj, bias, cosine, sine)
    return out.reshape((pairs * groups,) + out.shape[2:])


def rotary_in_body(grad_ref, cos_ref, sin_ref, out_ref):
    pairs = grad_ref.shape[0]
    cosine, sine = cos_ref[...], -sin_ref[...]
    lane = lax.broadcasted_iota(jnp.int32, cosine.shape, 1)
    rotate = pl.program_id(1) < 2
    for i in range(pairs):
        value = grad_ref[i].reshape(cosine.shape).astype(F32)
        value = jnp.where(rotate, turn(value, cosine, sine, lane), value)
        out_ref[:, i * LANES : (i + 1) * LANES] = value.astype(BF)


def rotary_in(grad, cosine, sine, pairs):
    dests, parts, rpg, t, _ = grad.shape
    groups = dests // pairs
    wide = pairs * LANES
    return pl.pallas_call(
        rotary_in_body,
        grid=(groups * rpg, parts),
        in_specs=[
            pl.BlockSpec(
                (pairs, 1, 1, 1, t, LANES), lambda b, p: (0, b // rpg, p, b % rpg, 0, 0)
            ),
            pl.BlockSpec((t, LANES), lambda b, p: (b, 0)),
            pl.BlockSpec((t, LANES), lambda b, p: (b, 0)),
        ],
        out_specs=pl.BlockSpec((t, wide), lambda b, p: (b, p)),
        out_shape=jax.ShapeDtypeStruct((groups * rpg * t, parts * wide), BF),
        cost_estimate=pl.CostEstimate(
            flops=1, bytes_accessed=1, transcendentals=0
        ),
        name="rotary_in",
    )(grad.reshape((pairs, groups) + grad.shape[1:]), cosine, sine)


def by_head(x):
    lane = lax.broadcasted_iota(jnp.int32, x.shape, 1)
    zero = jnp.zeros_like(x)
    return jnp.concatenate(
        [jnp.where(lane < HEAD_DIM, x, zero), jnp.where(lane >= HEAD_DIM, x, zero)], axis=0
    )


def one_head(x):
    t = x.shape[0] // 2
    lane = lax.broadcasted_iota(jnp.int32, (t, LANES), 1)
    return jnp.where(lane < HEAD_DIM, x[:t], x[t:])


def window_weights(q2, keys, start, row0, col0):
    scores = dot_nt(q2, keys) * (HEAD_DIM**-0.5)
    t = q2.shape[0] // 2
    shape = (t, keys.shape[0])
    rows = row0 + lax.broadcasted_iota(jnp.int32, shape, 0)
    cols = col0 + lax.broadcasted_iota(jnp.int32, shape, 1)
    allowed = (cols <= rows) & (cols >= start)
    allowed = jnp.concatenate([allowed, allowed], axis=0)
    scores = jnp.where(allowed, scores, NEG)
    weights = jnp.exp(scores - jnp.max(scores, axis=-1, keepdims=True))
    return weights / jnp.sum(weights, axis=-1, keepdims=True)


def forward_body(window, q_ref, k_ref, v_ref, start_ref, out_ref):
    number = pl.program_id(1)
    t = q_ref.shape[3]
    first = jnp.maximum(number - (window - 1), 0)
    keys = k_ref[pl.ds(first, window), 0, 0].reshape(window * t, LANES)
    values = v_ref[pl.ds(first, window), 0, 0].reshape(window * t, LANES)
    q2 = by_head(q_ref[0, 0, 0])
    weights = window_weights(q2, keys, start_ref[0, 0], number * t, first * t)
    out_ref[0, 0] = one_head(dot(weights.astype(BF), values)).astype(BF)


def attention_specs(blocks, t):
    return [
        pl.BlockSpec((1, 1, 1, t, LANES), lambda r, i: (i, 0, r, 0, 0)),
        pl.BlockSpec((blocks, 1, 1, t, LANES), lambda r, i: (0, 0, r, 0, 0)),
        pl.BlockSpec((blocks, 1, 1, t, LANES), lambda r, i: (0, 1, r, 0, 0)),
        pl.BlockSpec((1, 1, t, 1), lambda r, i: (r, i, 0, 0)),
    ]


def attend(q, kv, start, window):
    blocks, _, rpg, t, _ = q.shape
    work = rpg * blocks * 2 * t * window * t
    return pl.pallas_call(
        functools.partial(forward_body, window),
        grid=(rpg, blocks),
        in_specs=attention_specs(blocks, t),
        out_specs=pl.BlockSpec((1, 1, t, LANES), lambda r, i: (i, r, 0, 0)),
        out_shape=jax.ShapeDtypeStruct((blocks, rpg, t, LANES), BF),
        cost_estimate=pl.CostEstimate(
            flops=1, bytes_accessed=1, transcendentals=0
        ),
        name="attend",
    )(q, kv, kv, start)


def backward_body(window, q_ref, k_ref, v_ref, start_ref, do_ref, out_ref, dk_ref, dv_ref):
    number = pl.program_id(1)
    t = q_ref.shape[3]
    scale = HEAD_DIM**-0.5

    @pl.when(number == 0)
    def _():
        dk_ref[...] = jnp.zeros_like(dk_ref)
        dv_ref[...] = jnp.zeros_like(dv_ref)

    first = jnp.maximum(number - (window - 1), 0)
    keys = k_ref[pl.ds(first, window), 0, 0].reshape(window * t, LANES)
    values = v_ref[pl.ds(first, window), 0, 0].reshape(window * t, LANES)
    q2 = by_head(q_ref[0, 0, 0])
    do2 = by_head(do_ref[0, 0])
    weights = window_weights(q2, keys, start_ref[0, 0], number * t, first * t)
    grad = dot_nt(do2, values)
    inner = jnp.sum(weights * grad, axis=-1, keepdims=True)
    ds = (weights * (grad - inner)).astype(BF)
    out_ref[number, 0, 0] = one_head(dot(ds, keys) * scale).astype(BF)
    shape = (window, t, LANES)
    dk_ref[pl.ds(first, window)] += dot_tn(ds, q2).reshape(shape)
    dv_ref[pl.ds(first, window)] += dot_tn(weights.astype(BF), do2).reshape(shape)

    @pl.when(number == pl.num_programs(1) - 1)
    def _():
        out_ref[:, 1, 0] = (dk_ref[...] * scale).astype(BF)
        out_ref[:, 2, 0] = dv_ref[...].astype(BF)


def attend_back(q, kv, start, grad, window):
    blocks, _, rpg, t, _ = q.shape
    work = rpg * blocks * 2 * t * window * t
    return pl.pallas_call(
        functools.partial(backward_body, window),
        grid=(rpg, blocks),
        in_specs=attention_specs(blocks, t)
        + [pl.BlockSpec((1, 1, t, LANES), lambda r, i: (i, r, 0, 0))],
        out_specs=pl.BlockSpec((blocks, 3, 1, t, LANES), lambda r, i: (0, 0, r, 0, 0)),
        out_shape=jax.ShapeDtypeStruct((blocks, 3, rpg, t, LANES), BF),
        scratch_shapes=[
            pltpu.VMEM((blocks, t, LANES), F32),
            pltpu.VMEM((blocks, t, LANES), F32),
        ],
        cost_estimate=pl.CostEstimate(
            flops=1, bytes_accessed=1, transcendentals=0
        ),
        name="attend_back",
    )(q, kv, kv, start, grad)


FREE = pl.CostEstimate(flops=1, bytes_accessed=1, transcendentals=0)


def split_body(here_ref, x_ref, out_ref):
    count = x_ref.shape[1] // LANES
    first = here_ref[0] == 0
    for i in range(count):
        place = (i % 2) * (count // 2) + i // 2
        other = (1 - i % 2) * (count // 2) + i // 2
        value = x_ref[:, i * LANES : (i + 1) * LANES]

        @pl.when(first)
        def _():
            out_ref[:, place * LANES : (place + 1) * LANES] = value

        @pl.when(jnp.logical_not(first))
        def _():
            out_ref[:, other * LANES : (other + 1) * LANES] = value


def join_body(here_ref, x_ref, out_ref):
    count = x_ref.shape[1] // LANES
    first = here_ref[0] == 0
    for i in range(count):
        place = (i % 2) * (count // 2) + i // 2
        other = (1 - i % 2) * (count // 2) + i // 2
        one = x_ref[:, place * LANES : (place + 1) * LANES]
        two = x_ref[:, other * LANES : (other + 1) * LANES]
        out_ref[:, i * LANES : (i + 1) * LANES] = jnp.where(first, one, two)


def regroup(body, here, x, name):
    return pl.pallas_call(
        body,
        in_specs=[
            pl.BlockSpec(memory_space=pltpu.SMEM),
            pl.BlockSpec(memory_space=pltpu.VMEM),
        ],
        out_specs=pl.BlockSpec(memory_space=pltpu.VMEM),
        out_shape=jax.ShapeDtypeStruct(x.shape, x.dtype),
        cost_estimate=FREE,
        name=name,
    )(here.reshape(1), x)


def hidden_body(x_ref, gn_ref, gf_ref, un_ref, uf_ref, gate_ref, up_ref, act_ref):
    k = gn_ref.shape[0]
    tile = gn_ref.shape[1]
    near = jnp.concatenate([gn_ref[...], un_ref[...]], axis=1)
    far = jnp.concatenate([gf_ref[...], uf_ref[...]], axis=1)
    both = dot(x_ref[:, :k], near) + dot(x_ref[:, k:], far)
    gate, up = both[:, :tile], both[:, tile:]
    gate_ref[...] = gate
    up_ref[...] = up
    act_ref[...] = (gate * jax.nn.sigmoid(gate) * up).astype(BF)


def hidden_units(x, gate, up):
    m, width = x.shape
    k, n = gate[0].shape
    weight = pl.BlockSpec((k, LANES), lambda j: (0, j))
    tile = pl.BlockSpec((m, LANES), lambda j: (0, j))
    return pl.pallas_call(
        hidden_body,
        grid=(pl.cdiv(n, LANES),),
        in_specs=[pl.BlockSpec((m, width), lambda j: (0, 0))] + [weight] * 4,
        out_specs=[tile] * 3,
        out_shape=[jax.ShapeDtypeStruct((m, n), d) for d in (F32, F32, BF)],
        cost_estimate=FREE,
        name="hidden_units",
    )(x, *gate, *up)


def hidden_back_body(grad_ref, down_ref, gate_ref, up_ref, gg_ref, gu_ref):
    grad = dot_nt(grad_ref[...], down_ref[...])
    gate = gate_ref[...]
    sigmoid = jax.nn.sigmoid(gate)
    gg_ref[...] = (grad * up_ref[...] * sigmoid * (1.0 + gate * (1.0 - sigmoid))).astype(BF)
    gu_ref[...] = (grad * gate * sigmoid).astype(BF)


def hidden_back(grad, down, gate, up, t):
    m, width = grad.shape
    n = down.shape[0]
    tile = pl.BlockSpec((t, n), lambda i: (i, 0))
    return pl.pallas_call(
        hidden_back_body,
        grid=(m // t,),
        in_specs=[
            pl.BlockSpec((t, width), lambda i: (i, 0)),
            pl.BlockSpec((n, width), lambda i: (0, 0)),
            tile,
            tile,
        ],
        out_specs=[tile] * 2,
        out_shape=[jax.ShapeDtypeStruct((m, n), BF)] * 2,
        cost_estimate=FREE,
        name="hidden_back",
    )(grad, down, gate, up)


def input_back_body(steps, gg_ref, gu_ref, gn_ref, gf_ref, un_ref, uf_ref, out_ref):
    @pl.when(pl.program_id(0) < steps)
    def _():
        part = dot_nt(gg_ref[...], gn_ref[...]) + dot_nt(gu_ref[...], un_ref[...])
        out_ref[...] = part.astype(BF)

    @pl.when(pl.program_id(0) >= steps)
    def _():
        part = dot_nt(gg_ref[...], gf_ref[...]) + dot_nt(gu_ref[...], uf_ref[...])
        out_ref[...] = part.astype(BF)


def input_back(grad_gate, grad_up, gate, up):
    m, n = grad_gate.shape
    k = gate[0].shape[0]
    tile = 2 * LANES
    steps = k // tile
    whole = pl.BlockSpec((m, n), lambda i: (0, 0))
    near = pl.BlockSpec((tile, n), lambda i: (jnp.minimum(i, steps - 1), 0))
    far = pl.BlockSpec((tile, n), lambda i: (jnp.maximum(i - steps, 0), 0))
    return pl.pallas_call(
        functools.partial(input_back_body, steps),
        grid=(2 * steps,),
        in_specs=[whole, whole, near, far, near, far],
        out_specs=pl.BlockSpec((m, tile), lambda i: (0, i)),
        out_shape=jax.ShapeDtypeStruct((m, 2 * k), BF),
        cost_estimate=FREE,
        name="input_back",
    )(grad_gate, grad_up, *gate, *up)


def local(
    sizes,
    tokens_in,
    cotangent,
    segment_ids,
    attn_gain,
    attn_shift,
    qkv_weight,
    qkv_bias,
    out_weight,
    mlp_gain,
    mlp_shift,
    gate_weight,
    up_weight,
    down_weight,
):
    nz, ny, nx, nc = sizes
    seq, peers = nz * ny, nx * nc
    devices = seq * peers
    pair = nx == 2 and ny == 2
    att, att_rows = ("x", "y") if pair else (None, None)
    fwd, fwd_rows = ("y", "x") if pair else (None, None)
    fwd_axes = ("y", "c") if pair else BATCH
    t, width = tokens_in.shape[1:]
    length = segment_ids.shape[1]
    heads = width // HEAD_DIM // peers
    pairs = heads // 2
    groups = seq // pairs
    rpg = peers // groups
    ff = down_weight.shape[0] * devices
    strip = ff // devices
    own_head = width // devices == HEAD_DIM
    window = min((length // 3 - 1 + t - 1) // t + 1, length // t)
    me_seq = lax.axis_index(SEQ)
    me_peer = lax.axis_index(BATCH)

    small = jnp.concatenate([attn_gain, attn_shift, mlp_gain, mlp_shift, qkv_bias])
    small = jnp.broadcast_to(small[None], (devices, small.size))
    small = lax.all_to_all(small, ALL, split_axis=0, concat_axis=0, tiled=True).astype(F32)
    each = attn_gain.size
    gain_one, shift_one, gain_two, shift_two = [
        small[:, i * each : (i + 1) * each].reshape(1, width) for i in range(4)
    ]
    bias = small[:, 4 * each :].reshape(3, heads, peers, HEAD_DIM)
    bias = lax.dynamic_index_in_dim(bias, me_peer, 2, keepdims=False).reshape(1, -1)

    rows = qkv_weight.shape[0]
    third = width // peers
    qkv_mine = qkv_weight.reshape(rows, 3, heads, peers, HEAD_DIM).transpose(3, 0, 1, 2, 4)
    qkv_mine = swap_peers(qkv_mine.reshape(peers, rows, -1), BATCH).reshape(peers * rows, -1)

    def columns(w):
        if pair:
            w = w.reshape(rows, nz, 2, 2, nc, strip).transpose(2, 4, 0, 1, 3, 5)
        else:
            w = w.reshape(rows, seq, peers, strip).transpose(2, 0, 1, 3)
        return w.reshape(peers, rows, -1)

    merge_att = functools.partial(merge_rows, axis=att_rows, nz=nz)
    merge_ff = functools.partial(merge_rows, axis=fwd_rows, nz=nz)
    split = 2 if pair else 1
    mine = jnp.concatenate([columns(gate_weight), columns(up_weight)], axis=1)
    mine = swap_peers(after(mine, small), fwd_axes)
    gate_mine = mine[:, :rows].reshape(peers * rows, -1)
    up_mine = mine[:, rows:].reshape(peers * rows, -1)
    kv_near, q_near = gather_z(qkv_mine[:, third:]), gather_z(qkv_mine[:, :third])
    kv_near, gate_mine, up_mine = lax.optimization_barrier((kv_near, gate_mine, up_mine))
    kv_far = gather_far(kv_near, att_rows)
    gate_near = gather_z(gate_mine)
    gate_far = gather_far(gate_near, fwd_rows)
    if own_head:
        out_near = gather_z(after(out_weight, gate_near))
    else:
        out_full = lax.all_gather(out_weight, ALL, axis=0, tiled=True)
        out_full = out_full.reshape(heads, peers, HEAD_DIM, width)
        out_full = lax.dynamic_index_in_dim(out_full, me_peer, 1, keepdims=False)
        out_full = out_full.reshape(heads * HEAD_DIM, width)

    kv_far, q_near, segment = lax.optimization_barrier(
        (kv_far, q_near, gather_peers(segment_ids, att))
    )
    q_far = gather_far(q_near, att_rows)
    q_full, kv_full = merge_att(q_near, q_far), merge_att(kv_near, kv_far)
    start = jnp.zeros_like(segment)
    for doc in range(DOCS):
        count = jnp.sum((segment == doc).astype(jnp.int32), axis=1, keepdims=True)
        start = start + jnp.where(segment > doc, count, 0)
    places = me_seq * t + jnp.arange(t, dtype=jnp.int32)
    here = places[None] - lax.dynamic_slice_in_dim(start, me_seq * t, t, 1)
    half = ROT // 2
    inverse = 10000.0 ** (-jnp.arange(half, dtype=F32) / half)
    theta = inverse[:, None] * here.reshape(1, -1).astype(F32)
    cosine, sine = jnp.cos(theta), jnp.sin(theta)
    rest = jnp.ones((HEAD_DIM - ROT, theta.shape[1]), F32)
    cosine = jnp.concatenate([cosine, cosine, rest] * 2, axis=0).T
    sine = jnp.concatenate([-sine, sine, 0.0 * rest] * 2, axis=0).T
    start = lax.dynamic_slice_in_dim(start, (me_seq % groups) * rpg, rpg, 0)
    start = start.reshape(rpg, length // t, t, 1)

    inputs = tokens_in[0].astype(F32)
    unit_one, scale_one = norm_stats(inputs)
    normed = (unit_one * gain_one + shift_one).astype(BF)
    normed_all = gather_peers(normed, att)
    key_value = rotary_out(
        dot(normed_all, kv_full), bias[:, third:], cosine, sine, pairs, rpg, t, 1
    )
    key_value = swap_seq(key_value)
    query = rotary_out(dot(normed_all, q_full), bias[:, :third], cosine, sine, pairs, rpg, t, 1)
    query = swap_seq(after(query, key_value))
    qkv_full = jnp.concatenate([q_full, kv_full], axis=1)
    up_near = gather_z(up_mine)
    down_near = gather_z(down_weight)
    grad_output = cotangent[0]
    grad_all = gather_peers(grad_output, fwd)
    mixed = attend(query, key_value, start, window)
    mixed, gate_far, up_near = lax.optimization_barrier((mixed, gate_far, up_near))
    up_far = gather_far(up_near, fwd_rows)
    mixed = swap_seq(mixed)
    if own_head:
        out_full = merge_att(out_near, gather_far(out_near, att_rows))
    mixed, up_far, grad_all, qkv_full, out_full = lax.optimization_barrier(
        (mixed, up_far, grad_all, qkv_full, out_full)
    )

    def token_rows(x):
        x = x.reshape(pairs, groups * rpg * t, LANES).transpose(1, 0, 2)
        return x.reshape(groups * rpg * t, pairs * LANES)

    def head_rows(x):
        x = x.reshape(groups * rpg * t, pairs, LANES).transpose(1, 0, 2)
        return x.reshape(seq, rpg, t, LANES)

    mixed = token_rows(mixed)
    hidden = inputs + reduce_peers(dot(mixed, out_full, BF), att)
    hidden, down_near = lax.optimization_barrier((hidden, down_near))

    unit_two, scale_two = norm_stats(hidden)
    normed_two = (unit_two * gain_two + shift_two).astype(BF)
    down_far = gather_far(down_near, fwd_rows)
    if pair:
        here_x = lax.axis_index("x")
        normed_two = regroup(split_body, here_x, normed_two, "own_first")
        gate_full, up_full = (gate_near, gate_far), (up_near, up_far)
    else:
        gate_full = jnp.split(merge_ff(gate_near, gate_far), 2)
        up_full = jnp.split(merge_ff(up_near, up_far), 2)
    normed_two_all = gather_peers(normed_two, fwd)
    gate, up, act = hidden_units(normed_two_all, gate_full, up_full)
    down_full = merge_ff(down_near, after(down_far, gate))
    down_part = dot(act, down_full, BF)

    send_att = functools.partial(send_rows, axis=att_rows, nz=nz, na=ny)
    send_ff = functools.partial(send_rows, axis=fwd_rows, nz=nz, na=nx if pair else ny)
    wide = width // 2
    down_one = send_ff(dot_tn(act, grad_all[:, :wide], BF))
    down_two = dot_tn(act, grad_all[:, wide:], BF)
    grad_gate, grad_up = hidden_back(grad_all, down_full, gate, up, t)
    part = input_back(grad_gate, grad_up, gate_full, up_full)
    branch_two = reduce_peers(down_part, fwd)
    down_one = add_rows(*down_one)
    part, branch_two, down_one, down_two = lax.optimization_barrier(
        (part, branch_two, down_one, down_two)
    )
    down_two = send_ff(down_two)
    block_out = (hidden + branch_two).astype(BF).reshape(tokens_in.shape)
    grad_normed_two = reduce_peers(part, fwd)

    def dots(g):
        if not pair:
            return (dot_tn(normed_two_all, g, BF),)
        return dot_tn(normed_two_all[:, wide:], g, BF), dot_tn(normed_two_all[:, :wide], g, BF)

    def send_columns(g):
        if not pair:
            return send_ff(g[0])
        return g[1], lax.ppermute(g[0], "x", SWAP)

    cut_ff = grad_gate.shape[1] // 256 * 128 + LANES
    gate_one, gate_two = dots(grad_gate[:, :cut_ff]), dots(grad_gate[:, cut_ff:])
    grad_normed_two, gate_one, gate_two = lax.optimization_barrier(
        (grad_normed_two, gate_one, gate_two)
    )
    gate_one, gate_two, up_w = [send_columns(g) for g in (gate_one, gate_two, dots(grad_up))]
    down_one, down_two = scatter_z(down_one), add_rows(*down_two)
    grad_normed_two, down_one, down_two = lax.optimization_barrier(
        (grad_normed_two, down_one, down_two)
    )
    down_two = scatter_z(down_two)
    if pair:
        grad_normed_two = regroup(join_body, here_x, grad_normed_two, "own_back")
    back, grad_gain_two, grad_shift_two = norm_back(grad_normed_two, unit_two, scale_two, gain_two)
    grad_hidden = grad_output.astype(F32) + back

    def ff_columns(*parts):
        g = jnp.concatenate(parts, axis=1)
        g = swap_peers(g.reshape(peers, rows, -1), fwd_axes)
        if pair:
            g = g.reshape(2, nc, rows, nz, 2, strip).transpose(2, 3, 0, 4, 1, 5)
        else:
            g = g.reshape(peers, rows, seq, strip).transpose(1, 2, 0, 3)
        return g.reshape(rows, ff).astype(F32)

    branch = gather_peers(grad_hidden.astype(BF), att)
    grad_mixed = head_rows(dot_nt(branch, out_full, BF))
    grad_mixed, down_two = lax.optimization_barrier((grad_mixed, down_two))
    grad_mixed = swap_seq(grad_mixed)
    grad_out = dot_tn(mixed, branch, BF)
    gate_one = add_rows(*gate_one)
    grad_mixed, gate_one, grad_out = lax.optimization_barrier((grad_mixed, gate_one, grad_out))
    gate_one = scatter_z(gate_one)
    grad_qkv = attend_back(query, key_value, start, grad_mixed, window)
    if own_head:
        grad_out = send_att(grad_out)
    grad_qkv, gate_one, gate_two = lax.optimization_barrier((grad_qkv, gate_one, gate_two))
    gate_two = scatter_z(add_rows(*gate_two))
    grad_qkv = swap_seq(grad_qkv)
    grad_down = jnp.concatenate([down_one, down_two], axis=1).astype(F32)
    up_w = add_rows(*up_w)
    if own_head:
        grad_out = add_rows(*grad_out)
    grad_qkv, up_w, grad_out, grad_down, gate_two = lax.optimization_barrier(
        (grad_qkv, up_w, grad_out, grad_down, gate_two)
    )
    if own_head:
        grad_out = scatter_z(grad_out)
    up_w = scatter_z(up_w)
    if not own_head:
        mine = (jnp.arange(peers) == me_peer).astype(BF)[None, :, None, None]
        grad_out = grad_out.reshape(heads, 1, HEAD_DIM, width) * mine
        grad_out = lax.psum_scatter(
            grad_out.reshape(width, width), ALL, scatter_dimension=0, tiled=True
        )
    grad_proj = rotary_in(grad_qkv, cosine, sine, pairs)
    cut = 3 * third // 2
    first = dot_tn(normed_all, grad_proj[:, :cut], BF)
    second = dot_tn(normed_all, grad_proj[:, cut:], BF)
    grad_proj, first, second, grad_out = lax.optimization_barrier(
        (grad_proj, first, second, grad_out)
    )
    first, second = send_att(first), send_att(second)
    grad_normed = reduce_peers(dot_nt(grad_proj, qkv_full, BF), att)
    first = add_rows(*first)
    first, up_w = lax.optimization_barrier((first, up_w))
    if pair:
        second = (second[0], after(second[1], first))
    first = scatter_z(first)
    back, grad_gain_one, grad_shift_one = norm_back(grad_normed, unit_one, scale_one, gain_one)
    grad_tokens = (grad_hidden + back).astype(BF).reshape(tokens_in.shape)
    second = add_rows(*second)
    second, first, grad_tokens, gate_one, gate_two, up_w = lax.optimization_barrier(
        (second, first, grad_tokens, gate_one, gate_two, up_w)
    )
    second = scatter_z(second)
    grad_gate_w = ff_columns(gate_one, gate_two)
    grad_up_w = ff_columns(up_w)
    second, grad_gate_w, grad_up_w = lax.optimization_barrier((second, grad_gate_w, grad_up_w))
    grad_out = grad_out.astype(F32)
    grad_qkv_w = jnp.concatenate([first, second], axis=1)
    grad_qkv_w = swap_peers(grad_qkv_w.reshape(peers, rows, -1), BATCH)
    grad_qkv_w = grad_qkv_w.reshape(peers, rows, 3, heads, HEAD_DIM).transpose(1, 2, 3, 0, 4)
    grad_qkv_w = grad_qkv_w.reshape(rows, 3 * width).astype(F32)
    grad_bias = jnp.sum(grad_proj.astype(F32), axis=0).reshape(3, heads, 1, HEAD_DIM)
    mine = (jnp.arange(peers) == me_peer).astype(F32)[None, None, :, None]
    grad_bias = (grad_bias * mine).reshape(devices, -1)

    vectors = [grad_gain_one, grad_shift_one, grad_gain_two, grad_shift_two]
    vectors = [v.reshape(devices, each) for v in vectors] + [grad_bias]
    vectors = jnp.concatenate(vectors, axis=1)
    vectors = lax.all_to_all(vectors, ALL, split_axis=0, concat_axis=0, tiled=True)
    vectors = jnp.sum(vectors, axis=0)
    g1, s1, g2, s2 = [vectors[i * each : (i + 1) * each] for i in range(4)]
    return (
        block_out,
        grad_tokens,
        g1,
        s1,
        grad_qkv_w,
        vectors[4 * each :],
        grad_out,
        g2,
        s2,
        grad_gate_w,
        grad_up_w,
        grad_down,
    )


def solution(mesh):
    seq, batch = mesh.shape["seq"], mesh.shape["batch"]
    sizes = (4, seq // 4, batch // 2, 2)
    fine = Mesh(mesh.devices.reshape(sizes), ALL)
    token = P(BATCH, SEQ, None)
    vector = P(ALL)
    matrix = P(ALL, None)
    return jax.shard_map(
        functools.partial(local, sizes),
        mesh=fine,
        in_specs=(
            token,
            token,
            P(BATCH, None),
            vector,
            vector,
            matrix,
            vector,
            matrix,
            vector,
            vector,
            matrix,
            matrix,
            matrix,
        ),
        out_specs=(
            token,
            token,
            vector,
            vector,
            matrix,
            vector,
            matrix,
            vector,
            vector,
            matrix,
            matrix,
            matrix,
        ),
        check_vma=False,
    )
```

```python
import functools

import jax
import jax.numpy as jnp
from jax import lax
from jax.experimental import pallas as pl
from jax.experimental.pallas import tpu as pltpu
from jax.sharding import Mesh
from jax.sharding import PartitionSpec as P

HEAD_DIM = 64
ROT = 16
DOCS = 6
LANES = 128
EPS = 1e-05
BF = jnp.bfloat16
F32 = jnp.float32
NEG = -1e30
ALL = ("z", "y", "x", "c")
SEQ = ("z", "y")
BATCH = ("x", "c")
SWAP = ((0, 1), (1, 0))


def dot(a, b, out=F32):
    return jnp.dot(a, b, preferred_element_type=out)


def dot_nt(a, b, out=F32):
    return lax.dot_general(a, b, (((1,), (1,)), ((), ())), preferred_element_type=out)


def dot_tn(a, b, out=F32):
    return lax.dot_general(a, b, (((0,), (0,)), ((), ())), preferred_element_type=out)


def after(x, *first):
    return lax.optimization_barrier((x,) + first)[0]


def gather_peers(x, axis):
    if axis is None:
        return lax.all_gather(x, BATCH, axis=0, tiled=True)
    other = lax.ppermute(x, axis, SWAP)
    far = lax.ppermute(x, "c", SWAP)
    last = lax.ppermute(other, "c", SWAP)
    return jnp.concatenate([x, other, far, last], axis=0)


def reduce_peers(halves, axis):
    near, far = halves
    if axis is None:
        part = jnp.concatenate([near, far], axis=0)
        return lax.psum_scatter(part, BATCH, scatter_dimension=0, tiled=True).astype(F32)
    rows = near.shape[0] // 2
    got = lax.ppermute(far, "c", SWAP)
    send = (near[rows:].astype(F32) + got[rows:].astype(F32)).astype(BF)
    last = lax.ppermute(send, axis, SWAP)
    return near[:rows].astype(F32) + got[:rows].astype(F32) + last.astype(F32)


def reduce_pieces(halves, axis):
    near, far = halves
    rows = near.shape[0] // 2
    got = lax.ppermute(far, "c", SWAP)
    send = (near[rows:].astype(F32) + got[rows:].astype(F32)).astype(BF)
    return near, got, lax.ppermute(send, axis, SWAP)


def halves_of(product, x, w):
    rows = x.shape[0] // 2
    return product(x[:rows], w, BF), product(x[rows:], w, BF)


def gather_z(w):
    return lax.all_gather(w, "z", axis=0, tiled=True)


def gather_far(near, axis):
    if axis is None:
        return lax.all_gather(near, "y", axis=0)
    return lax.ppermute(near, axis, SWAP)


def merge_rows(near, far, axis, nz, inner=1):
    wide = near.shape[-1]
    if axis is None:
        far = far.reshape(far.shape[0], nz, -1, wide).transpose(1, 0, 2, 3)
        return far.reshape(-1, wide)
    near = near.reshape(nz * inner, 1, -1, wide)
    far = far.reshape(near.shape)
    first = lax.axis_index(axis) == 0
    full = jnp.concatenate([jnp.where(first, near, far), jnp.where(first, far, near)], axis=1)
    return full.reshape(-1, wide)


def send_rows(g, axis, nz, na, inner=1):
    rows = g.shape[0] // (nz * na)
    if axis is None:
        g = g.reshape(nz, na, rows, -1).transpose(1, 0, 2, 3).reshape(na, nz * rows, -1)
        return None, lax.psum_scatter(g, "y", scatter_dimension=0, tiled=True)[0]
    g = g.reshape(nz * inner, na, rows // inner, g.shape[1])
    here = lax.axis_index(axis)
    send = lax.dynamic_index_in_dim(g, 1 - here, 1, keepdims=False)
    keep = lax.dynamic_index_in_dim(g, here, 1, keepdims=False)
    return keep, lax.ppermute(send, axis, SWAP)


def add_rows(keep, got):
    if keep is None:
        return got
    got = (keep.astype(F32) + got.astype(F32)).astype(BF)
    return got.reshape(-1, got.shape[-1])


def scatter_z(g):
    return lax.psum_scatter(g, "z", scatter_dimension=0, tiled=True)


def reduce_z(keep, got):
    return scatter_z(add_rows(keep, got))


def swap_peers(x, axes):
    return lax.all_to_all(x, axes, split_axis=0, concat_axis=0, tiled=True)


def swap_seq(x):
    return lax.all_to_all(x, SEQ, split_axis=0, concat_axis=0, tiled=True)


def norm_stats(value):
    centred = value - jnp.mean(value, axis=-1, keepdims=True)
    scale = lax.rsqrt(jnp.mean(centred * centred, axis=-1, keepdims=True) + EPS)
    return centred * scale, scale


def norm_back(grad, unit, scale, gain):
    e = grad * gain
    back = scale * (
        e - jnp.mean(e, axis=-1, keepdims=True) - unit * jnp.mean(e * unit, axis=-1, keepdims=True)
    )
    return back, jnp.sum(grad * unit, axis=0), jnp.sum(grad, axis=0)


def turn(value, cosine, sine, lane):
    inner = lane % HEAD_DIM
    ahead = pltpu.roll(value, LANES - ROT // 2, 1)
    behind = pltpu.roll(value, ROT // 2, 1)
    return value * cosine + jnp.where(inner < ROT // 2, ahead, behind) * sine


def rotary_out_body(turned, proj_ref, bias_ref, cos_ref, sin_ref, out_ref):
    pairs = out_ref.shape[0]
    cosine, sine = cos_ref[...], sin_ref[...]
    lane = lax.broadcasted_iota(jnp.int32, cosine.shape, 1)
    rotate = pl.program_id(1) < turned
    for i in range(pairs):
        at = slice(i * LANES, (i + 1) * LANES)
        value = proj_ref[:, at] + bias_ref[:, at]
        value = jnp.where(rotate, turn(value, cosine, sine, lane), value)
        out_ref[i] = value.astype(BF).reshape(out_ref.shape[1:])


def rotary_out(proj, bias, cosine, sine, pairs, rpg, t, turned):
    peers = proj.shape[0] // t
    groups = peers // rpg
    wide = pairs * LANES
    parts = proj.shape[1] // wide
    out = pl.pallas_call(
        functools.partial(rotary_out_body, turned),
        grid=(peers, parts),
        in_specs=[
            pl.BlockSpec((t, wide), lambda b, p: (b, p)),
            pl.BlockSpec((1, wide), lambda b, p: (0, p)),
            pl.BlockSpec((t, LANES), lambda b, p: (b, 0)),
            pl.BlockSpec((t, LANES), lambda b, p: (b, 0)),
        ],
        out_specs=pl.BlockSpec(
            (pairs, 1, 1, 1, t, LANES), lambda b, p: (0, b // rpg, p, b % rpg, 0, 0)
        ),
        out_shape=jax.ShapeDtypeStruct((pairs, groups, parts, rpg, t, LANES), BF),
        cost_estimate=pl.CostEstimate(
            flops=1, bytes_accessed=1, transcendentals=0
        ),
        name="rotary_out",
    )(proj, bias, cosine, sine)
    return out.reshape((pairs * groups,) + out.shape[2:])


def rotary_in_body(grad_ref, cos_ref, sin_ref, out_ref):
    pairs = grad_ref.shape[0]
    cosine, sine = cos_ref[...], -sin_ref[...]
    lane = lax.broadcasted_iota(jnp.int32, cosine.shape, 1)
    rotate = pl.program_id(1) < 2
    for i in range(pairs):
        value = grad_ref[i].reshape(cosine.shape).astype(F32)
        value = jnp.where(rotate, turn(value, cosine, sine, lane), value)
        out_ref[:, i * LANES : (i + 1) * LANES] = value.astype(BF)


def rotary_in(grad, cosine, sine, pairs):
    dests, parts, rpg, t, _ = grad.shape
    groups = dests // pairs
    wide = pairs * LANES
    return pl.pallas_call(
        rotary_in_body,
        grid=(groups * rpg, parts),
        in_specs=[
            pl.BlockSpec(
                (pairs, 1, 1, 1, t, LANES), lambda b, p: (0, b // rpg, p, b % rpg, 0, 0)
            ),
            pl.BlockSpec((t, LANES), lambda b, p: (b, 0)),
            pl.BlockSpec((t, LANES), lambda b, p: (b, 0)),
        ],
        out_specs=pl.BlockSpec((t, wide), lambda b, p: (b, p)),
        out_shape=jax.ShapeDtypeStruct((groups * rpg * t, parts * wide), BF),
        cost_estimate=pl.CostEstimate(
            flops=1, bytes_accessed=1, transcendentals=0
        ),
        name="rotary_in",
    )(grad.reshape((pairs, groups) + grad.shape[1:]), cosine, sine)


def by_head(x):
    lane = lax.broadcasted_iota(jnp.int32, x.shape, 1)
    zero = jnp.zeros_like(x)
    return jnp.concatenate(
        [jnp.where(lane < HEAD_DIM, x, zero), jnp.where(lane >= HEAD_DIM, x, zero)], axis=0
    )


def one_head(x):
    t = x.shape[0] // 2
    lane = lax.broadcasted_iota(jnp.int32, (t, LANES), 1)
    return jnp.where(lane < HEAD_DIM, x[:t], x[t:])


def window_weights(q2, keys, start, row0, col0):
    scores = dot_nt(q2, keys) * (HEAD_DIM**-0.5)
    t = q2.shape[0] // 2
    shape = (t, keys.shape[0])
    rows = row0 + lax.broadcasted_iota(jnp.int32, shape, 0)
    cols = col0 + lax.broadcasted_iota(jnp.int32, shape, 1)
    allowed = (cols <= rows) & (cols >= start)
    allowed = jnp.concatenate([allowed, allowed], axis=0)
    scores = jnp.where(allowed, scores, NEG)
    weights = jnp.exp(scores - jnp.max(scores, axis=-1, keepdims=True))
    return weights / jnp.sum(weights, axis=-1, keepdims=True)


def by_window(window, body):
    number = pl.program_id(1)
    for w in range(1, window + 1):
        pl.when(number == w - 1 if w < window else number >= w - 1)(functools.partial(body, w))


def forward_body(window, q_ref, k_ref, v_ref, start_ref, out_ref):
    number = pl.program_id(1)
    t = q_ref.shape[3]

    def body(w):
        first = number - (w - 1)
        keys = k_ref[pl.ds(first, w), 0, 0].reshape(w * t, LANES)
        values = v_ref[pl.ds(first, w), 0, 0].reshape(w * t, LANES)
        q2 = by_head(q_ref[0, 0, 0])
        weights = window_weights(q2, keys, start_ref[0, 0], number * t, first * t)
        out_ref[0, 0] = one_head(dot(weights.astype(BF), values)).astype(BF)

    by_window(window, body)


def attention_specs(blocks, t):
    return [
        pl.BlockSpec((1, 1, 1, t, LANES), lambda r, i: (i, 0, r, 0, 0)),
        pl.BlockSpec((blocks, 1, 1, t, LANES), lambda r, i: (0, 0, r, 0, 0)),
        pl.BlockSpec((blocks, 1, 1, t, LANES), lambda r, i: (0, 1, r, 0, 0)),
        pl.BlockSpec((1, 1, t, 1), lambda r, i: (r, i, 0, 0)),
    ]


def attend(q, kv, start, window):
    blocks, _, rpg, t, _ = q.shape
    work = rpg * blocks * 2 * t * window * t
    return pl.pallas_call(
        functools.partial(forward_body, window),
        grid=(rpg, blocks),
        in_specs=attention_specs(blocks, t),
        out_specs=pl.BlockSpec((1, 1, t, LANES), lambda r, i: (i, r, 0, 0)),
        out_shape=jax.ShapeDtypeStruct((blocks, rpg, t, LANES), BF),
        cost_estimate=pl.CostEstimate(
            flops=1, bytes_accessed=1, transcendentals=0
        ),
        name="attend",
    )(q, kv, kv, start)


def backward_body(window, q_ref, k_ref, v_ref, start_ref, do_ref, out_ref, dk_ref, dv_ref):
    number = pl.program_id(1)
    t = q_ref.shape[3]
    scale = HEAD_DIM**-0.5

    @pl.when(number == 0)
    def _():
        dk_ref[...] = jnp.zeros_like(dk_ref)
        dv_ref[...] = jnp.zeros_like(dv_ref)

    def body(w):
        first = number - (w - 1)
        keys = k_ref[pl.ds(first, w), 0, 0].reshape(w * t, LANES)
        values = v_ref[pl.ds(first, w), 0, 0].reshape(w * t, LANES)
        q2 = by_head(q_ref[0, 0, 0])
        do2 = by_head(do_ref[0, 0])
        weights = window_weights(q2, keys, start_ref[0, 0], number * t, first * t)
        grad = dot_nt(do2, values)
        inner = jnp.sum(weights * grad, axis=-1, keepdims=True)
        ds = (weights * (grad - inner)).astype(BF)
        out_ref[number, 0, 0] = one_head(dot(ds, keys) * scale).astype(BF)
        shape = (w, t, LANES)
        dk_ref[pl.ds(first, w)] += dot_tn(ds, q2).reshape(shape)
        dv_ref[pl.ds(first, w)] += dot_tn(weights.astype(BF), do2).reshape(shape)

    by_window(window, body)

    @pl.when(number == pl.num_programs(1) - 1)
    def _():
        out_ref[:, 1, 0] = (dk_ref[...] * scale).astype(BF)
        out_ref[:, 2, 0] = dv_ref[...].astype(BF)


def attend_back(q, kv, start, grad, window):
    blocks, _, rpg, t, _ = q.shape
    work = rpg * blocks * 2 * t * window * t
    return pl.pallas_call(
        functools.partial(backward_body, window),
        grid=(rpg, blocks),
        in_specs=attention_specs(blocks, t)
        + [pl.BlockSpec((1, 1, t, LANES), lambda r, i: (i, r, 0, 0))],
        out_specs=pl.BlockSpec((blocks, 3, 1, t, LANES), lambda r, i: (0, 0, r, 0, 0)),
        out_shape=jax.ShapeDtypeStruct((blocks, 3, rpg, t, LANES), BF),
        scratch_shapes=[
            pltpu.VMEM((blocks, t, LANES), F32),
            pltpu.VMEM((blocks, t, LANES), F32),
        ],
        cost_estimate=pl.CostEstimate(
            flops=1, bytes_accessed=1, transcendentals=0
        ),
        name="attend_back",
    )(q, kv, kv, start, grad)


FREE = pl.CostEstimate(flops=1, bytes_accessed=1, transcendentals=0)


ROWS = 64


def places(count):
    half = count // 2
    return [((i % 2) * half + i // 2, (1 - i % 2) * half + i // 2) for i in range(count)]


def lanes_at(i):
    return slice(i * LANES, (i + 1) * LANES)


def unit_of(value):
    centred = value - jnp.mean(value, axis=-1, keepdims=True)
    scale = lax.rsqrt(jnp.mean(centred * centred, axis=-1, keepdims=True) + EPS)
    return centred * scale, scale


def hidden_norm_body(here_ref, x_ref, a_ref, b_ref, c_ref, gain_ref, shift_ref, hid_ref, out_ref):
    total = a_ref[...].astype(F32) + b_ref[...].astype(F32) + c_ref[...].astype(F32)
    hidden = x_ref[...].astype(F32) + total
    hid_ref[...] = hidden
    unit, _ = unit_of(hidden)
    normed = (unit * gain_ref[...] + shift_ref[...]).astype(BF)
    order = places(x_ref.shape[1] // LANES)

    @pl.when(here_ref[0] == 0)
    def _():
        for i, (place, _) in enumerate(order):
            out_ref[:, lanes_at(place)] = normed[:, lanes_at(i)]

    @pl.when(here_ref[0] != 0)
    def _():
        for i, (_, place) in enumerate(order):
            out_ref[:, lanes_at(place)] = normed[:, lanes_at(i)]


def hidden_norm(here, x, pieces, gain, shift):
    t, width = x.shape
    tile = pl.BlockSpec((ROWS, width), lambda i: (i, 0))
    line = pl.BlockSpec((1, width), lambda i: (0, 0))
    return pl.pallas_call(
        hidden_norm_body,
        grid=(t // ROWS,),
        in_specs=[pl.BlockSpec(memory_space=pltpu.SMEM)] + [tile] * 4 + [line] * 2,
        out_specs=[tile] * 2,
        out_shape=[jax.ShapeDtypeStruct((t, width), F32), jax.ShapeDtypeStruct((t, width), BF)],
        cost_estimate=FREE,
        name="hidden_norm",
    )(here.reshape(1), x, *pieces, gain, shift)


def norm_back_body(
    here_ref, hid_ref, cot_ref, a_ref, b_ref, c_ref, gain_ref, out_ref, bf_ref, sum_ref, tmp_ref
):
    grad = a_ref[...].astype(F32) + b_ref[...].astype(F32) + c_ref[...].astype(F32)
    order = places(cot_ref.shape[1] // LANES)

    @pl.when(here_ref[0] == 0)
    def _():
        for i, (place, _) in enumerate(order):
            tmp_ref[:, lanes_at(i)] = grad[:, lanes_at(place)]

    @pl.when(here_ref[0] != 0)
    def _():
        for i, (_, place) in enumerate(order):
            tmp_ref[:, lanes_at(i)] = grad[:, lanes_at(place)]

    grad = tmp_ref[...]
    unit, scale = unit_of(hid_ref[...])
    e = grad * gain_ref[...]
    mean = jnp.mean(e, axis=-1, keepdims=True)
    inner = jnp.mean(e * unit, axis=-1, keepdims=True)
    total = cot_ref[...].astype(F32) + scale * (e - mean - unit * inner)
    out_ref[...] = total
    bf_ref[...] = total.astype(BF)

    @pl.when(pl.program_id(0) == 0)
    def _():
        sum_ref[...] = jnp.zeros_like(sum_ref)

    sum_ref[0:1] += jnp.sum(grad * unit, axis=0, keepdims=True)
    sum_ref[1:2] += jnp.sum(grad, axis=0, keepdims=True)


def hidden_norm_back(here, hidden, cotangent, pieces, gain):
    t, width = hidden.shape
    tile = pl.BlockSpec((ROWS, width), lambda i: (i, 0))
    line = pl.BlockSpec((1, width), lambda i: (0, 0))
    return pl.pallas_call(
        norm_back_body,
        grid=(t // ROWS,),
        in_specs=[pl.BlockSpec(memory_space=pltpu.SMEM)] + [tile] * 5 + [line],
        out_specs=[tile, tile, pl.BlockSpec((8, width), lambda i: (0, 0))],
        out_shape=[
            jax.ShapeDtypeStruct((t, width), F32),
            jax.ShapeDtypeStruct((t, width), BF),
            jax.ShapeDtypeStruct((8, width), F32),
        ],
        scratch_shapes=[pltpu.VMEM((ROWS, width), F32)],
        cost_estimate=FREE,
        name="hidden_norm_back",
    )(here.reshape(1), hidden, cotangent, *pieces, gain)


def hidden_body(x_ref, gn_ref, gf_ref, un_ref, uf_ref, gate_ref, up_ref, act_ref):
    k = gn_ref.shape[0]
    tile = gn_ref.shape[1]
    near = jnp.concatenate([gn_ref[...], un_ref[...]], axis=1)
    far = jnp.concatenate([gf_ref[...], uf_ref[...]], axis=1)
    both = dot(x_ref[:, :k], near) + dot(x_ref[:, k:], far)
    gate, up = both[:, :tile], both[:, tile:]
    gate_ref[...] = gate
    up_ref[...] = up
    act_ref[...] = (gate * jax.nn.sigmoid(gate) * up).astype(BF)


def hidden_units(x, gate, up):
    m, width = x.shape
    k, n = gate[0].shape
    weight = pl.BlockSpec((k, LANES), lambda j: (0, j))
    tile = pl.BlockSpec((m, LANES), lambda j: (0, j))
    return pl.pallas_call(
        hidden_body,
        grid=(pl.cdiv(n, LANES),),
        in_specs=[pl.BlockSpec((m, width), lambda j: (0, 0))] + [weight] * 4,
        out_specs=[tile] * 3,
        out_shape=[jax.ShapeDtypeStruct((m, n), d) for d in (F32, F32, BF)],
        cost_estimate=FREE,
        name="hidden_units",
    )(x, *gate, *up)


def hidden_back_body(grad_ref, down_ref, gate_ref, up_ref, gg_ref, gu_ref):
    grad = dot_nt(grad_ref[...], down_ref[...])
    gate = gate_ref[...]
    sigmoid = jax.nn.sigmoid(gate)
    gg_ref[...] = (grad * up_ref[...] * sigmoid * (1.0 + gate * (1.0 - sigmoid))).astype(BF)
    gu_ref[...] = (grad * gate * sigmoid).astype(BF)


def hidden_back(grad, down, gate, up, t):
    m, width = grad.shape
    n = down.shape[0]
    tile = pl.BlockSpec((t, n), lambda i: (i, 0))
    return pl.pallas_call(
        hidden_back_body,
        grid=(m // t,),
        in_specs=[
            pl.BlockSpec((t, width), lambda i: (i, 0)),
            pl.BlockSpec((n, width), lambda i: (0, 0)),
            tile,
            tile,
        ],
        out_specs=[tile] * 2,
        out_shape=[jax.ShapeDtypeStruct((m, n), BF)] * 2,
        cost_estimate=FREE,
        name="hidden_back",
    )(grad, down, gate, up)


def input_back_body(steps, gg_ref, gu_ref, gn_ref, gf_ref, un_ref, uf_ref, one_ref, two_ref):
    rows = one_ref.shape[0]

    @pl.when(pl.program_id(0) < steps)
    def _():
        part = dot_nt(gg_ref[...], gn_ref[...]) + dot_nt(gu_ref[...], un_ref[...])
        one_ref[...] = part[:rows].astype(BF)
        two_ref[...] = part[rows:].astype(BF)

    @pl.when(pl.program_id(0) >= steps)
    def _():
        part = dot_nt(gg_ref[...], gf_ref[...]) + dot_nt(gu_ref[...], uf_ref[...])
        one_ref[...] = part[:rows].astype(BF)
        two_ref[...] = part[rows:].astype(BF)


def input_back(grad_gate, grad_up, gate, up):
    m, n = grad_gate.shape
    k = gate[0].shape[0]
    tile = 2 * LANES
    steps = k // tile
    whole = pl.BlockSpec((m, n), lambda i: (0, 0))
    near = pl.BlockSpec((tile, n), lambda i: (jnp.minimum(i, steps - 1), 0))
    far = pl.BlockSpec((tile, n), lambda i: (jnp.maximum(i - steps, 0), 0))
    return pl.pallas_call(
        functools.partial(input_back_body, steps),
        grid=(2 * steps,),
        in_specs=[whole, whole, near, far, near, far],
        out_specs=[pl.BlockSpec((m // 2, tile), lambda i: (0, i))] * 2,
        out_shape=[jax.ShapeDtypeStruct((m // 2, 2 * k), BF)] * 2,
        cost_estimate=FREE,
        name="input_back",
    )(grad_gate, grad_up, *gate, *up)


def local(
    sizes,
    tokens_in,
    cotangent,
    segment_ids,
    attn_gain,
    attn_shift,
    qkv_weight,
    qkv_bias,
    out_weight,
    mlp_gain,
    mlp_shift,
    gate_weight,
    up_weight,
    down_weight,
):
    nz, ny, nx, nc = sizes
    seq, peers = nz * ny, nx * nc
    devices = seq * peers
    pair = nx == 2 and ny == 2
    att, att_rows = ("x", "y") if pair else (None, None)
    fwd, fwd_rows = ("y", "x") if pair else (None, None)
    fwd_axes = ("y", "c") if pair else BATCH
    t, width = tokens_in.shape[1:]
    length = segment_ids.shape[1]
    heads = width // HEAD_DIM // peers
    pairs = heads // 2
    groups = seq // pairs
    rpg = peers // groups
    ff = down_weight.shape[0] * devices
    strip = ff // devices
    own_head = width // devices == HEAD_DIM
    window = min((length // 3 - 1 + t - 1) // t + 1, length // t)
    me_seq = lax.axis_index(SEQ)
    me_peer = lax.axis_index(BATCH)

    small = jnp.concatenate([attn_gain, attn_shift, mlp_gain, mlp_shift, qkv_bias])
    small = jnp.broadcast_to(small[None], (devices, small.size))
    small = lax.all_to_all(small, ALL, split_axis=0, concat_axis=0, tiled=True).astype(F32)
    each = attn_gain.size
    gain_one, shift_one, gain_two, shift_two = [
        small[:, i * each : (i + 1) * each].reshape(1, width) for i in range(4)
    ]
    bias = small[:, 4 * each :].reshape(3, heads, peers, HEAD_DIM)
    bias = lax.dynamic_index_in_dim(bias, me_peer, 2, keepdims=False).reshape(1, -1)

    rows = qkv_weight.shape[0]
    third = width // peers
    qkv_mine = qkv_weight.reshape(rows, 3, heads, peers, HEAD_DIM).transpose(3, 0, 1, 2, 4)
    qkv_mine = swap_peers(qkv_mine.reshape(peers, rows, -1), BATCH).reshape(peers * rows, -1)

    def columns(w):
        if pair:
            w = w.reshape(rows, nz, 2, 2, nc, strip).transpose(2, 4, 0, 1, 3, 5)
        else:
            w = w.reshape(rows, seq, peers, strip).transpose(2, 0, 1, 3)
        return w.reshape(peers, rows, -1)

    merge_att = functools.partial(merge_rows, axis=att_rows, nz=nz)
    merge_ff = functools.partial(merge_rows, axis=fwd_rows, nz=nz)
    split = 2 if pair else 1
    mine = jnp.concatenate([columns(gate_weight), columns(up_weight)], axis=1)
    mine = swap_peers(after(mine, small), fwd_axes)
    gate_mine = mine[:, :rows].reshape(peers * rows, -1)
    up_mine = mine[:, rows:].reshape(peers * rows, -1)
    kv_near, q_near = gather_z(qkv_mine[:, third:]), gather_z(qkv_mine[:, :third])
    kv_near, gate_mine, up_mine = lax.optimization_barrier((kv_near, gate_mine, up_mine))
    kv_far = gather_far(kv_near, att_rows)
    gate_near = gather_z(gate_mine)
    gate_far = gather_far(gate_near, fwd_rows)
    if own_head:
        out_near = gather_z(after(out_weight, gate_near))
    else:
        out_full = lax.all_gather(out_weight, ALL, axis=0, tiled=True)
        out_full = out_full.reshape(heads, peers, HEAD_DIM, width)
        out_full = lax.dynamic_index_in_dim(out_full, me_peer, 1, keepdims=False)
        out_full = out_full.reshape(heads * HEAD_DIM, width)

    kv_far, q_near, segment = lax.optimization_barrier(
        (kv_far, q_near, gather_peers(segment_ids, att))
    )
    q_far = gather_far(q_near, att_rows)
    q_full, kv_full = merge_att(q_near, q_far), merge_att(kv_near, kv_far)
    start = jnp.zeros_like(segment)
    for doc in range(DOCS):
        count = jnp.sum((segment == doc).astype(jnp.int32), axis=1, keepdims=True)
        start = start + jnp.where(segment > doc, count, 0)
    places = me_seq * t + jnp.arange(t, dtype=jnp.int32)
    here = places[None] - lax.dynamic_slice_in_dim(start, me_seq * t, t, 1)
    half = ROT // 2
    inverse = 10000.0 ** (-jnp.arange(half, dtype=F32) / half)
    theta = inverse[:, None] * here.reshape(1, -1).astype(F32)
    cosine, sine = jnp.cos(theta), jnp.sin(theta)
    rest = jnp.ones((HEAD_DIM - ROT, theta.shape[1]), F32)
    cosine = jnp.concatenate([cosine, cosine, rest] * 2, axis=0).T
    sine = jnp.concatenate([-sine, sine, 0.0 * rest] * 2, axis=0).T
    start = lax.dynamic_slice_in_dim(start, (me_seq % groups) * rpg, rpg, 0)
    start = start.reshape(rpg, length // t, t, 1)

    inputs = tokens_in[0].astype(F32)
    unit_one, scale_one = norm_stats(inputs)
    normed = (unit_one * gain_one + shift_one).astype(BF)
    normed_all = gather_peers(normed, att)
    key_value = rotary_out(
        dot(normed_all, kv_full), bias[:, third:], cosine, sine, pairs, rpg, t, 1
    )
    key_value = swap_seq(key_value)
    query = rotary_out(dot(normed_all, q_full), bias[:, :third], cosine, sine, pairs, rpg, t, 1)
    query = swap_seq(after(query, key_value))
    qkv_full = jnp.concatenate([q_full, kv_full], axis=1)
    up_near = gather_z(up_mine)
    grad_output = cotangent[0]
    grad_all = gather_peers(grad_output, fwd)
    query, key_value, up_near = lax.optimization_barrier((query, key_value, up_near))
    mixed = attend(query, key_value, start, window)
    mixed, gate_far = lax.optimization_barrier((mixed, gate_far))
    if own_head:
        out_near = after(out_near, mixed)
    up_far = gather_far(up_near, fwd_rows)
    mixed = swap_seq(mixed)
    if own_head:
        out_full = merge_att(out_near, gather_far(out_near, att_rows))
    down_near = gather_z(down_weight)
    mixed, up_far, grad_all, qkv_full, out_full = lax.optimization_barrier(
        (mixed, up_far, grad_all, qkv_full, out_full)
    )

    def token_rows(x):
        x = x.reshape(pairs, groups * rpg * t, LANES).transpose(1, 0, 2)
        return x.reshape(groups * rpg * t, pairs * LANES)

    def head_rows(x):
        x = x.reshape(groups * rpg * t, pairs, LANES).transpose(1, 0, 2)
        return x.reshape(seq, rpg, t, LANES)

    mixed = token_rows(mixed)
    branch_one = halves_of(dot, mixed, out_full)
    if pair:
        here_x = lax.axis_index("x")
        branch_one = reduce_pieces(branch_one, att)
        hidden, normed_two = hidden_norm(here_x, tokens_in[0], branch_one, gain_two, shift_two)
        gate_full, up_full = (gate_near, gate_far), (up_near, up_far)
    else:
        hidden = inputs + reduce_peers(branch_one, att)
        unit_two, scale_two = norm_stats(hidden)
        normed_two = (unit_two * gain_two + shift_two).astype(BF)
        gate_full = jnp.split(merge_ff(gate_near, gate_far), 2)
        up_full = jnp.split(merge_ff(up_near, up_far), 2)
    ready = branch_one[2] if pair else normed_two
    down_far = gather_far(after(down_near, ready), fwd_rows)
    normed_two_all = gather_peers(normed_two, fwd)
    gate, up, act = hidden_units(normed_two_all, gate_full, up_full)
    down_full = merge_ff(down_near, after(down_far, gate))

    send_att = functools.partial(send_rows, axis=att_rows, nz=nz, na=ny)
    send_ff = functools.partial(send_rows, axis=fwd_rows, nz=nz, na=nx if pair else ny)
    wide = width // 2
    down_one = send_ff(dot_tn(act, grad_all[:, :wide], BF))
    grad_gate, grad_up = hidden_back(grad_all, down_full, gate, up, t)
    part = input_back(grad_gate, grad_up, gate_full, up_full)
    down_one = add_rows(*down_one)
    part, down_one = lax.optimization_barrier((part, down_one))
    down_two = send_ff(dot_tn(act, grad_all[:, wide:], BF))
    if pair:
        grad_normed_two = reduce_pieces(part, fwd)
    else:
        grad_normed_two = reduce_peers(part, fwd)

    def dots(g):
        if not pair:
            return (dot_tn(normed_two_all, g, BF),)
        return dot_tn(normed_two_all[:, wide:], g, BF), dot_tn(normed_two_all[:, :wide], g, BF)

    def send_columns(g):
        if not pair:
            return send_ff(g[0])
        return g[1], lax.ppermute(g[0], "x", SWAP)

    cut_ff = grad_gate.shape[1] // 256 * 128 + LANES
    gate_one, gate_two = dots(grad_gate[:, :cut_ff]), dots(grad_gate[:, cut_ff:])
    grad_normed_two, gate_one, gate_two = lax.optimization_barrier(
        (grad_normed_two, gate_one, gate_two)
    )
    gate_one, gate_two, up_w = [send_columns(g) for g in (gate_one, gate_two, dots(grad_up))]
    down_one, down_two = scatter_z(down_one), add_rows(*down_two)
    grad_normed_two, down_one, down_two = lax.optimization_barrier(
        (grad_normed_two, down_one, down_two)
    )
    down_two = scatter_z(down_two)
    if pair:
        grad_hidden, branch, sums = hidden_norm_back(
            here_x, hidden, grad_output, grad_normed_two, gain_two
        )
        grad_gain_two, grad_shift_two = sums[0], sums[1]
    else:
        back, grad_gain_two, grad_shift_two = norm_back(
            grad_normed_two, unit_two, scale_two, gain_two
        )
        grad_hidden = grad_output.astype(F32) + back
        branch = grad_hidden.astype(BF)

    def ff_swap(g):
        return swap_peers(g.reshape(peers, rows, -1), fwd_axes)

    def ff_columns(g):
        if pair:
            g = g.reshape(2, nc, rows, nz, 2, strip).transpose(2, 3, 0, 4, 1, 5)
        else:
            g = g.reshape(peers, rows, seq, strip).transpose(1, 2, 0, 3)
        return g.reshape(rows, ff).astype(F32)

    branch = gather_peers(branch, att)
    grad_mixed = head_rows(dot_nt(branch, out_full, BF))
    grad_mixed, down_two = lax.optimization_barrier((grad_mixed, down_two))
    branch_two = reduce_peers(halves_of(dot, after(act, grad_mixed), down_full), fwd)
    block_out = (hidden + branch_two).astype(BF).reshape(tokens_in.shape)
    grad_mixed = swap_seq(grad_mixed)
    grad_out = dot_tn(mixed, branch, BF)
    if pair:
        near, far, grad_out = lax.optimization_barrier((*gate_one, grad_out))
        gate_one = near, far
    gate_one = add_rows(*gate_one)
    grad_mixed, gate_one = lax.optimization_barrier((grad_mixed, gate_one))
    gate_one = scatter_z(gate_one)
    grad_qkv = attend_back(query, key_value, start, grad_mixed, window)
    if own_head:
        grad_out = send_att(grad_out)
    grad_qkv, gate_one, gate_two, grad_out = lax.optimization_barrier(
        (grad_qkv, gate_one, gate_two, grad_out)
    )
    if own_head:
        grad_out = scatter_z(add_rows(*grad_out))
    gate_two = scatter_z(add_rows(*gate_two))
    grad_qkv = swap_seq(grad_qkv)
    grad_down = jnp.concatenate([down_one, down_two], axis=1).astype(F32)
    up_sum = add_rows(*up_w)
    up_w = scatter_z(up_sum)
    grad_qkv, up_sum, grad_out, grad_down, block_out = lax.optimization_barrier(
        (grad_qkv, up_sum, grad_out, grad_down, block_out)
    )
    if not own_head:
        mine = (jnp.arange(peers) == me_peer).astype(BF)[None, :, None, None]
        grad_out = grad_out.reshape(heads, 1, HEAD_DIM, width) * mine
        grad_out = lax.psum_scatter(
            grad_out.reshape(width, width), ALL, scatter_dimension=0, tiled=True
        )
    grad_proj = rotary_in(grad_qkv, cosine, sine, pairs)
    gate_w = ff_swap(jnp.concatenate([gate_one, gate_two], axis=1))
    cut = 3 * third // 2
    first = send_att(dot_tn(normed_all, grad_proj[:, :cut], BF))
    second = dot_tn(normed_all, grad_proj[:, cut:], BF)
    grad_normed = halves_of(dot_nt, grad_proj, qkv_full)
    grad_normed, first, second, gate_w = lax.optimization_barrier(
        (grad_normed, first, second, gate_w)
    )
    grad_gate_w = ff_columns(gate_w)
    second = send_att(second)
    grad_normed = reduce_peers(grad_normed, att)
    first = add_rows(*first)
    first, up_w = lax.optimization_barrier((first, up_w))
    if pair:
        second = (second[0], after(second[1], first))
    first = scatter_z(first)
    back, grad_gain_one, grad_shift_one = norm_back(grad_normed, unit_one, scale_one, gain_one)
    grad_tokens = (grad_hidden + back).astype(BF).reshape(tokens_in.shape)
    second = add_rows(*second)
    second, first, grad_tokens, up_w, grad_gate_w = lax.optimization_barrier(
        (second, first, grad_tokens, up_w, grad_gate_w)
    )
    second = scatter_z(second)
    grad_up_w = ff_columns(ff_swap(up_w))
    second, grad_up_w = lax.optimization_barrier((second, grad_up_w))
    grad_out = grad_out.astype(F32)
    grad_qkv_w = []
    for half in (first, second):
        half = swap_peers(half.reshape(peers, rows, -1), BATCH)
        half = half.reshape(peers, rows, -1, HEAD_DIM).transpose(1, 2, 0, 3)
        grad_qkv_w.append(half.reshape(rows, -1).astype(F32))
    grad_qkv_w = jnp.concatenate(grad_qkv_w, axis=1)
    grad_bias = jnp.sum(grad_proj.astype(F32), axis=0).reshape(3, heads, 1, HEAD_DIM)
    mine = (jnp.arange(peers) == me_peer).astype(F32)[None, None, :, None]
    grad_bias = (grad_bias * mine).reshape(devices, -1)

    vectors = [grad_gain_one, grad_shift_one, grad_gain_two, grad_shift_two]
    vectors = [v.reshape(devices, each) for v in vectors] + [grad_bias]
    vectors = jnp.concatenate(vectors, axis=1)
    vectors = lax.all_to_all(vectors, ALL, split_axis=0, concat_axis=0, tiled=True)
    vectors = jnp.sum(vectors, axis=0)
    g1, s1, g2, s2 = [vectors[i * each : (i + 1) * each] for i in range(4)]
    return (
        block_out,
        grad_tokens,
        g1,
        s1,
        grad_qkv_w,
        vectors[4 * each :],
        grad_out,
        g2,
        s2,
        grad_gate_w,
        grad_up_w,
        grad_down,
    )


def solution(mesh):
    seq, batch = mesh.shape["seq"], mesh.shape["batch"]
    sizes = (4, seq // 4, batch // 2, 2)
    fine = Mesh(mesh.devices.reshape(sizes), ALL)
    token = P(BATCH, SEQ, None)
    vector = P(ALL)
    matrix = P(ALL, None)
    return jax.shard_map(
        functools.partial(local, sizes),
        mesh=fine,
        in_specs=(
            token,
            token,
            P(BATCH, None),
            vector,
            vector,
            matrix,
            vector,
            matrix,
            vector,
            vector,
            matrix,
            matrix,
            matrix,
        ),
        out_specs=(
            token,
            token,
            vector,
            vector,
            matrix,
            vector,
            matrix,
            vector,
            vector,
            matrix,
            matrix,
            matrix,
        ),
        check_vma=False,
    )
```

```python
import functools

import jax
import jax.numpy as jnp
from jax import lax
from jax.experimental import pallas as pl
from jax.experimental.pallas import tpu as pltpu
from jax.sharding import Mesh
from jax.sharding import PartitionSpec as P

HEAD_DIM = 64
ROT = 16
DOCS = 6
LANES = 128
EPS = 1e-05
BF = jnp.bfloat16
F32 = jnp.float32
NEG = -1e30
ALL = ("z", "y", "x", "c")
SEQ = ("z", "y")
BATCH = ("x", "c")
SWAP = ((0, 1), (1, 0))


def dot(a, b, out=F32):
    return jnp.dot(a, b, preferred_element_type=out)


def dot_nt(a, b, out=F32):
    return lax.dot_general(a, b, (((1,), (1,)), ((), ())), preferred_element_type=out)


def dot_tn(a, b, out=F32):
    return lax.dot_general(a, b, (((0,), (0,)), ((), ())), preferred_element_type=out)


def after(x, *first):
    return lax.optimization_barrier((x,) + first)[0]


def gather_peers(x, axis):
    if axis is None:
        return lax.all_gather(x, BATCH, axis=0, tiled=True)
    other = lax.ppermute(x, axis, SWAP)
    far = lax.ppermute(x, "c", SWAP)
    last = lax.ppermute(other, "c", SWAP)
    return jnp.concatenate([x, other, far, last], axis=0)


def reduce_peers(halves, axis):
    near, far = halves
    if axis is None:
        part = jnp.concatenate([near, far], axis=0)
        return lax.psum_scatter(part, BATCH, scatter_dimension=0, tiled=True).astype(F32)
    rows = near.shape[0] // 2
    got = lax.ppermute(far, "c", SWAP)
    send = (near[rows:].astype(F32) + got[rows:].astype(F32)).astype(BF)
    last = lax.ppermute(send, axis, SWAP)
    return near[:rows].astype(F32) + got[:rows].astype(F32) + last.astype(F32)


def reduce_pieces(halves, axis):
    near, far = halves
    rows = near.shape[0] // 2
    got = lax.ppermute(far, "c", SWAP)
    send = (near[rows:].astype(F32) + got[rows:].astype(F32)).astype(BF)
    return near, got, lax.ppermute(send, axis, SWAP)


def halves_of(product, x, w):
    rows = x.shape[0] // 2
    return product(x[:rows], w, BF), product(x[rows:], w, BF)


def gather_z(w):
    return lax.all_gather(w, "z", axis=0, tiled=True)


def gather_far(near, axis):
    if axis is None:
        return lax.all_gather(near, "y", axis=0)
    return lax.ppermute(near, axis, SWAP)


def merge_rows(near, far, axis, nz, inner=1):
    wide = near.shape[-1]
    if axis is None:
        far = far.reshape(far.shape[0], nz, -1, wide).transpose(1, 0, 2, 3)
        return far.reshape(-1, wide)
    near = near.reshape(nz * inner, 1, -1, wide)
    far = far.reshape(near.shape)
    first = lax.axis_index(axis) == 0
    full = jnp.concatenate([jnp.where(first, near, far), jnp.where(first, far, near)], axis=1)
    return full.reshape(-1, wide)


def send_rows(g, axis, nz, na, inner=1):
    rows = g.shape[0] // (nz * na)
    if axis is None:
        g = g.reshape(nz, na, rows, -1).transpose(1, 0, 2, 3).reshape(na, nz * rows, -1)
        return None, lax.psum_scatter(g, "y", scatter_dimension=0, tiled=True)[0]
    g = g.reshape(nz * inner, na, rows // inner, g.shape[1])
    here = lax.axis_index(axis)
    send = lax.dynamic_index_in_dim(g, 1 - here, 1, keepdims=False)
    keep = lax.dynamic_index_in_dim(g, here, 1, keepdims=False)
    return keep, lax.ppermute(send, axis, SWAP)


def add_rows(keep, got):
    if keep is None:
        return got
    got = (keep.astype(F32) + got.astype(F32)).astype(BF)
    return got.reshape(-1, got.shape[-1])


def scatter_z(g):
    return lax.psum_scatter(g, "z", scatter_dimension=0, tiled=True)


def reduce_z(keep, got):
    return scatter_z(add_rows(keep, got))


def swap_peers(x, axes):
    return lax.all_to_all(x, axes, split_axis=0, concat_axis=0, tiled=True)


def swap_seq(x):
    return lax.all_to_all(x, SEQ, split_axis=0, concat_axis=0, tiled=True)


def norm_stats(value):
    centred = value - jnp.mean(value, axis=-1, keepdims=True)
    scale = lax.rsqrt(jnp.mean(centred * centred, axis=-1, keepdims=True) + EPS)
    return centred * scale, scale


def norm_back(grad, unit, scale, gain):
    e = grad * gain
    back = scale * (
        e - jnp.mean(e, axis=-1, keepdims=True) - unit * jnp.mean(e * unit, axis=-1, keepdims=True)
    )
    return back, jnp.sum(grad * unit, axis=0), jnp.sum(grad, axis=0)


def turn(value, cosine, sine, lane):
    inner = lane % HEAD_DIM
    ahead = pltpu.roll(value, LANES - ROT // 2, 1)
    behind = pltpu.roll(value, ROT // 2, 1)
    return value * cosine + jnp.where(inner < ROT // 2, ahead, behind) * sine


def rotary_out_body(turned, proj_ref, bias_ref, cos_ref, sin_ref, out_ref):
    pairs = out_ref.shape[0]
    cosine, sine = cos_ref[...], sin_ref[...]
    lane = lax.broadcasted_iota(jnp.int32, cosine.shape, 1)
    rotate = pl.program_id(1) < turned
    for i in range(pairs):
        at = slice(i * LANES, (i + 1) * LANES)
        value = proj_ref[:, at] + bias_ref[:, at]
        value = jnp.where(rotate, turn(value, cosine, sine, lane), value)
        out_ref[i] = value.astype(BF).reshape(out_ref.shape[1:])


def rotary_out(proj, bias, cosine, sine, pairs, rpg, t, turned):
    peers = proj.shape[0] // t
    groups = peers // rpg
    wide = pairs * LANES
    parts = proj.shape[1] // wide
    out = pl.pallas_call(
        functools.partial(rotary_out_body, turned),
        grid=(peers, parts),
        in_specs=[
            pl.BlockSpec((t, wide), lambda b, p: (b, p)),
            pl.BlockSpec((1, wide), lambda b, p: (0, p)),
            pl.BlockSpec((t, LANES), lambda b, p: (b, 0)),
            pl.BlockSpec((t, LANES), lambda b, p: (b, 0)),
        ],
        out_specs=pl.BlockSpec(
            (pairs, 1, 1, 1, t, LANES), lambda b, p: (0, b // rpg, p, b % rpg, 0, 0)
        ),
        out_shape=jax.ShapeDtypeStruct((pairs, groups, parts, rpg, t, LANES), BF),
        cost_estimate=pl.CostEstimate(
            flops=1, bytes_accessed=1, transcendentals=0
        ),
        name="rotary_out",
    )(proj, bias, cosine, sine)
    return out.reshape((pairs * groups,) + out.shape[2:])


def rotary_in_body(grad_ref, cos_ref, sin_ref, out_ref):
    pairs = grad_ref.shape[0]
    cosine, sine = cos_ref[...], -sin_ref[...]
    lane = lax.broadcasted_iota(jnp.int32, cosine.shape, 1)
    rotate = pl.program_id(1) < 2
    for i in range(pairs):
        value = grad_ref[i].reshape(cosine.shape).astype(F32)
        value = jnp.where(rotate, turn(value, cosine, sine, lane), value)
        out_ref[:, i * LANES : (i + 1) * LANES] = value.astype(BF)


def rotary_in(grad, cosine, sine, pairs):
    dests, parts, rpg, t, _ = grad.shape
    groups = dests // pairs
    wide = pairs * LANES
    return pl.pallas_call(
        rotary_in_body,
        grid=(groups * rpg, parts),
        in_specs=[
            pl.BlockSpec(
                (pairs, 1, 1, 1, t, LANES), lambda b, p: (0, b // rpg, p, b % rpg, 0, 0)
            ),
            pl.BlockSpec((t, LANES), lambda b, p: (b, 0)),
            pl.BlockSpec((t, LANES), lambda b, p: (b, 0)),
        ],
        out_specs=pl.BlockSpec((t, wide), lambda b, p: (b, p)),
        out_shape=jax.ShapeDtypeStruct((groups * rpg * t, parts * wide), BF),
        cost_estimate=pl.CostEstimate(
            flops=1, bytes_accessed=1, transcendentals=0
        ),
        name="rotary_in",
    )(grad.reshape((pairs, groups) + grad.shape[1:]), cosine, sine)


def by_head(x):
    lane = lax.broadcasted_iota(jnp.int32, x.shape, 1)
    zero = jnp.zeros_like(x)
    return jnp.concatenate(
        [jnp.where(lane < HEAD_DIM, x, zero), jnp.where(lane >= HEAD_DIM, x, zero)], axis=0
    )


def one_head(x):
    t = x.shape[0] // 2
    lane = lax.broadcasted_iota(jnp.int32, (t, LANES), 1)
    return jnp.where(lane < HEAD_DIM, x[:t], x[t:])


def window_weights(q2, keys, start, row0, col0):
    scores = dot_nt(q2, keys) * (HEAD_DIM**-0.5)
    t = q2.shape[0] // 2
    shape = (t, keys.shape[0])
    rows = row0 + lax.broadcasted_iota(jnp.int32, shape, 0)
    cols = col0 + lax.broadcasted_iota(jnp.int32, shape, 1)
    allowed = (cols <= rows) & (cols >= start)
    allowed = jnp.concatenate([allowed, allowed], axis=0)
    scores = jnp.where(allowed, scores, NEG)
    weights = jnp.exp(scores - jnp.max(scores, axis=-1, keepdims=True))
    return weights / jnp.sum(weights, axis=-1, keepdims=True)


def by_window(window, body):
    number = pl.program_id(1)
    for w in range(1, window + 1):
        pl.when(number == w - 1 if w < window else number >= w - 1)(functools.partial(body, w))


def forward_body(window, q_ref, k_ref, v_ref, start_ref, out_ref):
    number = pl.program_id(1)
    t = q_ref.shape[3]

    def body(w):
        first = number - (w - 1)
        keys = k_ref[pl.ds(first, w), 0, 0].reshape(w * t, LANES)
        values = v_ref[pl.ds(first, w), 0, 0].reshape(w * t, LANES)
        q2 = by_head(q_ref[0, 0, 0])
        weights = window_weights(q2, keys, start_ref[0, 0], number * t, first * t)
        out_ref[0, 0] = one_head(dot(weights.astype(BF), values)).astype(BF)

    by_window(window, body)


def attention_specs(blocks, t):
    return [
        pl.BlockSpec((1, 1, 1, t, LANES), lambda r, i: (i, 0, r, 0, 0)),
        pl.BlockSpec((blocks, 1, 1, t, LANES), lambda r, i: (0, 0, r, 0, 0)),
        pl.BlockSpec((blocks, 1, 1, t, LANES), lambda r, i: (0, 1, r, 0, 0)),
        pl.BlockSpec((1, 1, t, 1), lambda r, i: (r, i, 0, 0)),
    ]


def attend(q, kv, start, window):
    blocks, _, rpg, t, _ = q.shape
    work = rpg * blocks * 2 * t * window * t
    return pl.pallas_call(
        functools.partial(forward_body, window),
        grid=(rpg, blocks),
        in_specs=attention_specs(blocks, t),
        out_specs=pl.BlockSpec((1, 1, t, LANES), lambda r, i: (i, r, 0, 0)),
        out_shape=jax.ShapeDtypeStruct((blocks, rpg, t, LANES), BF),
        cost_estimate=pl.CostEstimate(
            flops=1, bytes_accessed=1, transcendentals=0
        ),
        name="attend",
    )(q, kv, kv, start)


def backward_body(window, q_ref, k_ref, v_ref, start_ref, do_ref, out_ref, dk_ref, dv_ref):
    number = pl.program_id(1)
    t = q_ref.shape[3]
    scale = HEAD_DIM**-0.5

    @pl.when(number == 0)
    def _():
        dk_ref[...] = jnp.zeros_like(dk_ref)
        dv_ref[...] = jnp.zeros_like(dv_ref)

    def body(w):
        first = number - (w - 1)
        keys = k_ref[pl.ds(first, w), 0, 0].reshape(w * t, LANES)
        values = v_ref[pl.ds(first, w), 0, 0].reshape(w * t, LANES)
        q2 = by_head(q_ref[0, 0, 0])
        do2 = by_head(do_ref[0, 0])
        weights = window_weights(q2, keys, start_ref[0, 0], number * t, first * t)
        grad = dot_nt(do2, values)
        inner = jnp.sum(weights * grad, axis=-1, keepdims=True)
        ds = (weights * (grad - inner)).astype(BF)
        out_ref[number, 0, 0] = one_head(dot(ds, keys) * scale).astype(BF)
        shape = (w, t, LANES)
        dk_ref[pl.ds(first, w)] += dot_tn(ds, q2).reshape(shape)
        dv_ref[pl.ds(first, w)] += dot_tn(weights.astype(BF), do2).reshape(shape)

    by_window(window, body)

    @pl.when(number == pl.num_programs(1) - 1)
    def _():
        out_ref[:, 1, 0] = (dk_ref[...] * scale).astype(BF)
        out_ref[:, 2, 0] = dv_ref[...].astype(BF)


def attend_back(q, kv, start, grad, window):
    blocks, _, rpg, t, _ = q.shape
    work = rpg * blocks * 2 * t * window * t
    return pl.pallas_call(
        functools.partial(backward_body, window),
        grid=(rpg, blocks),
        in_specs=attention_specs(blocks, t)
        + [pl.BlockSpec((1, 1, t, LANES), lambda r, i: (i, r, 0, 0))],
        out_specs=pl.BlockSpec((blocks, 3, 1, t, LANES), lambda r, i: (0, 0, r, 0, 0)),
        out_shape=jax.ShapeDtypeStruct((blocks, 3, rpg, t, LANES), BF),
        scratch_shapes=[
            pltpu.VMEM((blocks, t, LANES), F32),
            pltpu.VMEM((blocks, t, LANES), F32),
        ],
        cost_estimate=pl.CostEstimate(
            flops=1, bytes_accessed=1, transcendentals=0
        ),
        name="attend_back",
    )(q, kv, kv, start, grad)


FREE = pl.CostEstimate(flops=1, bytes_accessed=1, transcendentals=0)


ROWS = 64


def places(count):
    half = count // 2
    return [((i % 2) * half + i // 2, (1 - i % 2) * half + i // 2) for i in range(count)]


def lanes_at(i):
    return slice(i * LANES, (i + 1) * LANES)


def unit_of(value):
    centred = value - jnp.mean(value, axis=-1, keepdims=True)
    scale = lax.rsqrt(jnp.mean(centred * centred, axis=-1, keepdims=True) + EPS)
    return centred * scale, scale


def hidden_norm_body(here_ref, x_ref, a_ref, b_ref, c_ref, gain_ref, shift_ref, hid_ref, out_ref):
    total = a_ref[...].astype(F32) + b_ref[...].astype(F32) + c_ref[...].astype(F32)
    hidden = x_ref[...].astype(F32) + total
    hid_ref[...] = hidden
    unit, _ = unit_of(hidden)
    normed = (unit * gain_ref[...] + shift_ref[...]).astype(BF)
    order = places(x_ref.shape[1] // LANES)

    @pl.when(here_ref[0] == 0)
    def _():
        for i, (place, _) in enumerate(order):
            out_ref[:, lanes_at(place)] = normed[:, lanes_at(i)]

    @pl.when(here_ref[0] != 0)
    def _():
        for i, (_, place) in enumerate(order):
            out_ref[:, lanes_at(place)] = normed[:, lanes_at(i)]


def hidden_norm(here, x, pieces, gain, shift):
    t, width = x.shape
    tile = pl.BlockSpec((ROWS, width), lambda i: (i, 0))
    line = pl.BlockSpec((1, width), lambda i: (0, 0))
    return pl.pallas_call(
        hidden_norm_body,
        grid=(t // ROWS,),
        in_specs=[pl.BlockSpec(memory_space=pltpu.SMEM)] + [tile] * 4 + [line] * 2,
        out_specs=[tile] * 2,
        out_shape=[jax.ShapeDtypeStruct((t, width), F32), jax.ShapeDtypeStruct((t, width), BF)],
        cost_estimate=FREE,
        name="hidden_norm",
    )(here.reshape(1), x, *pieces, gain, shift)


def norm_back_body(
    here_ref, hid_ref, cot_ref, a_ref, b_ref, c_ref, gain_ref, out_ref, bf_ref, sum_ref, tmp_ref
):
    grad = a_ref[...].astype(F32) + b_ref[...].astype(F32) + c_ref[...].astype(F32)
    order = places(cot_ref.shape[1] // LANES)

    @pl.when(here_ref[0] == 0)
    def _():
        for i, (place, _) in enumerate(order):
            tmp_ref[:, lanes_at(i)] = grad[:, lanes_at(place)]

    @pl.when(here_ref[0] != 0)
    def _():
        for i, (_, place) in enumerate(order):
            tmp_ref[:, lanes_at(i)] = grad[:, lanes_at(place)]

    grad = tmp_ref[...]
    unit, scale = unit_of(hid_ref[...])
    e = grad * gain_ref[...]
    mean = jnp.mean(e, axis=-1, keepdims=True)
    inner = jnp.mean(e * unit, axis=-1, keepdims=True)
    total = cot_ref[...].astype(F32) + scale * (e - mean - unit * inner)
    out_ref[...] = total
    bf_ref[...] = total.astype(BF)

    @pl.when(pl.program_id(0) == 0)
    def _():
        sum_ref[...] = jnp.zeros_like(sum_ref)

    sum_ref[0:1] += jnp.sum(grad * unit, axis=0, keepdims=True)
    sum_ref[1:2] += jnp.sum(grad, axis=0, keepdims=True)


def hidden_norm_back(here, hidden, cotangent, pieces, gain):
    t, width = hidden.shape
    tile = pl.BlockSpec((ROWS, width), lambda i: (i, 0))
    line = pl.BlockSpec((1, width), lambda i: (0, 0))
    return pl.pallas_call(
        norm_back_body,
        grid=(t // ROWS,),
        in_specs=[pl.BlockSpec(memory_space=pltpu.SMEM)] + [tile] * 5 + [line],
        out_specs=[tile, tile, pl.BlockSpec((8, width), lambda i: (0, 0))],
        out_shape=[
            jax.ShapeDtypeStruct((t, width), F32),
            jax.ShapeDtypeStruct((t, width), BF),
            jax.ShapeDtypeStruct((8, width), F32),
        ],
        scratch_shapes=[pltpu.VMEM((ROWS, width), F32)],
        cost_estimate=FREE,
        name="hidden_norm_back",
    )(here.reshape(1), hidden, cotangent, *pieces, gain)


def hidden_body(x_ref, gn_ref, gf_ref, un_ref, uf_ref, gate_ref, up_ref, act_ref):
    k = gn_ref.shape[0]
    tile = gn_ref.shape[1]
    near = jnp.concatenate([gn_ref[...], un_ref[...]], axis=1)
    far = jnp.concatenate([gf_ref[...], uf_ref[...]], axis=1)
    both = dot(x_ref[:, :k], near) + dot(x_ref[:, k:], far)
    gate, up = both[:, :tile], both[:, tile:]
    gate_ref[...] = gate
    up_ref[...] = up
    act_ref[...] = (gate * jax.nn.sigmoid(gate) * up).astype(BF)


def hidden_units(x, gate, up):
    m, width = x.shape
    k, n = gate[0].shape
    weight = pl.BlockSpec((k, LANES), lambda j: (0, j))
    tile = pl.BlockSpec((m, LANES), lambda j: (0, j))
    return pl.pallas_call(
        hidden_body,
        grid=(pl.cdiv(n, LANES),),
        in_specs=[pl.BlockSpec((m, width), lambda j: (0, 0))] + [weight] * 4,
        out_specs=[tile] * 3,
        out_shape=[jax.ShapeDtypeStruct((m, n), d) for d in (F32, F32, BF)],
        cost_estimate=FREE,
        name="hidden_units",
    )(x, *gate, *up)


def hidden_back_body(grad_ref, one_ref, two_ref, gate_ref, up_ref, gg_ref, gu_ref):
    k = one_ref.shape[1]
    grad = dot_nt(grad_ref[:, :k], one_ref[...]) + dot_nt(grad_ref[:, k:], two_ref[...])
    gate = gate_ref[...]
    sigmoid = jax.nn.sigmoid(gate)
    gg_ref[...] = (grad * up_ref[...] * sigmoid * (1.0 + gate * (1.0 - sigmoid))).astype(BF)
    gu_ref[...] = (grad * gate * sigmoid).astype(BF)


def hidden_back(grad, down, gate, up, t):
    m, width = grad.shape
    n, k = down[0].shape
    tile = pl.BlockSpec((t, n), lambda i: (i, 0))
    return pl.pallas_call(
        hidden_back_body,
        grid=(m // t,),
        in_specs=[
            pl.BlockSpec((t, width), lambda i: (i, 0)),
            pl.BlockSpec((n, k), lambda i: (0, 0)),
            pl.BlockSpec((n, k), lambda i: (0, 0)),
            tile,
            tile,
        ],
        out_specs=[tile] * 2,
        out_shape=[jax.ShapeDtypeStruct((m, n), BF)] * 2,
        cost_estimate=FREE,
        name="hidden_back",
    )(grad, *down, gate, up)


def input_back_body(steps, gg_ref, gu_ref, gn_ref, gf_ref, un_ref, uf_ref, one_ref, two_ref):
    rows = one_ref.shape[0]

    @pl.when(pl.program_id(0) < steps)
    def _():
        part = dot_nt(gg_ref[...], gn_ref[...]) + dot_nt(gu_ref[...], un_ref[...])
        one_ref[...] = part[:rows].astype(BF)
        two_ref[...] = part[rows:].astype(BF)

    @pl.when(pl.program_id(0) >= steps)
    def _():
        part = dot_nt(gg_ref[...], gf_ref[...]) + dot_nt(gu_ref[...], uf_ref[...])
        one_ref[...] = part[:rows].astype(BF)
        two_ref[...] = part[rows:].astype(BF)


def input_back(grad_gate, grad_up, gate, up):
    m, n = grad_gate.shape
    k = gate[0].shape[0]
    tile = 2 * LANES
    steps = k // tile
    whole = pl.BlockSpec((m, n), lambda i: (0, 0))
    near = pl.BlockSpec((tile, n), lambda i: (jnp.minimum(i, steps - 1), 0))
    far = pl.BlockSpec((tile, n), lambda i: (jnp.maximum(i - steps, 0), 0))
    return pl.pallas_call(
        functools.partial(input_back_body, steps),
        grid=(2 * steps,),
        in_specs=[whole, whole, near, far, near, far],
        out_specs=[pl.BlockSpec((m // 2, tile), lambda i: (0, i))] * 2,
        out_shape=[jax.ShapeDtypeStruct((m // 2, 2 * k), BF)] * 2,
        cost_estimate=FREE,
        name="input_back",
    )(grad_gate, grad_up, *gate, *up)


def local(
    sizes,
    tokens_in,
    cotangent,
    segment_ids,
    attn_gain,
    attn_shift,
    qkv_weight,
    qkv_bias,
    out_weight,
    mlp_gain,
    mlp_shift,
    gate_weight,
    up_weight,
    down_weight,
):
    nz, ny, nx, nc = sizes
    seq, peers = nz * ny, nx * nc
    devices = seq * peers
    pair = nx == 2 and ny == 2
    att, att_rows = ("x", "y") if pair else (None, None)
    fwd, fwd_rows = ("y", "x") if pair else (None, None)
    fwd_axes = ("y", "c") if pair else BATCH
    t, width = tokens_in.shape[1:]
    length = segment_ids.shape[1]
    heads = width // HEAD_DIM // peers
    pairs = heads // 2
    groups = seq // pairs
    rpg = peers // groups
    ff = down_weight.shape[0] * devices
    strip = ff // devices
    own_head = width // devices == HEAD_DIM
    window = min((length // 3 - 1 + t - 1) // t + 1, length // t)
    me_seq = lax.axis_index(SEQ)
    me_peer = lax.axis_index(BATCH)

    small = jnp.concatenate([attn_gain, attn_shift, mlp_gain, mlp_shift, qkv_bias])
    small = jnp.broadcast_to(small[None], (devices, small.size))
    small = lax.all_to_all(small, ALL, split_axis=0, concat_axis=0, tiled=True).astype(F32)
    each = attn_gain.size
    gain_one, shift_one, gain_two, shift_two = [
        small[:, i * each : (i + 1) * each].reshape(1, width) for i in range(4)
    ]
    bias = small[:, 4 * each :].reshape(3, heads, peers, HEAD_DIM)
    bias = lax.dynamic_index_in_dim(bias, me_peer, 2, keepdims=False).reshape(1, -1)

    rows = qkv_weight.shape[0]
    third = width // peers
    qkv_mine = qkv_weight.reshape(rows, 3, heads, peers, HEAD_DIM).transpose(3, 0, 1, 2, 4)
    qkv_mine = swap_peers(qkv_mine.reshape(peers, rows, -1), BATCH).reshape(peers * rows, -1)

    def columns(w):
        if pair:
            w = w.reshape(rows, nz, 2, 2, nc, strip).transpose(2, 4, 0, 1, 3, 5)
        else:
            w = w.reshape(rows, seq, peers, strip).transpose(2, 0, 1, 3)
        return w.reshape(peers, rows, -1)

    merge_att = functools.partial(merge_rows, axis=att_rows, nz=nz)
    merge_ff = functools.partial(merge_rows, axis=fwd_rows, nz=nz)
    split = 2 if pair else 1
    mine = jnp.concatenate([columns(gate_weight), columns(up_weight)], axis=1)
    mine = swap_peers(after(mine, small), fwd_axes)
    gate_mine = mine[:, :rows].reshape(peers * rows, -1)
    up_mine = mine[:, rows:].reshape(peers * rows, -1)
    kv_near, q_near = gather_z(qkv_mine[:, third:]), gather_z(qkv_mine[:, :third])
    kv_near, gate_mine, up_mine = lax.optimization_barrier((kv_near, gate_mine, up_mine))
    kv_far = gather_far(kv_near, att_rows)
    gate_near = gather_z(gate_mine)
    gate_far = gather_far(gate_near, fwd_rows)
    if own_head:
        out_near = gather_z(after(out_weight, gate_near))
    else:
        out_full = lax.all_gather(out_weight, ALL, axis=0, tiled=True)
        out_full = out_full.reshape(heads, peers, HEAD_DIM, width)
        out_full = lax.dynamic_index_in_dim(out_full, me_peer, 1, keepdims=False)
        out_full = out_full.reshape(heads * HEAD_DIM, width)

    kv_far, q_near, segment = lax.optimization_barrier(
        (kv_far, q_near, gather_peers(segment_ids, att))
    )
    q_far = gather_far(q_near, att_rows)
    q_full, kv_full = merge_att(q_near, q_far), merge_att(kv_near, kv_far)
    start = jnp.zeros_like(segment)
    for doc in range(DOCS):
        count = jnp.sum((segment == doc).astype(jnp.int32), axis=1, keepdims=True)
        start = start + jnp.where(segment > doc, count, 0)
    places = me_seq * t + jnp.arange(t, dtype=jnp.int32)
    here = places[None] - lax.dynamic_slice_in_dim(start, me_seq * t, t, 1)
    half = ROT // 2
    inverse = 10000.0 ** (-jnp.arange(half, dtype=F32) / half)
    theta = inverse[:, None] * here.reshape(1, -1).astype(F32)
    cosine, sine = jnp.cos(theta), jnp.sin(theta)
    rest = jnp.ones((HEAD_DIM - ROT, theta.shape[1]), F32)
    cosine = jnp.concatenate([cosine, cosine, rest] * 2, axis=0).T
    sine = jnp.concatenate([-sine, sine, 0.0 * rest] * 2, axis=0).T
    start = lax.dynamic_slice_in_dim(start, (me_seq % groups) * rpg, rpg, 0)
    start = start.reshape(rpg, length // t, t, 1)

    inputs = tokens_in[0].astype(F32)
    unit_one, scale_one = norm_stats(inputs)
    normed = (unit_one * gain_one + shift_one).astype(BF)
    normed_all = gather_peers(normed, att)
    key_value = rotary_out(
        dot(normed_all, kv_full), bias[:, third:], cosine, sine, pairs, rpg, t, 1
    )
    key_value = swap_seq(key_value)
    query = rotary_out(dot(normed_all, q_full), bias[:, :third], cosine, sine, pairs, rpg, t, 1)
    query = swap_seq(after(query, key_value))
    qkv_full = jnp.concatenate([q_full, kv_full], axis=1)
    up_near = gather_z(up_mine)
    grad_output = cotangent[0]
    grad_all = gather_peers(grad_output, fwd)
    query, key_value, up_near = lax.optimization_barrier((query, key_value, up_near))
    mixed = attend(query, key_value, start, window)
    mixed, gate_far = lax.optimization_barrier((mixed, gate_far))
    if own_head:
        out_near = after(out_near, mixed)
    up_far = gather_far(up_near, fwd_rows)
    mixed = swap_seq(mixed)
    if own_head:
        out_full = merge_att(out_near, gather_far(out_near, att_rows))
    wide = width // 2
    down_near = gather_z(down_weight[:, :wide]), gather_z(down_weight[:, wide:])
    mixed, up_far, grad_all, qkv_full, out_full = lax.optimization_barrier(
        (mixed, up_far, grad_all, qkv_full, out_full)
    )

    def token_rows(x):
        x = x.reshape(pairs, groups * rpg * t, LANES).transpose(1, 0, 2)
        return x.reshape(groups * rpg * t, pairs * LANES)

    def head_rows(x):
        x = x.reshape(groups * rpg * t, pairs, LANES).transpose(1, 0, 2)
        return x.reshape(seq, rpg, t, LANES)

    mixed = token_rows(mixed)
    branch_one = halves_of(dot, mixed, out_full)
    if pair:
        here_x = lax.axis_index("x")
        branch_one = reduce_pieces(branch_one, att)
        hidden, normed_two = hidden_norm(here_x, tokens_in[0], branch_one, gain_two, shift_two)
        gate_full, up_full = (gate_near, gate_far), (up_near, up_far)
    else:
        hidden = inputs + reduce_peers(branch_one, att)
        unit_two, scale_two = norm_stats(hidden)
        normed_two = (unit_two * gain_two + shift_two).astype(BF)
        gate_full = jnp.split(merge_ff(gate_near, gate_far), 2)
        up_full = jnp.split(merge_ff(up_near, up_far), 2)
    down_one, down_two = down_near
    normed_two, down_one = lax.optimization_barrier((normed_two, down_one))
    down_far = [gather_far(w, fwd_rows) for w in (down_one, after(down_two, normed_two))]
    normed_two_all = gather_peers(normed_two, fwd)
    normed_two_all, down_far[0] = lax.optimization_barrier((normed_two_all, down_far[0]))
    gate, up, act = hidden_units(normed_two_all, gate_full, up_full)
    down_full = [merge_ff(near, after(far, gate)) for near, far in zip(down_near, down_far)]

    send_att = functools.partial(send_rows, axis=att_rows, nz=nz, na=ny)
    send_ff = functools.partial(send_rows, axis=fwd_rows, nz=nz, na=nx if pair else ny)
    down_one = send_ff(dot_tn(act, grad_all[:, :wide], BF))
    grad_gate, grad_up = hidden_back(grad_all, down_full, gate, up, t)
    part = input_back(grad_gate, grad_up, gate_full, up_full)
    down_one = add_rows(*down_one)
    part, down_one = lax.optimization_barrier((part, down_one))
    down_two = send_ff(dot_tn(act, grad_all[:, wide:], BF))
    if pair:
        grad_normed_two = reduce_pieces(part, fwd)
    else:
        grad_normed_two = reduce_peers(part, fwd)

    def dots(g):
        if not pair:
            return (dot_tn(normed_two_all, g, BF),)
        return dot_tn(normed_two_all[:, wide:], g, BF), dot_tn(normed_two_all[:, :wide], g, BF)

    def send_columns(g):
        if not pair:
            return send_ff(g[0])
        return g[1], lax.ppermute(g[0], "x", SWAP)

    cut_ff = grad_gate.shape[1] // 256 * 128 + LANES
    gate_one, gate_two = dots(grad_gate[:, :cut_ff]), dots(grad_gate[:, cut_ff:])
    grad_normed_two, gate_one, gate_two = lax.optimization_barrier(
        (grad_normed_two, gate_one, gate_two)
    )
    gate_one, gate_two, up_w = [send_columns(g) for g in (gate_one, gate_two, dots(grad_up))]
    down_one, down_two = scatter_z(down_one), add_rows(*down_two)
    grad_normed_two, down_one, down_two = lax.optimization_barrier(
        (grad_normed_two, down_one, down_two)
    )
    down_two = scatter_z(down_two)
    if pair:
        grad_hidden, branch, sums = hidden_norm_back(
            here_x, hidden, grad_output, grad_normed_two, gain_two
        )
        grad_gain_two, grad_shift_two = sums[0], sums[1]
    else:
        back, grad_gain_two, grad_shift_two = norm_back(
            grad_normed_two, unit_two, scale_two, gain_two
        )
        grad_hidden = grad_output.astype(F32) + back
        branch = grad_hidden.astype(BF)

    def ff_swap(g):
        return swap_peers(g.reshape(peers, rows, -1), fwd_axes)

    def ff_columns(g):
        if pair:
            g = g.reshape(2, nc, rows, nz, 2, strip).transpose(2, 3, 0, 4, 1, 5)
        else:
            g = g.reshape(peers, rows, seq, strip).transpose(1, 2, 0, 3)
        return g.reshape(rows, ff).astype(F32)

    branch = gather_peers(branch, att)
    grad_mixed = head_rows(dot_nt(branch, out_full, BF))
    grad_mixed, down_two = lax.optimization_barrier((grad_mixed, down_two))
    down_full = jnp.concatenate([after(down_full[0], grad_mixed), down_full[1]], axis=1)
    branch_two = reduce_peers(halves_of(dot, after(act, grad_mixed), down_full), fwd)
    block_out = (hidden + branch_two).astype(BF).reshape(tokens_in.shape)
    grad_mixed = swap_seq(grad_mixed)
    grad_out = dot_tn(mixed, branch, BF)
    if pair:
        near, far, grad_out = lax.optimization_barrier((*gate_one, grad_out))
        gate_one = near, far
    gate_one = add_rows(*gate_one)
    grad_mixed, gate_one = lax.optimization_barrier((grad_mixed, gate_one))
    gate_one = scatter_z(gate_one)
    grad_qkv = attend_back(query, key_value, start, grad_mixed, window)
    if own_head:
        grad_out = send_att(grad_out)
    grad_qkv, gate_one, gate_two, grad_out = lax.optimization_barrier(
        (grad_qkv, gate_one, gate_two, grad_out)
    )
    if own_head:
        grad_out = scatter_z(add_rows(*grad_out))
    gate_two = scatter_z(add_rows(*gate_two))
    grad_qkv = swap_seq(grad_qkv)
    grad_down = jnp.concatenate([down_one, down_two], axis=1).astype(F32)
    up_sum = add_rows(*up_w)
    up_w = scatter_z(up_sum)
    grad_qkv, up_sum, grad_out, grad_down, block_out = lax.optimization_barrier(
        (grad_qkv, up_sum, grad_out, grad_down, block_out)
    )
    if not own_head:
        mine = (jnp.arange(peers) == me_peer).astype(BF)[None, :, None, None]
        grad_out = grad_out.reshape(heads, 1, HEAD_DIM, width) * mine
        grad_out = lax.psum_scatter(
            grad_out.reshape(width, width), ALL, scatter_dimension=0, tiled=True
        )
    grad_proj = rotary_in(grad_qkv, cosine, sine, pairs)
    gate_w = ff_swap(jnp.concatenate([gate_one, gate_two], axis=1))
    cut = 3 * third // 2
    first = send_att(dot_tn(normed_all, grad_proj[:, :cut], BF))
    second = dot_tn(normed_all, grad_proj[:, cut:], BF)
    grad_normed = halves_of(dot_nt, grad_proj, qkv_full)
    grad_normed, first, second, gate_w = lax.optimization_barrier(
        (grad_normed, first, second, gate_w)
    )
    grad_gate_w = ff_columns(gate_w)
    second = send_att(second)
    grad_normed = reduce_peers(grad_normed, att)
    first = add_rows(*first)
    first, up_w = lax.optimization_barrier((first, up_w))
    if pair:
        second = (second[0], after(second[1], first))
    first = scatter_z(first)
    back, grad_gain_one, grad_shift_one = norm_back(grad_normed, unit_one, scale_one, gain_one)
    grad_tokens = (grad_hidden + back).astype(BF).reshape(tokens_in.shape)
    second = add_rows(*second)
    second, first, grad_tokens, up_w, grad_gate_w = lax.optimization_barrier(
        (second, first, grad_tokens, up_w, grad_gate_w)
    )
    second = scatter_z(second)
    grad_up_w = ff_columns(ff_swap(up_w))
    second, grad_up_w = lax.optimization_barrier((second, grad_up_w))
    grad_out = grad_out.astype(F32)
    grad_qkv_w = []
    for half in (first, second):
        half = swap_peers(half.reshape(peers, rows, -1), BATCH)
        half = half.reshape(peers, rows, -1, HEAD_DIM).transpose(1, 2, 0, 3)
        grad_qkv_w.append(half.reshape(rows, -1).astype(F32))
    grad_qkv_w = jnp.concatenate(grad_qkv_w, axis=1)
    grad_bias = jnp.sum(grad_proj.astype(F32), axis=0).reshape(3, heads, 1, HEAD_DIM)
    mine = (jnp.arange(peers) == me_peer).astype(F32)[None, None, :, None]
    grad_bias = (grad_bias * mine).reshape(devices, -1)

    vectors = [grad_gain_one, grad_shift_one, grad_gain_two, grad_shift_two]
    vectors = [v.reshape(devices, each) for v in vectors] + [grad_bias]
    vectors = jnp.concatenate(vectors, axis=1)
    vectors = lax.all_to_all(vectors, ALL, split_axis=0, concat_axis=0, tiled=True)
    vectors = jnp.sum(vectors, axis=0)
    g1, s1, g2, s2 = [vectors[i * each : (i + 1) * each] for i in range(4)]
    return (
        block_out,
        grad_tokens,
        g1,
        s1,
        grad_qkv_w,
        vectors[4 * each :],
        grad_out,
        g2,
        s2,
        grad_gate_w,
        grad_up_w,
        grad_down,
    )


def solution(mesh):
    seq, batch = mesh.shape["seq"], mesh.shape["batch"]
    sizes = (4, seq // 4, batch // 2, 2)
    fine = Mesh(mesh.devices.reshape(sizes), ALL)
    token = P(BATCH, SEQ, None)
    vector = P(ALL)
    matrix = P(ALL, None)
    return jax.shard_map(
        functools.partial(local, sizes),
        mesh=fine,
        in_specs=(
            token,
            token,
            P(BATCH, None),
            vector,
            vector,
            matrix,
            vector,
            matrix,
            vector,
            vector,
            matrix,
            matrix,
            matrix,
        ),
        out_specs=(
            token,
            token,
            vector,
            vector,
            matrix,
            vector,
            matrix,
            vector,
            vector,
            matrix,
            matrix,
            matrix,
        ),
        check_vma=False,
    )
```

```python
import functools

import jax
import jax.numpy as jnp
from jax import lax
from jax.experimental import pallas as pl
from jax.experimental.pallas import tpu as pltpu
from jax.sharding import Mesh
from jax.sharding import PartitionSpec as P

HEAD_DIM = 64
ROT = 16
DOCS = 6
LANES = 128
EPS = 1e-05
BF = jnp.bfloat16
F32 = jnp.float32
NEG = -1e30
ALL = ("z", "y", "x", "c")
SEQ = ("z", "y")
BATCH = ("x", "c")
SWAP = ((0, 1), (1, 0))


def dot(a, b, out=F32):
    return jnp.dot(a, b, preferred_element_type=out)


def dot_nt(a, b, out=F32):
    return lax.dot_general(a, b, (((1,), (1,)), ((), ())), preferred_element_type=out)


def dot_tn(a, b, out=F32):
    return lax.dot_general(a, b, (((0,), (0,)), ((), ())), preferred_element_type=out)


def after(x, *first):
    return lax.optimization_barrier((x,) + first)[0]


def gather_peers(x, axis):
    if axis is None:
        return lax.all_gather(x, BATCH, axis=0, tiled=True)
    other = lax.ppermute(x, axis, SWAP)
    far = lax.ppermute(x, "c", SWAP)
    last = lax.ppermute(other, "c", SWAP)
    return jnp.concatenate([x, other, far, last], axis=0)


def reduce_peers(halves, axis):
    near, far = halves
    if axis is None:
        part = jnp.concatenate([near, far], axis=0)
        return lax.psum_scatter(part, BATCH, scatter_dimension=0, tiled=True).astype(F32)
    rows = near.shape[0] // 2
    got = lax.ppermute(far, "c", SWAP)
    send = (near[rows:].astype(F32) + got[rows:].astype(F32)).astype(BF)
    last = lax.ppermute(send, axis, SWAP)
    return near[:rows].astype(F32) + got[:rows].astype(F32) + last.astype(F32)


def reduce_pieces(halves, axis):
    near, far = halves
    rows = near.shape[0] // 2
    got = lax.ppermute(far, "c", SWAP)
    send = (near[rows:].astype(F32) + got[rows:].astype(F32)).astype(BF)
    return near, got, lax.ppermute(send, axis, SWAP)


def halves_of(product, x, w):
    rows = x.shape[0] // 2
    return product(x[:rows], w, BF), product(x[rows:], w, BF)


def gather_z(w):
    return lax.all_gather(w, "z", axis=0, tiled=True)


def gather_far(near, axis):
    if axis is None:
        return lax.all_gather(near, "y", axis=0)
    return lax.ppermute(near, axis, SWAP)


def merge_rows(near, far, axis, nz, inner=1):
    wide = near.shape[-1]
    if axis is None:
        far = far.reshape(far.shape[0], nz, -1, wide).transpose(1, 0, 2, 3)
        return far.reshape(-1, wide)
    near = near.reshape(nz * inner, 1, -1, wide)
    far = far.reshape(near.shape)
    first = lax.axis_index(axis) == 0
    full = jnp.concatenate([jnp.where(first, near, far), jnp.where(first, far, near)], axis=1)
    return full.reshape(-1, wide)


def send_rows(g, axis, nz, na, inner=1):
    rows = g.shape[0] // (nz * na)
    if axis is None:
        g = g.reshape(nz, na, rows, -1).transpose(1, 0, 2, 3).reshape(na, nz * rows, -1)
        return None, lax.psum_scatter(g, "y", scatter_dimension=0, tiled=True)[0]
    g = g.reshape(nz * inner, na, rows // inner, g.shape[1])
    here = lax.axis_index(axis)
    send = lax.dynamic_index_in_dim(g, 1 - here, 1, keepdims=False)
    keep = lax.dynamic_index_in_dim(g, here, 1, keepdims=False)
    return keep, lax.ppermute(send, axis, SWAP)


def add_rows(keep, got):
    if keep is None:
        return got
    got = (keep.astype(F32) + got.astype(F32)).astype(BF)
    return got.reshape(-1, got.shape[-1])


def scatter_z(g):
    return lax.psum_scatter(g, "z", scatter_dimension=0, tiled=True)


def reduce_z(keep, got):
    return scatter_z(add_rows(keep, got))


def swap_peers(x, axes):
    return lax.all_to_all(x, axes, split_axis=0, concat_axis=0, tiled=True)


def swap_seq(x):
    return lax.all_to_all(x, SEQ, split_axis=0, concat_axis=0, tiled=True)


def norm_stats(value):
    centred = value - jnp.mean(value, axis=-1, keepdims=True)
    scale = lax.rsqrt(jnp.mean(centred * centred, axis=-1, keepdims=True) + EPS)
    return centred * scale, scale


def norm_back(grad, unit, scale, gain):
    e = grad * gain
    back = scale * (
        e - jnp.mean(e, axis=-1, keepdims=True) - unit * jnp.mean(e * unit, axis=-1, keepdims=True)
    )
    return back, jnp.sum(grad * unit, axis=0), jnp.sum(grad, axis=0)


def turn(value, cosine, sine, lane):
    inner = lane % HEAD_DIM
    ahead = pltpu.roll(value, LANES - ROT // 2, 1)
    behind = pltpu.roll(value, ROT // 2, 1)
    return value * cosine + jnp.where(inner < ROT // 2, ahead, behind) * sine


def rotary_out_body(turned, proj_ref, bias_ref, cos_ref, sin_ref, out_ref):
    pairs = out_ref.shape[0]
    cosine, sine = cos_ref[...], sin_ref[...]
    lane = lax.broadcasted_iota(jnp.int32, cosine.shape, 1)
    rotate = pl.program_id(1) < turned
    for i in range(pairs):
        at = slice(i * LANES, (i + 1) * LANES)
        value = proj_ref[:, at] + bias_ref[:, at]
        value = jnp.where(rotate, turn(value, cosine, sine, lane), value)
        out_ref[i] = value.astype(BF).reshape(out_ref.shape[1:])


def rotary_out(proj, bias, cosine, sine, pairs, rpg, t, turned):
    peers = proj.shape[0] // t
    groups = peers // rpg
    wide = pairs * LANES
    parts = proj.shape[1] // wide
    out = pl.pallas_call(
        functools.partial(rotary_out_body, turned),
        grid=(peers, parts),
        in_specs=[
            pl.BlockSpec((t, wide), lambda b, p: (b, p)),
            pl.BlockSpec((1, wide), lambda b, p: (0, p)),
            pl.BlockSpec((t, LANES), lambda b, p: (b, 0)),
            pl.BlockSpec((t, LANES), lambda b, p: (b, 0)),
        ],
        out_specs=pl.BlockSpec(
            (pairs, 1, 1, 1, t, LANES), lambda b, p: (0, b // rpg, p, b % rpg, 0, 0)
        ),
        out_shape=jax.ShapeDtypeStruct((pairs, groups, parts, rpg, t, LANES), BF),
        cost_estimate=pl.CostEstimate(
            flops=1, bytes_accessed=1, transcendentals=0
        ),
        name="rotary_out",
    )(proj, bias, cosine, sine)
    return out.reshape((pairs * groups,) + out.shape[2:])


def rotary_in_body(grad_ref, cos_ref, sin_ref, out_ref):
    pairs = grad_ref.shape[0]
    cosine, sine = cos_ref[...], -sin_ref[...]
    lane = lax.broadcasted_iota(jnp.int32, cosine.shape, 1)
    rotate = pl.program_id(1) < 2
    for i in range(pairs):
        value = grad_ref[i].reshape(cosine.shape).astype(F32)
        value = jnp.where(rotate, turn(value, cosine, sine, lane), value)
        out_ref[:, i * LANES : (i + 1) * LANES] = value.astype(BF)


def rotary_in(grad, cosine, sine, pairs):
    dests, parts, rpg, t, _ = grad.shape
    groups = dests // pairs
    wide = pairs * LANES
    return pl.pallas_call(
        rotary_in_body,
        grid=(groups * rpg, parts),
        in_specs=[
            pl.BlockSpec(
                (pairs, 1, 1, 1, t, LANES), lambda b, p: (0, b // rpg, p, b % rpg, 0, 0)
            ),
            pl.BlockSpec((t, LANES), lambda b, p: (b, 0)),
            pl.BlockSpec((t, LANES), lambda b, p: (b, 0)),
        ],
        out_specs=pl.BlockSpec((t, wide), lambda b, p: (b, p)),
        out_shape=jax.ShapeDtypeStruct((groups * rpg * t, parts * wide), BF),
        cost_estimate=pl.CostEstimate(
            flops=1, bytes_accessed=1, transcendentals=0
        ),
        name="rotary_in",
    )(grad.reshape((pairs, groups) + grad.shape[1:]), cosine, sine)


def by_head(x):
    lane = lax.broadcasted_iota(jnp.int32, x.shape, 1)
    zero = jnp.zeros_like(x)
    return jnp.concatenate(
        [jnp.where(lane < HEAD_DIM, x, zero), jnp.where(lane >= HEAD_DIM, x, zero)], axis=0
    )


def one_head(x):
    t = x.shape[0] // 2
    lane = lax.broadcasted_iota(jnp.int32, (t, LANES), 1)
    return jnp.where(lane < HEAD_DIM, x[:t], x[t:])


def window_weights(q2, keys, start, row0, col0):
    scores = dot_nt(q2, keys) * (HEAD_DIM**-0.5)
    t = q2.shape[0] // 2
    shape = (t, keys.shape[0])
    rows = row0 + lax.broadcasted_iota(jnp.int32, shape, 0)
    cols = col0 + lax.broadcasted_iota(jnp.int32, shape, 1)
    allowed = (cols <= rows) & (cols >= start)
    allowed = jnp.concatenate([allowed, allowed], axis=0)
    scores = jnp.where(allowed, scores, NEG)
    weights = jnp.exp(scores - jnp.max(scores, axis=-1, keepdims=True))
    return weights / jnp.sum(weights, axis=-1, keepdims=True)


def by_window(window, body):
    number = pl.program_id(1)
    for w in range(1, window + 1):
        pl.when(number == w - 1 if w < window else number >= w - 1)(functools.partial(body, w))


def forward_body(window, q_ref, k_ref, v_ref, start_ref, out_ref):
    number = pl.program_id(1)
    t = q_ref.shape[3]

    def body(w):
        first = number - (w - 1)
        keys = k_ref[pl.ds(first, w), 0, 0].reshape(w * t, LANES)
        values = v_ref[pl.ds(first, w), 0, 0].reshape(w * t, LANES)
        q2 = by_head(q_ref[0, 0, 0])
        weights = window_weights(q2, keys, start_ref[0, 0], number * t, first * t)
        out_ref[0, 0] = one_head(dot(weights.astype(BF), values)).astype(BF)

    by_window(window, body)


def attention_specs(blocks, t):
    return [
        pl.BlockSpec((1, 1, 1, t, LANES), lambda r, i: (i, 0, r, 0, 0)),
        pl.BlockSpec((blocks, 1, 1, t, LANES), lambda r, i: (0, 0, r, 0, 0)),
        pl.BlockSpec((blocks, 1, 1, t, LANES), lambda r, i: (0, 1, r, 0, 0)),
        pl.BlockSpec((1, 1, t, 1), lambda r, i: (r, i, 0, 0)),
    ]


def attend(q, kv, start, window):
    blocks, _, rpg, t, _ = q.shape
    work = rpg * blocks * 2 * t * window * t
    return pl.pallas_call(
        functools.partial(forward_body, window),
        grid=(rpg, blocks),
        in_specs=attention_specs(blocks, t),
        out_specs=pl.BlockSpec((1, 1, t, LANES), lambda r, i: (i, r, 0, 0)),
        out_shape=jax.ShapeDtypeStruct((blocks, rpg, t, LANES), BF),
        cost_estimate=pl.CostEstimate(
            flops=1, bytes_accessed=1, transcendentals=0
        ),
        name="attend",
    )(q, kv, kv, start)


def backward_body(window, q_ref, k_ref, v_ref, start_ref, do_ref, out_ref, dk_ref, dv_ref):
    number = pl.program_id(1)
    t = q_ref.shape[3]
    scale = HEAD_DIM**-0.5

    @pl.when(number == 0)
    def _():
        dk_ref[...] = jnp.zeros_like(dk_ref)
        dv_ref[...] = jnp.zeros_like(dv_ref)

    def body(w):
        first = number - (w - 1)
        keys = k_ref[pl.ds(first, w), 0, 0].reshape(w * t, LANES)
        values = v_ref[pl.ds(first, w), 0, 0].reshape(w * t, LANES)
        q2 = by_head(q_ref[0, 0, 0])
        do2 = by_head(do_ref[0, 0])
        weights = window_weights(q2, keys, start_ref[0, 0], number * t, first * t)
        grad = dot_nt(do2, values)
        inner = jnp.sum(weights * grad, axis=-1, keepdims=True)
        ds = (weights * (grad - inner)).astype(BF)
        out_ref[number, 0, 0] = one_head(dot(ds, keys) * scale).astype(BF)
        shape = (w, t, LANES)
        dk_ref[pl.ds(first, w)] += dot_tn(ds, q2).reshape(shape)
        dv_ref[pl.ds(first, w)] += dot_tn(weights.astype(BF), do2).reshape(shape)

    by_window(window, body)

    @pl.when(number == pl.num_programs(1) - 1)
    def _():
        out_ref[:, 1, 0] = (dk_ref[...] * scale).astype(BF)
        out_ref[:, 2, 0] = dv_ref[...].astype(BF)


def attend_back(q, kv, start, grad, window):
    blocks, _, rpg, t, _ = q.shape
    work = rpg * blocks * 2 * t * window * t
    return pl.pallas_call(
        functools.partial(backward_body, window),
        grid=(rpg, blocks),
        in_specs=attention_specs(blocks, t)
        + [pl.BlockSpec((1, 1, t, LANES), lambda r, i: (i, r, 0, 0))],
        out_specs=pl.BlockSpec((blocks, 3, 1, t, LANES), lambda r, i: (0, 0, r, 0, 0)),
        out_shape=jax.ShapeDtypeStruct((blocks, 3, rpg, t, LANES), BF),
        scratch_shapes=[
            pltpu.VMEM((blocks, t, LANES), F32),
            pltpu.VMEM((blocks, t, LANES), F32),
        ],
        cost_estimate=pl.CostEstimate(
            flops=1, bytes_accessed=1, transcendentals=0
        ),
        name="attend_back",
    )(q, kv, kv, start, grad)


FREE = pl.CostEstimate(flops=1, bytes_accessed=1, transcendentals=0)


ROWS = 64


def places(count):
    half = count // 2
    return [((i % 2) * half + i // 2, (1 - i % 2) * half + i // 2) for i in range(count)]


def lanes_at(i):
    return slice(i * LANES, (i + 1) * LANES)


def unit_of(value):
    centred = value - jnp.mean(value, axis=-1, keepdims=True)
    scale = lax.rsqrt(jnp.mean(centred * centred, axis=-1, keepdims=True) + EPS)
    return centred * scale, scale


def hidden_norm_body(here_ref, x_ref, a_ref, b_ref, c_ref, gain_ref, shift_ref, hid_ref, out_ref):
    total = a_ref[...].astype(F32) + b_ref[...].astype(F32) + c_ref[...].astype(F32)
    hidden = x_ref[...].astype(F32) + total
    hid_ref[...] = hidden
    unit, _ = unit_of(hidden)
    normed = (unit * gain_ref[...] + shift_ref[...]).astype(BF)
    order = places(x_ref.shape[1] // LANES)

    @pl.when(here_ref[0] == 0)
    def _():
        for i, (place, _) in enumerate(order):
            out_ref[:, lanes_at(place)] = normed[:, lanes_at(i)]

    @pl.when(here_ref[0] != 0)
    def _():
        for i, (_, place) in enumerate(order):
            out_ref[:, lanes_at(place)] = normed[:, lanes_at(i)]


def hidden_norm(here, x, pieces, gain, shift):
    t, width = x.shape
    tile = pl.BlockSpec((ROWS, width), lambda i: (i, 0))
    line = pl.BlockSpec((1, width), lambda i: (0, 0))
    return pl.pallas_call(
        hidden_norm_body,
        grid=(t // ROWS,),
        in_specs=[pl.BlockSpec(memory_space=pltpu.SMEM)] + [tile] * 4 + [line] * 2,
        out_specs=[tile] * 2,
        out_shape=[jax.ShapeDtypeStruct((t, width), F32), jax.ShapeDtypeStruct((t, width), BF)],
        cost_estimate=FREE,
        name="hidden_norm",
    )(here.reshape(1), x, *pieces, gain, shift)


def norm_back_body(
    here_ref, hid_ref, cot_ref, a_ref, b_ref, c_ref, gain_ref, out_ref, bf_ref, sum_ref, tmp_ref
):
    grad = a_ref[...].astype(F32) + b_ref[...].astype(F32) + c_ref[...].astype(F32)
    order = places(cot_ref.shape[1] // LANES)

    @pl.when(here_ref[0] == 0)
    def _():
        for i, (place, _) in enumerate(order):
            tmp_ref[:, lanes_at(i)] = grad[:, lanes_at(place)]

    @pl.when(here_ref[0] != 0)
    def _():
        for i, (_, place) in enumerate(order):
            tmp_ref[:, lanes_at(i)] = grad[:, lanes_at(place)]

    grad = tmp_ref[...]
    unit, scale = unit_of(hid_ref[...])
    e = grad * gain_ref[...]
    mean = jnp.mean(e, axis=-1, keepdims=True)
    inner = jnp.mean(e * unit, axis=-1, keepdims=True)
    total = cot_ref[...].astype(F32) + scale * (e - mean - unit * inner)
    out_ref[...] = total
    bf_ref[...] = total.astype(BF)

    @pl.when(pl.program_id(0) == 0)
    def _():
        sum_ref[...] = jnp.zeros_like(sum_ref)

    sum_ref[0:1] += jnp.sum(grad * unit, axis=0, keepdims=True)
    sum_ref[1:2] += jnp.sum(grad, axis=0, keepdims=True)


def hidden_norm_back(here, hidden, cotangent, pieces, gain):
    t, width = hidden.shape
    tile = pl.BlockSpec((ROWS, width), lambda i: (i, 0))
    line = pl.BlockSpec((1, width), lambda i: (0, 0))
    return pl.pallas_call(
        norm_back_body,
        grid=(t // ROWS,),
        in_specs=[pl.BlockSpec(memory_space=pltpu.SMEM)] + [tile] * 5 + [line],
        out_specs=[tile, tile, pl.BlockSpec((8, width), lambda i: (0, 0))],
        out_shape=[
            jax.ShapeDtypeStruct((t, width), F32),
            jax.ShapeDtypeStruct((t, width), BF),
            jax.ShapeDtypeStruct((8, width), F32),
        ],
        scratch_shapes=[pltpu.VMEM((ROWS, width), F32)],
        cost_estimate=FREE,
        name="hidden_norm_back",
    )(here.reshape(1), hidden, cotangent, *pieces, gain)


def hidden_body(x_ref, gn_ref, gf_ref, un_ref, uf_ref, gate_ref, up_ref, act_ref):
    k = gn_ref.shape[0]
    tile = gn_ref.shape[1]
    near = jnp.concatenate([gn_ref[...], un_ref[...]], axis=1)
    far = jnp.concatenate([gf_ref[...], uf_ref[...]], axis=1)
    both = dot(x_ref[:, :k], near) + dot(x_ref[:, k:], far)
    gate, up = both[:, :tile], both[:, tile:]
    gate_ref[...] = gate
    up_ref[...] = up
    act_ref[...] = (gate * jax.nn.sigmoid(gate) * up).astype(BF)


def hidden_units(x, gate, up):
    m, width = x.shape
    k, n = gate[0].shape
    weight = pl.BlockSpec((k, LANES), lambda j: (0, j))
    tile = pl.BlockSpec((m, LANES), lambda j: (0, j))
    return pl.pallas_call(
        hidden_body,
        grid=(pl.cdiv(n, LANES),),
        in_specs=[pl.BlockSpec((m, width), lambda j: (0, 0))] + [weight] * 4,
        out_specs=[tile] * 3,
        out_shape=[jax.ShapeDtypeStruct((m, n), d) for d in (F32, F32, BF)],
        cost_estimate=FREE,
        name="hidden_units",
    )(x, *gate, *up)


def hidden_back_body(grad_ref, one_ref, two_ref, gate_ref, up_ref, gg_ref, gu_ref):
    k = one_ref.shape[1]
    grad = dot_nt(grad_ref[:, :k], one_ref[...]) + dot_nt(grad_ref[:, k:], two_ref[...])
    gate = gate_ref[...]
    sigmoid = jax.nn.sigmoid(gate)
    gg_ref[...] = (grad * up_ref[...] * sigmoid * (1.0 + gate * (1.0 - sigmoid))).astype(BF)
    gu_ref[...] = (grad * gate * sigmoid).astype(BF)


def hidden_back(grad, down, gate, up, t):
    m, width = grad.shape
    n, k = down[0].shape
    tile = pl.BlockSpec((t, n), lambda i: (i, 0))
    return pl.pallas_call(
        hidden_back_body,
        grid=(m // t,),
        in_specs=[
            pl.BlockSpec((t, width), lambda i: (i, 0)),
            pl.BlockSpec((n, k), lambda i: (0, 0)),
            pl.BlockSpec((n, k), lambda i: (0, 0)),
            tile,
            tile,
        ],
        out_specs=[tile] * 2,
        out_shape=[jax.ShapeDtypeStruct((m, n), BF)] * 2,
        cost_estimate=FREE,
        name="hidden_back",
    )(grad, *down, gate, up)


def input_back_body(steps, gg_ref, gu_ref, gn_ref, gf_ref, un_ref, uf_ref, one_ref, two_ref):
    rows = one_ref.shape[0]

    @pl.when(pl.program_id(0) < steps)
    def _():
        part = dot_nt(gg_ref[...], gn_ref[...]) + dot_nt(gu_ref[...], un_ref[...])
        one_ref[...] = part[:rows].astype(BF)
        two_ref[...] = part[rows:].astype(BF)

    @pl.when(pl.program_id(0) >= steps)
    def _():
        part = dot_nt(gg_ref[...], gf_ref[...]) + dot_nt(gu_ref[...], uf_ref[...])
        one_ref[...] = part[:rows].astype(BF)
        two_ref[...] = part[rows:].astype(BF)


def input_back(grad_gate, grad_up, gate, up):
    m, n = grad_gate.shape
    k = gate[0].shape[0]
    tile = 2 * LANES
    steps = k // tile
    whole = pl.BlockSpec((m, n), lambda i: (0, 0))
    near = pl.BlockSpec((tile, n), lambda i: (jnp.minimum(i, steps - 1), 0))
    far = pl.BlockSpec((tile, n), lambda i: (jnp.maximum(i - steps, 0), 0))
    return pl.pallas_call(
        functools.partial(input_back_body, steps),
        grid=(2 * steps,),
        in_specs=[whole, whole, near, far, near, far],
        out_specs=[pl.BlockSpec((m // 2, tile), lambda i: (0, i))] * 2,
        out_shape=[jax.ShapeDtypeStruct((m // 2, 2 * k), BF)] * 2,
        cost_estimate=FREE,
        name="input_back",
    )(grad_gate, grad_up, *gate, *up)


def local(
    sizes,
    tokens_in,
    cotangent,
    segment_ids,
    attn_gain,
    attn_shift,
    qkv_weight,
    qkv_bias,
    out_weight,
    mlp_gain,
    mlp_shift,
    gate_weight,
    up_weight,
    down_weight,
):
    nz, ny, nx, nc = sizes
    seq, peers = nz * ny, nx * nc
    devices = seq * peers
    pair = nx == 2 and ny == 2
    att, att_rows = ("x", "y") if pair else (None, None)
    fwd, fwd_rows = ("y", "x") if pair else (None, None)
    fwd_axes = ("y", "c") if pair else BATCH
    t, width = tokens_in.shape[1:]
    length = segment_ids.shape[1]
    heads = width // HEAD_DIM // peers
    pairs = heads // 2
    groups = seq // pairs
    rpg = peers // groups
    ff = down_weight.shape[0] * devices
    strip = ff // devices
    own_head = width // devices == HEAD_DIM
    window = min((length // 3 - 1 + t - 1) // t + 1, length // t)
    me_seq = lax.axis_index(SEQ)
    me_peer = lax.axis_index(BATCH)

    small = jnp.concatenate([attn_gain, attn_shift, mlp_gain, mlp_shift, qkv_bias])
    small = jnp.broadcast_to(small[None], (devices, small.size))
    small = lax.all_to_all(small, ALL, split_axis=0, concat_axis=0, tiled=True).astype(F32)
    each = attn_gain.size
    gain_one, shift_one, gain_two, shift_two = [
        small[:, i * each : (i + 1) * each].reshape(1, width) for i in range(4)
    ]
    bias = small[:, 4 * each :].reshape(3, heads, peers, HEAD_DIM)
    bias = lax.dynamic_index_in_dim(bias, me_peer, 2, keepdims=False).reshape(1, -1)

    rows = qkv_weight.shape[0]
    third = width // peers
    qkv_mine = qkv_weight.reshape(rows, 3, heads, peers, HEAD_DIM).transpose(3, 0, 1, 2, 4)
    qkv_mine = swap_peers(qkv_mine.reshape(peers, rows, -1), BATCH).reshape(peers * rows, -1)

    def columns(w):
        if pair:
            w = w.reshape(rows, nz, 2, 2, nc, strip).transpose(2, 4, 0, 1, 3, 5)
        else:
            w = w.reshape(rows, seq, peers, strip).transpose(2, 0, 1, 3)
        return w.reshape(peers, rows, -1)

    merge_att = functools.partial(merge_rows, axis=att_rows, nz=nz)
    merge_ff = functools.partial(merge_rows, axis=fwd_rows, nz=nz)
    split = 2 if pair else 1
    mine = jnp.concatenate([columns(gate_weight), columns(up_weight)], axis=1)
    mine = swap_peers(after(mine, small), fwd_axes)
    gate_mine = mine[:, :rows].reshape(peers * rows, -1)
    up_mine = mine[:, rows:].reshape(peers * rows, -1)
    kv_near, q_near = gather_z(qkv_mine[:, third:]), gather_z(qkv_mine[:, :third])
    kv_near, gate_mine, up_mine = lax.optimization_barrier((kv_near, gate_mine, up_mine))
    kv_far = gather_far(kv_near, att_rows)
    gate_near = gather_z(gate_mine)
    gate_far = gather_far(gate_near, fwd_rows)
    if own_head:
        out_near = gather_z(after(out_weight, gate_near))
    else:
        out_full = lax.all_gather(out_weight, ALL, axis=0, tiled=True)
        out_full = out_full.reshape(heads, peers, HEAD_DIM, width)
        out_full = lax.dynamic_index_in_dim(out_full, me_peer, 1, keepdims=False)
        out_full = out_full.reshape(heads * HEAD_DIM, width)

    kv_far, q_near, segment = lax.optimization_barrier(
        (kv_far, q_near, gather_peers(segment_ids, att))
    )
    q_far = gather_far(q_near, att_rows)
    q_full, kv_full = merge_att(q_near, q_far), merge_att(kv_near, kv_far)
    start = jnp.zeros_like(segment)
    for doc in range(DOCS):
        count = jnp.sum((segment == doc).astype(jnp.int32), axis=1, keepdims=True)
        start = start + jnp.where(segment > doc, count, 0)
    places = me_seq * t + jnp.arange(t, dtype=jnp.int32)
    here = places[None] - lax.dynamic_slice_in_dim(start, me_seq * t, t, 1)
    half = ROT // 2
    inverse = 10000.0 ** (-jnp.arange(half, dtype=F32) / half)
    theta = inverse[:, None] * here.reshape(1, -1).astype(F32)
    cosine, sine = jnp.cos(theta), jnp.sin(theta)
    rest = jnp.ones((HEAD_DIM - ROT, theta.shape[1]), F32)
    cosine = jnp.concatenate([cosine, cosine, rest] * 2, axis=0).T
    sine = jnp.concatenate([-sine, sine, 0.0 * rest] * 2, axis=0).T
    start = lax.dynamic_slice_in_dim(start, (me_seq % groups) * rpg, rpg, 0)
    start = start.reshape(rpg, length // t, t, 1)

    inputs = tokens_in[0].astype(F32)
    unit_one, scale_one = norm_stats(inputs)
    normed = (unit_one * gain_one + shift_one).astype(BF)
    normed_all = gather_peers(normed, att)
    key_value = rotary_out(
        dot(normed_all, kv_full), bias[:, third:], cosine, sine, pairs, rpg, t, 1
    )
    key_value = swap_seq(key_value)
    query = rotary_out(dot(normed_all, q_full), bias[:, :third], cosine, sine, pairs, rpg, t, 1)
    query = swap_seq(after(query, key_value))
    qkv_full = jnp.concatenate([q_full, kv_full], axis=1)
    up_near = gather_z(up_mine)
    grad_output = cotangent[0]
    grad_all = gather_peers(grad_output, fwd)
    query, key_value, up_near = lax.optimization_barrier((query, key_value, up_near))
    mixed = attend(query, key_value, start, window)
    mixed, gate_far = lax.optimization_barrier((mixed, gate_far))
    if own_head:
        out_near = after(out_near, mixed)
    up_far = gather_far(up_near, fwd_rows)
    mixed = swap_seq(mixed)
    if own_head:
        out_full = merge_att(out_near, gather_far(out_near, att_rows))
    wide = width // 2
    down_near = gather_z(down_weight[:, :wide]), gather_z(down_weight[:, wide:])
    mixed, up_far, grad_all, qkv_full, out_full = lax.optimization_barrier(
        (mixed, up_far, grad_all, qkv_full, out_full)
    )

    def token_rows(x):
        x = x.reshape(pairs, groups * rpg * t, LANES).transpose(1, 0, 2)
        return x.reshape(groups * rpg * t, pairs * LANES)

    def head_rows(x):
        x = x.reshape(groups * rpg * t, pairs, LANES).transpose(1, 0, 2)
        return x.reshape(seq, rpg, t, LANES)

    mixed = token_rows(mixed)
    branch_one = halves_of(dot, mixed, out_full)
    if pair:
        here_x = lax.axis_index("x")
        branch_one = reduce_pieces(branch_one, att)
        hidden, normed_two = hidden_norm(here_x, tokens_in[0], branch_one, gain_two, shift_two)
        gate_full, up_full = (gate_near, gate_far), (up_near, up_far)
    else:
        hidden = inputs + reduce_peers(branch_one, att)
        unit_two, scale_two = norm_stats(hidden)
        normed_two = (unit_two * gain_two + shift_two).astype(BF)
        gate_full = jnp.split(merge_ff(gate_near, gate_far), 2)
        up_full = jnp.split(merge_ff(up_near, up_far), 2)
    down_one, down_two = down_near
    normed_two, down_one = lax.optimization_barrier((normed_two, down_one))
    down_far = [gather_far(w, fwd_rows) for w in (down_one, after(down_two, normed_two))]
    normed_two_all = gather_peers(normed_two, fwd)
    normed_two_all, down_far[0] = lax.optimization_barrier((normed_two_all, down_far[0]))
    gate, up, act = hidden_units(normed_two_all, gate_full, up_full)
    down_full = [merge_ff(near, after(far, gate)) for near, far in zip(down_near, down_far)]

    send_att = functools.partial(send_rows, axis=att_rows, nz=nz, na=ny)
    send_ff = functools.partial(send_rows, axis=fwd_rows, nz=nz, na=nx if pair else ny)
    down_one = send_ff(dot_tn(act, grad_all[:, :wide], BF))
    grad_gate, grad_up = hidden_back(grad_all, down_full, gate, up, t)
    part = input_back(grad_gate, grad_up, gate_full, up_full)
    down_one = add_rows(*down_one)
    part, down_one = lax.optimization_barrier((part, down_one))
    down_two = send_ff(dot_tn(act, grad_all[:, wide:], BF))
    if pair:
        grad_normed_two = reduce_pieces(part, fwd)
    else:
        grad_normed_two = reduce_peers(part, fwd)

    def dots(g):
        if not pair:
            return (dot_tn(normed_two_all, g, BF),)
        return dot_tn(normed_two_all[:, wide:], g, BF), dot_tn(normed_two_all[:, :wide], g, BF)

    def send_columns(g):
        if not pair:
            return send_ff(g[0])
        return g[1], lax.ppermute(g[0], "x", SWAP)

    cut_ff = grad_gate.shape[1] // 256 * LANES - LANES
    gate_one, gate_two = dots(grad_gate[:, :cut_ff]), dots(grad_gate[:, cut_ff:])
    grad_normed_two, gate_one, gate_two = lax.optimization_barrier(
        (grad_normed_two, gate_one, gate_two)
    )
    gate_one, gate_two, up_w = [send_columns(g) for g in (gate_one, gate_two, dots(grad_up))]
    down_one, down_two = scatter_z(down_one), add_rows(*down_two)
    grad_normed_two, down_one, down_two = lax.optimization_barrier(
        (grad_normed_two, down_one, down_two)
    )
    down_two = scatter_z(down_two)
    if pair:
        grad_hidden, branch, sums = hidden_norm_back(
            here_x, hidden, grad_output, grad_normed_two, gain_two
        )
        grad_gain_two, grad_shift_two = sums[0], sums[1]
    else:
        back, grad_gain_two, grad_shift_two = norm_back(
            grad_normed_two, unit_two, scale_two, gain_two
        )
        grad_hidden = grad_output.astype(F32) + back
        branch = grad_hidden.astype(BF)

    def ff_swap(g):
        return swap_peers(g.reshape(peers, rows, -1), fwd_axes)

    def ff_columns(g):
        if pair:
            g = g.reshape(2, nc, rows, nz, 2, strip).transpose(2, 3, 0, 4, 1, 5)
        else:
            g = g.reshape(peers, rows, seq, strip).transpose(1, 2, 0, 3)
        return g.reshape(rows, ff).astype(F32)

    branch = gather_peers(branch, att)
    grad_mixed = head_rows(dot_nt(branch, out_full, BF))
    grad_mixed, down_two = lax.optimization_barrier((grad_mixed, down_two))
    down_full = jnp.concatenate([after(down_full[0], grad_mixed), down_full[1]], axis=1)
    branch_two = reduce_peers(halves_of(dot, after(act, grad_mixed), down_full), fwd)
    block_out = (hidden + branch_two).astype(BF).reshape(tokens_in.shape)
    grad_mixed = swap_seq(grad_mixed)
    grad_out = dot_tn(mixed, branch, BF)
    if pair:
        near, far, grad_out = lax.optimization_barrier((*gate_one, grad_out))
        gate_one = near, far
    gate_one = add_rows(*gate_one)
    grad_mixed, gate_one = lax.optimization_barrier((grad_mixed, gate_one))
    gate_one = scatter_z(gate_one)
    grad_qkv = attend_back(query, key_value, start, grad_mixed, window)
    if own_head:
        grad_out = send_att(grad_out)
    grad_qkv, gate_one, gate_two, grad_out = lax.optimization_barrier(
        (grad_qkv, gate_one, gate_two, grad_out)
    )
    if own_head:
        grad_out = scatter_z(add_rows(*grad_out))
    gate_two = scatter_z(add_rows(*gate_two))
    grad_qkv = swap_seq(grad_qkv)
    grad_down = jnp.concatenate([down_one, down_two], axis=1).astype(F32)
    up_sum = add_rows(*up_w)
    up_w = scatter_z(up_sum)
    grad_qkv, up_sum, grad_out, grad_down, block_out = lax.optimization_barrier(
        (grad_qkv, up_sum, grad_out, grad_down, block_out)
    )
    if not own_head:
        mine = (jnp.arange(peers) == me_peer).astype(BF)[None, :, None, None]
        grad_out = grad_out.reshape(heads, 1, HEAD_DIM, width) * mine
        grad_out = lax.psum_scatter(
            grad_out.reshape(width, width), ALL, scatter_dimension=0, tiled=True
        )
    grad_proj = rotary_in(grad_qkv, cosine, sine, pairs)
    gate_w = ff_swap(jnp.concatenate([gate_one, gate_two], axis=1))
    cut = 3 * third // 2
    first = send_att(dot_tn(normed_all, grad_proj[:, :cut], BF))
    second = dot_tn(normed_all, grad_proj[:, cut:], BF)
    grad_normed = halves_of(dot_nt, grad_proj, qkv_full)
    grad_normed, first, second, gate_w = lax.optimization_barrier(
        (grad_normed, first, second, gate_w)
    )
    grad_gate_w = ff_columns(gate_w)
    second = send_att(second)
    grad_normed = reduce_peers(grad_normed, att)
    first = add_rows(*first)
    first, up_w = lax.optimization_barrier((first, up_w))
    if pair:
        second = (second[0], after(second[1], first))
    first = scatter_z(first)
    back, grad_gain_one, grad_shift_one = norm_back(grad_normed, unit_one, scale_one, gain_one)
    grad_tokens = (grad_hidden + back).astype(BF).reshape(tokens_in.shape)
    second = add_rows(*second)
    second, first, grad_tokens, up_w, grad_gate_w = lax.optimization_barrier(
        (second, first, grad_tokens, up_w, grad_gate_w)
    )
    second = scatter_z(second)
    grad_up_w = ff_columns(ff_swap(up_w))
    second, grad_up_w = lax.optimization_barrier((second, grad_up_w))
    grad_out = grad_out.astype(F32)
    grad_qkv_w = []
    for half in (first, second):
        half = swap_peers(half.reshape(peers, rows, -1), BATCH)
        half = half.reshape(peers, rows, -1, HEAD_DIM).transpose(1, 2, 0, 3)
        grad_qkv_w.append(half.reshape(rows, -1).astype(F32))
    grad_qkv_w = jnp.concatenate(grad_qkv_w, axis=1)
    grad_bias = jnp.sum(grad_proj.astype(F32), axis=0).reshape(3, heads, 1, HEAD_DIM)
    mine = (jnp.arange(peers) == me_peer).astype(F32)[None, None, :, None]
    grad_bias = (grad_bias * mine).reshape(devices, -1)

    vectors = [grad_gain_one, grad_shift_one, grad_gain_two, grad_shift_two]
    vectors = [v.reshape(devices, each) for v in vectors] + [grad_bias]
    vectors = jnp.concatenate(vectors, axis=1)
    vectors = lax.all_to_all(vectors, ALL, split_axis=0, concat_axis=0, tiled=True)
    vectors = jnp.sum(vectors, axis=0)
    g1, s1, g2, s2 = [vectors[i * each : (i + 1) * each] for i in range(4)]
    return (
        block_out,
        grad_tokens,
        g1,
        s1,
        grad_qkv_w,
        vectors[4 * each :],
        grad_out,
        g2,
        s2,
        grad_gate_w,
        grad_up_w,
        grad_down,
    )


def solution(mesh):
    seq, batch = mesh.shape["seq"], mesh.shape["batch"]
    sizes = (4, seq // 4, batch // 2, 2)
    fine = Mesh(mesh.devices.reshape(sizes), ALL)
    token = P(BATCH, SEQ, None)
    vector = P(ALL)
    matrix = P(ALL, None)
    return jax.shard_map(
        functools.partial(local, sizes),
        mesh=fine,
        in_specs=(
            token,
            token,
            P(BATCH, None),
            vector,
            vector,
            matrix,
            vector,
            matrix,
            vector,
            vector,
            matrix,
            matrix,
            matrix,
        ),
        out_specs=(
            token,
            token,
            vector,
            vector,
            matrix,
            vector,
            matrix,
            vector,
            vector,
            matrix,
            matrix,
            matrix,
        ),
        check_vma=False,
    )
```
